128 devices in a mesh: box: 32 (over z, y, core), orb: 4 (over x).
Axes of the slice: x: 4, y: 4, z: 4, core: 2. Of those that a mesh axis runs over, the one named last changes fastest.
Arguments:
- orbitals: bfloat16 [64, 1000, 1536], P('box', None, 'orb'), may hold values from -0.02734375 to 0.02734375
- potential: float32 [64, 1000], P('box'), may hold values from -3 to 1
- deriv_blocks: bfloat16 [3, 10, 10], replicated, may hold values from -1 to 1
- levels: int32 [64], P('box'), may hold values from 0 to 2
- box_counts: int32 [32], P('box'), may hold values from 1 to 2, as said below
- neighbours: int32 [64, 3, 2], P('box'), may hold values from -1 to 63, as said below
Outputs:
- fock: float32 [1536, 1536], P('box', 'orb')
- correlation: float32 [1536, 1536], P('box', 'orb')
- inverse_root: float32 [1536, 1536], P('box', 'orb')
The draws below stay inside these ranges and needn't reach their ends.
Inputs may be any that keep to these rules, and one draw needn't show every extreme that they name: Each index of box holds box_counts of live slots, which are its first slots; the counts sum to 48, and some index holds 2. `neighbours`: an entry is -1 or the global slot of a live slot, other than the slot itself, on the same index of box or on the index just before or just after it; every entry of a non-live slot is -1.
All inputs are finite; a program needn't handle non-finite values.
Results may differ from the reference program's by a relative error of at most 0.0012.
Values may be sent and summed in bfloat16 or wider, within the bound.
A program may use at most 128 MiB of HBM per device.

```python
import jax
import jax.numpy as jnp
from jax import lax

ORBITAL_COUNT = 1536
SCALING_PER_DIM = 10
SLOTS_PER_INDEX = 2
TOTAL_BOX_SLOTS = 64
LIVE_BOX_TOTAL = 48


def layout_helper(key):
    base_key = jax.random.fold_in(key, 7331)
    key_rank, key_shift, key_selection, key_boundary = jax.random.split(base_key, 4)
    device_list = TOTAL_BOX_SLOTS // SLOTS_PER_INDEX
    ordering = jax.random.permutation(key_rank, device_list)
    count_list = jnp.where(ordering < device_list // 2, SLOTS_PER_INDEX, 1).astype(jnp.int32)
    slot_position_index = jnp.arange(TOTAL_BOX_SLOTS, dtype=jnp.int32)
    owner_dev = slot_position_index // SLOTS_PER_INDEX
    within_dev = slot_position_index % SLOTS_PER_INDEX
    offset_amount = jax.random.randint(key_shift, (TOTAL_BOX_SLOTS, 3, 2), -1, 2).astype(jnp.int32)
    dir_index = jnp.arange(3, dtype=jnp.int32)[None, :, None]
    side_index = jnp.arange(2, dtype=jnp.int32)[None, None, :]
    forced_boxes = (within_dev[:, None, None] == 0) & (dir_index == 0)
    offset_amount = jnp.where(forced_boxes, 2 * side_index - 1, offset_amount)
    target = owner_dev[:, None, None] + offset_amount
    inside = (target >= 0) & (target < device_list)
    target_device = jnp.clip(target, 0, device_list - 1)
    selected_boxes = jax.random.randint(key_selection, (TOTAL_BOX_SLOTS, 3, 2), 0, SLOTS_PER_INDEX).astype(jnp.int32) % count_list[target_device]
    boundary_edge = (jax.random.randint(key_boundary, (TOTAL_BOX_SLOTS, 3, 2), 0, 6) == 0) & jnp.logical_not(forced_boxes)
    self_ref = (offset_amount == 0) & (selected_boxes == within_dev[:, None, None])
    is_live = within_dev < count_list[owner_dev]
    accepted = inside & is_live[:, None, None] & jnp.logical_not(self_ref) & jnp.logical_not(boundary_edge)
    neighbour_slots = jnp.where(accepted, target_device * SLOTS_PER_INDEX + selected_boxes, -1).astype(jnp.int32)
    return (count_list, neighbour_slots)


def draw_box_counts(key, part):
    count_list, neighbour_slots = layout_helper(key)
    return count_list


def draw_neighbours(key, part):
    count_list, neighbour_slots = layout_helper(key)
    return neighbour_slots


def with_ends(drawn, key, least, top_value):
    longest = drawn.shape.index(max(drawn.shape))
    spots = []
    for shift in (0, 1):
        where = [jax.random.randint(jax.random.fold_in(key, axis), (), 0, length) for axis, length in enumerate(drawn.shape)]
        where[longest] = (where[longest] + shift) % drawn.shape[longest]
        spots.append(tuple(where))
    return drawn.at[spots[0]].set(least).at[spots[1]].set(top_value)


def block_scale(rng, dims, cuts, low, top_value):
    loudness, own = 1.0, jax.random.fold_in(rng, 6)
    for position, shards_of in cuts:
        heights = jnp.exp(jax.random.uniform(jax.random.fold_in(own, position), (shards_of,), jnp.float32, low / len(cuts), top_value / len(cuts)))
        loudness = loudness * jnp.repeat(heights, dims[position] // shards_of).reshape([-1 if axis == position else 1 for axis in range(len(dims))])
    return loudness


def gaussian(key, shape, spread, bound, cuts=(), kind=jnp.bfloat16):
    array = jax.random.normal(key, shape, jnp.float32) * spread
    if len(cuts) > 0:
        array = block_scale(key, shape, cuts, -0.22, 0.18) * array
    return jnp.clip(array, min=-bound, max=bound).astype(kind)


def setup_inputs(seed: int = 0) -> dict:
    key_of = jax.random.split(jax.random.key(seed), 7)
    return {
        "orbitals": gaussian(key_of[0], (TOTAL_BOX_SLOTS, SCALING_PER_DIM ** 3, ORBITAL_COUNT), (1.0 / (SCALING_PER_DIM ** 3 * LIVE_BOX_TOTAL) ** 0.5), 0.02734375, ((0, 32), (2, 4))),
        "potential": jnp.clip(-3.0 + 4.0 * jax.random.uniform(key_of[1], (TOTAL_BOX_SLOTS, SCALING_PER_DIM ** 3), jnp.float32) ** block_scale(key_of[1], (TOTAL_BOX_SLOTS, SCALING_PER_DIM ** 3), ((0, 32),), -0.2, 0.2), -3.0, 1.0),
        "deriv_blocks": gaussian(key_of[2], (3, SCALING_PER_DIM, SCALING_PER_DIM), (3 * SCALING_PER_DIM) ** -0.5, 1.0),
        "levels": with_ends(jax.random.randint(key_of[3], (TOTAL_BOX_SLOTS,), 0, 3), jax.random.fold_in(key_of[3], 1), 0, 2).astype(jnp.int32),
        "box_counts": draw_box_counts(jax.random.fold_in(key_of[6], 71), 0),
        "neighbours": draw_neighbours(jax.random.fold_in(key_of[6], 71), 0),
    }


def contract(left, right):
    return lax.dot_general(left, right, (((0,), (0,)), ((), ())), preferred_element_type=jnp.float32)


def highest(left, right):
    return jnp.dot(left, right, precision=lax.Precision.HIGHEST, preferred_element_type=jnp.float32)


def reference(orbitals, potential, deriv_blocks, levels, box_counts, neighbours):
    cube_edge_length = SCALING_PER_DIM
    coefficient_count = SCALING_PER_DIM ** 3
    slot_position_index = jnp.arange(TOTAL_BOX_SLOTS, dtype=jnp.int32)
    is_live = (slot_position_index % SLOTS_PER_INDEX) < box_counts[slot_position_index // SLOTS_PER_INDEX]
    active_boxes = jnp.where(is_live[:, None, None], orbitals, jnp.zeros((), jnp.bfloat16))
    padded = jnp.concatenate([jnp.zeros((1, coefficient_count, ORBITAL_COUNT), jnp.bfloat16), active_boxes], axis=0)
    blocks = deriv_blocks.astype(jnp.float32)
    level_scale = jnp.where(levels == 0, 0.5, jnp.where(levels == 1, 1.0, 2.0)).astype(jnp.float32)
    einsum_forms = ["ij,sjbco->sibco", "ij,sajco->saico", "ij,sabjo->sabio"]
    cube_shape_tuple = (TOTAL_BOX_SLOTS, cube_edge_length, cube_edge_length, cube_edge_length, ORBITAL_COUNT)
    kinetic = jnp.zeros((ORBITAL_COUNT, ORBITAL_COUNT), jnp.float32)
    for direction in range(3):
        lower_side = padded[(neighbours[:, direction, 0] + 1).astype(jnp.int32)].reshape(cube_shape_tuple)
        upper_side = padded[(neighbours[:, direction, 1] + 1).astype(jnp.int32)].reshape(cube_shape_tuple)
        middle = active_boxes.reshape(cube_shape_tuple)
        form = einsum_forms[direction]
        raw_sum = jnp.einsum(form, blocks[0], lower_side.astype(jnp.float32))
        raw_sum = raw_sum + jnp.einsum(form, blocks[1], middle.astype(jnp.float32))
        raw_sum = raw_sum + jnp.einsum(form, blocks[2], upper_side.astype(jnp.float32))
        derivative_matrix = (level_scale[:, None, None, None, None] * raw_sum).astype(jnp.bfloat16)
        derivative_matrix = derivative_matrix.reshape(TOTAL_BOX_SLOTS * coefficient_count, ORBITAL_COUNT)
        kinetic = kinetic + contract(derivative_matrix, derivative_matrix)
    flattened_active = active_boxes.reshape(TOTAL_BOX_SLOTS * coefficient_count, ORBITAL_COUNT)
    weighted_values = (potential[:, :, None] * active_boxes.astype(jnp.float32)).astype(jnp.bfloat16)
    weighted_values = weighted_values.reshape(TOTAL_BOX_SLOTS * coefficient_count, ORBITAL_COUNT)
    correlation = contract(flattened_active, flattened_active)
    fock = 0.5 * kinetic + contract(flattened_active, weighted_values)
    identity = jnp.eye(ORBITAL_COUNT, dtype=jnp.float32)
    first_turn = 1.5 * identity - 0.5 * correlation
    scaled_root = highest(correlation, first_turn)
    mixed_term = highest(first_turn, scaled_root)
    second_turn = 1.5 * identity - 0.5 * mixed_term
    inverse_root = highest(second_turn, first_turn)
    return fock, correlation, inverse_root
```

```python
import functools

import jax
import jax.numpy as jnp
from jax import lax
from jax.experimental import pallas as pl
from jax.experimental.pallas import tpu as pltpu
from jax.sharding import PartitionSpec as P

MESH = pl.DeviceIdType.MESH
HIGH = lax.Precision.HIGHEST
F32 = jnp.float32
BF16 = jnp.bfloat16


def quotient(x, n):
    return jnp.floor((x + 0.5) * (1.0 / n))


def rows_and_cols(shape):
    r = lax.broadcasted_iota(jnp.int32, shape, 0).astype(F32)
    c = lax.broadcasted_iota(jnp.int32, shape, 1).astype(F32)
    return r, c


def split_two(x):
    hi = x.astype(BF16)
    return hi, (x - hi.astype(F32)).astype(BF16)


def hdot(a, b):
    return jnp.dot(a, b, precision=HIGH, preferred_element_type=F32)


def gram_kernel(n, pad, boxes, groups, a_ref, ids_ref, sc_ref, gid_ref, bt_ref, pot_ref, live_ref, out_ref,
                gath, halo, S, Wsc, R, m12, m0, xs_sem, xr_sem, hs_sem, hr_sem):
    b = lax.axis_index("box")
    o = lax.axis_index("orb")
    sgn = 1 - 2 * lax.rem(b, 2)
    partner = b + sgn
    back1 = lax.rem(b - sgn + boxes, boxes)
    fwd2 = lax.rem(b + 2 * sgn + boxes, boxes)
    back2 = lax.rem(b - 2 * sgn + boxes, boxes)
    right = lax.rem(o + 1, groups)
    left = lax.rem(o + groups - 1, groups)
    nn = n * n
    w = a_ref.shape[2]

    barrier = pltpu.get_barrier_semaphore()
    for dev in ((b, right), (b, left), (partner, o), (back1, o), (fwd2, o), (back2, o)):
        pl.semaphore_signal(barrier, inc=1, device_id=dev, device_id_type=MESH)
    pl.semaphore_wait(barrier, 6)

    def remote(src, dst, ssem, rsem, dev):
        return pltpu.make_async_remote_copy(src_ref=src, dst_ref=dst, send_sem=ssem, recv_sem=rsem,
                                            device_id=dev, device_id_type=MESH)

    sends = {}
    for i, (k, q, dev) in enumerate(((0, 0, (b, right)), (1, 1, (b, left)), (1, 0, (b, right)), (0, 1, (b, left)))):
        sends[i] = remote(a_ref.at[k], gath.at[q, k], xs_sem.at[i], xr_sem.at[q, k], dev)
    xf0 = remote(gath.at[0, 0], gath.at[2, 0], xs_sem.at[4], xr_sem.at[2, 0], (b, right))
    xf1 = remote(gath.at[1, 1], gath.at[2, 1], xs_sem.at[5], xr_sem.at[2, 1], (b, left))
    h1 = [remote(a_ref.at[k], halo.at[1, k], hs_sem.at[k], hr_sem.at[1, k], (back1, o)) for k in range(2)]
    h2 = [remote(a_ref.at[k], halo.at[2, k], hs_sem.at[2 + k], hr_sem.at[2, k], (fwd2, o)) for k in range(2)]
    h0 = [remote(a_ref.at[k], halo.at[0, k], hs_sem.at[4 + k], hr_sem.at[0, k], (partner, o)) for k in range(2)]
    h3 = [remote(halo.at[1, k], halo.at[3, k], hs_sem.at[6 + k], hr_sem.at[3, k], (partner, o)) for k in range(2)]
    sends[0].start()
    sends[1].start()
    h1[0].start()
    h2[0].start()
    h0[0].start()
    h0[1].start()
    sends[2].start()
    sends[3].start()
    h1[1].start()
    h2[1].start()

    for k in range(2):
        R[k, :, 0:w] = (a_ref[k].astype(F32) * live_ref[k]).astype(BF16)

    T = []
    for a in range(3):
        t = jnp.zeros(bt_ref.shape[1:], F32)
        for u in range(3):
            t = t + jnp.where(ids_ref[:, a * 3 + u:a * 3 + u + 1] == gid_ref[...], bt_ref[u], 0.0)
        T.append(t * sc_ref[...])
    M = []
    for a in range(3):
        M.append(0.5 * lax.dot_general(T[a][:, 0:2 * n], T[a], (((0,), (0,)), ((), ())), precision=HIGH,
                                       preferred_element_type=F32))
    half = 2 * pad
    wide = 10 * pad
    r, c = rows_and_cols((half, 2 * n))
    rs = quotient(r, pad)
    rq = r - rs * pad
    ri1 = quotient(rq, n)
    ri2 = rq - ri1 * n
    ok = rq < nn
    cs = quotient(c, n)
    ci = c - cs * n
    L1 = jnp.where(ok & (cs == rs) & (ci == ri1), 1.0, 0.0)
    L2 = jnp.where(ok & (cs == rs) & (ci == ri2), 1.0, 0.0)
    r, c = rows_and_cols((10 * n, wide))
    cs = quotient(c, pad)
    cq = c - cs * pad
    cl1 = quotient(cq, n)
    cl2 = cq - cl1 * n
    ok = cq < nn
    rs = quotient(r, n)
    ri = r - rs * n
    C1 = jnp.where(ok & (cs == rs) & (ri == cl1), 1.0, 0.0)
    C2 = jnp.where(ok & (cs == rs) & (ri == cl2), 1.0, 0.0)
    r, c = rows_and_cols((half, wide))
    rq = r - quotient(r, pad) * pad
    cq = c - quotient(c, pad) * pad
    ri1 = quotient(rq, n)
    cl1 = quotient(cq, n)
    same1 = ri1 == cl1
    same2 = (rq - ri1 * n) == (cq - cl1 * n)
    full = jnp.where(same2, hdot(hdot(L1, M[1]), C1), 0.0) + jnp.where(same1, hdot(hdot(L2, M[2]), C2), 0.0)
    hi, lo = split_two(full)
    m12[0:half, :] = hi
    m12[half:2 * half, :] = lo
    r, c = rows_and_cols((n * 32, 2 * n))
    ri = quotient(r, 32)
    rs = quotient(r, 16) - 2 * ri
    cs = quotient(c, n)
    L0 = jnp.where((cs == rs) & ((c - cs * n) == ri), 1.0, 0.0)
    r, c = rows_and_cols((10 * n, n * 160))
    cl = quotient(c, 160)
    cs = quotient(c, 16) - 10 * cl
    rs = quotient(r, n)
    C0 = jnp.where((rs == cs) & ((r - rs * n) == cl), 1.0, 0.0)
    r, c = rows_and_cols((n * 32, n * 160))
    same = (r - 16 * quotient(r, 16)) == (c - 16 * quotient(c, 16))
    full = jnp.where(same, hdot(hdot(L0, M[0]), C0), 0.0)
    hi, lo = split_two(full)
    m0[0:n * 32, :] = hi
    m0[n * 32:n * 64, :] = lo

    def correlate(block, place):
        @pl.loop(0, w // 128)
        def _(i):
            cols = pl.ds(pl.multiple_of(i * 128, 128), 128)
            rows = pl.ds(pl.multiple_of(place * w + i * 128, 128), 128)
            total = jnp.zeros((128, w), F32)
            for k in range(2):
                total = total + lax.dot_general(block[k, :, cols], R[k, :, 0:w], (((0,), (0,)), ((), ())),
                                                preferred_element_type=F32)
            out_ref[rows, 0:w] = total

    def fock_part(block, place):
        @pl.loop(0, w // 128)
        def _(i):
            cols = pl.ds(pl.multiple_of(i * 128, 128), 128)
            rows = pl.ds(pl.multiple_of(place * w + i * 128, 128), 128)
            total = jnp.zeros((128, 2 * w), F32)
            for k in range(2):
                total = total + lax.dot_general(block[k, :, cols], R[k, :, w:3 * w], (((0,), (0,)), ((), ())),
                                                preferred_element_type=F32)
            out_ref[rows, w:2 * w] = total[:, 0:w] + total[:, w:2 * w]

    def spread(block, d):
        for l in range(n):
            for k in range(2):
                S[l, 2 * d + k, 0:nn, :] = block[k, l * nn:(l + 1) * nn, :]

    S[:, :, nn // 16 * 16:pad, :] = jnp.zeros((n, 10, pad - nn // 16 * 16, w), BF16)
    spread(a_ref, 0)
    correlate(a_ref, o)

    sends[0].wait_recv()
    xf0.start()
    sends[1].wait_recv()
    xf1.start()
    h1[0].wait_recv()
    h3[0].start()
    for k in range(2):
        h0[k].wait_recv()
    spread(halo.at[0], 1)
    h1[1].wait_recv()
    h3[1].start()
    spread(halo.at[1], 2)
    for k in range(2):
        h2[k].wait_recv()
    spread(halo.at[2], 3)
    for k in range(2):
        h3[k].wait_recv()
    spread(halo.at[3], 4)

    @pl.loop(0, n)
    def _(i):
        got = jnp.dot(m12[...], S[i].reshape(wide, w), preferred_element_type=F32)
        Wsc[i] = (got[0:half] + got[half:2 * half]).reshape(2, pad, w)

    @pl.loop(0, pad // 16)
    def _(i):
        rows = pl.ds(pl.multiple_of(i * 16, 16), 16)
        got = jnp.dot(m0[...], S[:, :, rows, :].reshape(n * 160, w), preferred_element_type=F32)
        Wsc[:, :, rows, :] = Wsc[:, :, rows, :] + (got[0:n * 32] + got[n * 32:n * 64]).reshape(n, 2, 16, w)

    for k in range(2):
        for l in range(n):
            full = Wsc[l, k] + pot_ref[k, l] * S[l, k].astype(F32)
            hi, lo = split_two(full)
            R[k, l * nn:(l + 1) * nn, w:2 * w] = hi[0:nn]
            R[k, l * nn:(l + 1) * nn, 2 * w:3 * w] = lo[0:nn]

    fock_part(a_ref, o)
    sends[2].wait_recv()
    correlate(gath.at[0], left)
    fock_part(gath.at[0], left)
    sends[3].wait_recv()
    correlate(gath.at[1], right)
    fock_part(gath.at[1], right)
    xf0.wait_recv()
    xf1.wait_recv()
    far = lax.rem(o + 2, groups)
    correlate(gath.at[2], far)
    fock_part(gath.at[2], far)
    for i in range(4):
        sends[i].wait_send()
    xf0.wait_send()
    xf1.wait_send()
    for k in range(2):
        h0[k].wait_send()
        h1[k].wait_send()
        h2[k].wait_send()
        h3[k].wait_send()


def partial_sums(orbitals, potential, deriv_blocks, levels, box_counts, neighbours):
    slots, coefs, w = orbitals.shape
    n = deriv_blocks.shape[1]
    nn = n * n
    pad = -(-nn // 16) * 16
    boxes = lax.axis_size("box")
    groups = lax.axis_size("orb")
    b = lax.axis_index("box")
    sgn = 1 - 2 * lax.rem(b, 2)
    live = (jnp.arange(slots, dtype=jnp.int32) < box_counts[0])
    scale = jnp.where(levels == 0, 0.5, jnp.where(levels == 1, 1.0, 2.0)).astype(F32)
    level_code = jnp.where(live, levels, -1)
    gid_own = b * slots + jnp.arange(slots, dtype=jnp.int32)
    ids = jnp.stack([neighbours[:, :, 0], jnp.broadcast_to(gid_own[:, None], (slots, 3)), neighbours[:, :, 1]], axis=2)
    table = jnp.concatenate([ids.reshape(slots, 9), level_code[:, None]], axis=1)
    before = lax.ppermute(table, "box", [(i, (i + 1) % boxes) for i in range(boxes)])
    after = lax.ppermute(table, "box", [(i, (i - 1) % boxes) for i in range(boxes)])
    table = jnp.concatenate([before, table, after], axis=0)
    code = table[:, 9:10]
    factor = jnp.where(code < 0, 0.0, jnp.where(code == 0, 0.5, jnp.where(code == 1, 1.0, 2.0))).astype(F32)
    ids_rows = jnp.repeat(table, n, axis=0)
    sc_rows = jnp.repeat(factor, n, axis=0)
    sources = jnp.stack([b, b + sgn, b - sgn, b - 2 * sgn, b + 2 * sgn])
    sources = (sources + boxes) % boxes
    gid = (sources[:, None] * slots + jnp.arange(slots, dtype=jnp.int32)[None, :]).reshape(-1)
    gid_cols = jnp.repeat(gid, n)[None, :]
    bt = jnp.tile(deriv_blocks.astype(F32), (1, 3 * slots, 5 * slots))
    pot = (potential * live[:, None]).astype(F32).reshape(slots, n, nn, 1)
    pot = jnp.pad(pot, ((0, 0), (0, 0), (0, pad - nn), (0, 0)))
    live_f = live.astype(F32)
    vm = pl.BlockSpec(memory_space=pltpu.VMEM)
    return pl.pallas_call(
        functools.partial(gram_kernel, n, pad, boxes, groups),
        out_shape=jax.ShapeDtypeStruct((groups * w, 2 * w), F32),
        in_specs=[vm, vm, vm, vm, vm, vm, pl.BlockSpec(memory_space=pltpu.SMEM)],
        out_specs=vm,
        scratch_shapes=[
            pltpu.VMEM((3, slots, coefs, w), BF16),
            pltpu.VMEM((4, slots, coefs, w), BF16),
            pltpu.VMEM((n, 10, pad, w), BF16),
            pltpu.VMEM((n, 2, pad, w), F32),
            pltpu.VMEM((slots, coefs, 3 * w), BF16),
            pltpu.VMEM((4 * pad, 10 * pad), BF16),
            pltpu.VMEM((n * 64, n * 160), BF16),
            pltpu.SemaphoreType.DMA((6,)),
            pltpu.SemaphoreType.DMA((3, 2)),
            pltpu.SemaphoreType.DMA((8,)),
            pltpu.SemaphoreType.DMA((4, 2)),
        ],
        compiler_params=pltpu.CompilerParams(collective_id=0, has_side_effects=True, vmem_limit_bytes=60 << 20),
        name="gram",
    )(orbitals, ids_rows, sc_rows, gid_cols, bt, pot, live_f)


def joined_along(parts, dim):
    shape = list(parts.shape[1:])
    shape[dim] *= parts.shape[0]
    return jnp.moveaxis(parts, 0, dim).reshape(shape)


def copy_for_each(value, axis):
    devices = lax.axis_size(axis)
    return lax.all_to_all(
        jnp.broadcast_to(value[None], (devices, *value.shape)), axis, 0, 0, tiled=True
    )


def gathered_copies(value, axis, dim):
    return joined_along(copy_for_each(value, axis), dim)


def product(left_block, right_block):
    gathered_row = gathered_copies(left_block, "orb", 1)
    return jnp.dot(
        gathered_row,
        gathered_copies(right_block, "box", 0),
        precision=lax.Precision.HIGHEST,
        preferred_element_type=jnp.float32,
    )


def body(orbitals, potential, deriv_blocks, levels, box_counts, neighbours):
    own_width = orbitals.shape[2]
    box_index = lax.axis_index("box")
    both = partial_sums(orbitals, potential, deriv_blocks, levels, box_counts, neighbours)
    both = lax.psum_scatter(both, "box", scatter_dimension=0, tiled=True)
    correlation, fock = both[:, :own_width], both[:, own_width:]
    block_rows = fock.shape[0]
    row_ids = box_index * block_rows + jnp.arange(block_rows, dtype=jnp.int32)
    col_ids = lax.axis_index("orb") * own_width + jnp.arange(own_width, dtype=jnp.int32)
    identity = (row_ids[:, None] == col_ids[None, :]).astype(jnp.float32)
    first_turn = 1.5 * identity - 0.5 * correlation
    scaled_root = product(correlation, first_turn)
    mixed_term = product(first_turn, scaled_root)
    second_turn = 1.5 * identity - 0.5 * mixed_term
    inverse_root = product(second_turn, first_turn)
    return (fock, correlation, inverse_root)


def solution(mesh):
    in_specs = (
        P("box", None, "orb"),
        P("box", None),
        P(),
        P("box"),
        P("box"),
        P("box", None, None),
    )
    out_specs = (P("box", "orb"), P("box", "orb"), P("box", "orb"))
    return jax.shard_map(body, mesh=mesh, in_specs=in_specs, out_specs=out_specs, check_vma=False)
```

```python
import functools

import jax
import jax.numpy as jnp
from jax import lax
from jax.experimental import pallas as pl
from jax.experimental.pallas import tpu as pltpu
from jax.sharding import PartitionSpec as P

MESH = pl.DeviceIdType.MESH
HIGH = lax.Precision.HIGHEST
F32 = jnp.float32
BF16 = jnp.bfloat16


def quotient(x, n):
    return jnp.floor((x + 0.5) * (1.0 / n))


def rows_and_cols(shape):
    r = lax.broadcasted_iota(jnp.int32, shape, 0).astype(F32)
    c = lax.broadcasted_iota(jnp.int32, shape, 1).astype(F32)
    return r, c


def split_two(x):
    hi = x.astype(BF16)
    return hi, (x - hi.astype(F32)).astype(BF16)


def hdot(a, b):
    return jnp.dot(a, b, precision=HIGH, preferred_element_type=F32)


def gram_kernel(n, pad, boxes, groups, a_ref, ids_ref, sc_ref, gid_ref, bt_ref, pot_ref, live_ref, out_ref,
                gath, halo, S, Wsc, R, m12, m0, xs_sem, xr_sem, hs_sem, hr_sem):
    b = lax.axis_index("box")
    o = lax.axis_index("orb")
    sgn = 1 - 2 * lax.rem(b, 2)
    partner = b + sgn
    back1 = lax.rem(b - sgn + boxes, boxes)
    fwd2 = lax.rem(b + 2 * sgn + boxes, boxes)
    back2 = lax.rem(b - 2 * sgn + boxes, boxes)
    right = lax.rem(o + 1, groups)
    left = lax.rem(o + groups - 1, groups)
    nn = n * n
    w = a_ref.shape[2]

    barrier = pltpu.get_barrier_semaphore()
    for dev in ((b, right), (b, left), (partner, o), (back1, o), (fwd2, o), (back2, o)):
        pl.semaphore_signal(barrier, inc=1, device_id=dev, device_id_type=MESH)
    pl.semaphore_wait(barrier, 6)

    def remote(src, dst, ssem, rsem, dev):
        return pltpu.make_async_remote_copy(src_ref=src, dst_ref=dst, send_sem=ssem, recv_sem=rsem,
                                            device_id=dev, device_id_type=MESH)

    sends = {}
    for i, (k, q, dev) in enumerate(((0, 0, (b, right)), (1, 1, (b, left)), (1, 0, (b, right)), (0, 1, (b, left)))):
        sends[i] = remote(a_ref.at[k], gath.at[q, k], xs_sem.at[i], xr_sem.at[q, k], dev)
    xf0 = remote(gath.at[0, 0], gath.at[2, 0], xs_sem.at[4], xr_sem.at[2, 0], (b, right))
    xf1 = remote(gath.at[1, 1], gath.at[2, 1], xs_sem.at[5], xr_sem.at[2, 1], (b, left))
    h1 = [remote(a_ref.at[k], halo.at[1, k], hs_sem.at[k], hr_sem.at[1, k], (back1, o)) for k in range(2)]
    h2 = [remote(a_ref.at[k], halo.at[2, k], hs_sem.at[2 + k], hr_sem.at[2, k], (fwd2, o)) for k in range(2)]
    h0 = [remote(a_ref.at[k], halo.at[0, k], hs_sem.at[4 + k], hr_sem.at[0, k], (partner, o)) for k in range(2)]
    h3 = [remote(halo.at[1, k], halo.at[3, k], hs_sem.at[6 + k], hr_sem.at[3, k], (partner, o)) for k in range(2)]
    sends[0].start()
    sends[1].start()
    h1[0].start()
    h2[0].start()
    h0[0].start()
    h0[1].start()
    sends[2].start()
    sends[3].start()
    h1[1].start()
    h2[1].start()

    for k in range(2):
        R[k, :, 0:w] = (a_ref[k].astype(F32) * live_ref[k]).astype(BF16)

    T = []
    for a in range(3):
        t = jnp.zeros(bt_ref.shape[1:], F32)
        for u in range(3):
            t = t + jnp.where(ids_ref[:, a * 3 + u:a * 3 + u + 1] == gid_ref[...], bt_ref[u], 0.0)
        T.append(t * sc_ref[...])
    M = []
    for a in range(3):
        M.append(0.5 * lax.dot_general(T[a][:, 0:2 * n], T[a], (((0,), (0,)), ((), ())), precision=HIGH,
                                       preferred_element_type=F32))
    half = 2 * pad
    wide = 10 * pad
    r, c = rows_and_cols((half, 2 * n))
    rs = quotient(r, pad)
    rq = r - rs * pad
    ri1 = quotient(rq, n)
    ri2 = rq - ri1 * n
    ok = rq < nn
    cs = quotient(c, n)
    ci = c - cs * n
    L1 = jnp.where(ok & (cs == rs) & (ci == ri1), 1.0, 0.0)
    L2 = jnp.where(ok & (cs == rs) & (ci == ri2), 1.0, 0.0)
    r, c = rows_and_cols((10 * n, wide))
    cs = quotient(c, pad)
    cq = c - cs * pad
    cl1 = quotient(cq, n)
    cl2 = cq - cl1 * n
    ok = cq < nn
    rs = quotient(r, n)
    ri = r - rs * n
    C1 = jnp.where(ok & (cs == rs) & (ri == cl1), 1.0, 0.0)
    C2 = jnp.where(ok & (cs == rs) & (ri == cl2), 1.0, 0.0)
    r, c = rows_and_cols((half, wide))
    rq = r - quotient(r, pad) * pad
    cq = c - quotient(c, pad) * pad
    ri1 = quotient(rq, n)
    cl1 = quotient(cq, n)
    same1 = ri1 == cl1
    same2 = (rq - ri1 * n) == (cq - cl1 * n)
    full = jnp.where(same2, hdot(hdot(L1, M[1]), C1), 0.0) + jnp.where(same1, hdot(hdot(L2, M[2]), C2), 0.0)
    hi, lo = split_two(full)
    m12[0:half, :] = hi
    m12[half:2 * half, :] = lo
    r, c = rows_and_cols((n * 32, 2 * n))
    ri = quotient(r, 32)
    rs = quotient(r, 16) - 2 * ri
    cs = quotient(c, n)
    L0 = jnp.where((cs == rs) & ((c - cs * n) == ri), 1.0, 0.0)
    r, c = rows_and_cols((10 * n, n * 160))
    cl = quotient(c, 160)
    cs = quotient(c, 16) - 10 * cl
    rs = quotient(r, n)
    C0 = jnp.where((rs == cs) & ((r - rs * n) == cl), 1.0, 0.0)
    r, c = rows_and_cols((n * 32, n * 160))
    same = (r - 16 * quotient(r, 16)) == (c - 16 * quotient(c, 16))
    full = jnp.where(same, hdot(hdot(L0, M[0]), C0), 0.0)
    hi, lo = split_two(full)
    m0[0:n * 32, :] = hi
    m0[n * 32:n * 64, :] = lo

    def correlate(block, place):
        @pl.loop(0, w // 128)
        def _(i):
            cols = pl.ds(pl.multiple_of(i * 128, 128), 128)
            rows = pl.ds(pl.multiple_of(place * w + i * 128, 128), 128)
            total = jnp.zeros((128, w), F32)
            for k in range(2):
                total = total + lax.dot_general(block[k, :, cols], R[k, :, 0:w], (((0,), (0,)), ((), ())),
                                                preferred_element_type=F32)
            out_ref[rows, 0:w] = total

    def fock_part(block, place):
        @pl.loop(0, w // 128)
        def _(i):
            cols = pl.ds(pl.multiple_of(i * 128, 128), 128)
            rows = pl.ds(pl.multiple_of(place * w + i * 128, 128), 128)
            total = jnp.zeros((128, 2 * w), F32)
            for k in range(2):
                total = total + lax.dot_general(block[k, :, cols], R[k, :, w:3 * w], (((0,), (0,)), ((), ())),
                                                preferred_element_type=F32)
            out_ref[rows, w:2 * w] = total[:, 0:w] + total[:, w:2 * w]

    def spread(block, d):
        for l in range(n):
            for k in range(2):
                S[l, 2 * d + k, 0:nn, :] = block[k, l * nn:(l + 1) * nn, :]

    S[:, :, nn // 16 * 16:pad, :] = jnp.zeros((n, 10, pad - nn // 16 * 16, w), BF16)
    spread(a_ref, 0)
    correlate(a_ref, o)

    sends[0].wait_recv()
    xf0.start()
    sends[1].wait_recv()
    xf1.start()
    h1[0].wait_recv()
    h3[0].start()
    for k in range(2):
        h0[k].wait_recv()
    spread(halo.at[0], 1)
    h1[1].wait_recv()
    h3[1].start()
    spread(halo.at[1], 2)
    for k in range(2):
        h2[k].wait_recv()
    spread(halo.at[2], 3)
    for k in range(2):
        h3[k].wait_recv()
    spread(halo.at[3], 4)

    @pl.loop(0, n)
    def _(i):
        got = jnp.dot(m12[...], S[i].reshape(wide, w), preferred_element_type=F32)
        Wsc[i] = (got[0:half] + got[half:2 * half]).reshape(2, pad, w)

    @pl.loop(0, pad // 16)
    def _(i):
        rows = pl.ds(pl.multiple_of(i * 16, 16), 16)
        got = jnp.dot(m0[...], S[:, :, rows, :].reshape(n * 160, w), preferred_element_type=F32)
        Wsc[:, :, rows, :] = Wsc[:, :, rows, :] + (got[0:n * 32] + got[n * 32:n * 64]).reshape(n, 2, 16, w)

    for k in range(2):
        for l in range(n):
            full = Wsc[l, k] + pot_ref[k, l] * S[l, k].astype(F32)
            hi, lo = split_two(full)
            R[k, l * nn:(l + 1) * nn, w:2 * w] = hi[0:nn]
            R[k, l * nn:(l + 1) * nn, 2 * w:3 * w] = lo[0:nn]

    fock_part(a_ref, o)
    sends[2].wait_recv()
    correlate(gath.at[0], left)
    fock_part(gath.at[0], left)
    sends[3].wait_recv()
    correlate(gath.at[1], right)
    fock_part(gath.at[1], right)
    xf0.wait_recv()
    xf1.wait_recv()
    far = lax.rem(o + 2, groups)
    correlate(gath.at[2], far)
    fock_part(gath.at[2], far)
    for i in range(4):
        sends[i].wait_send()
    xf0.wait_send()
    xf1.wait_send()
    for k in range(2):
        h0[k].wait_send()
        h1[k].wait_send()
        h2[k].wait_send()
        h3[k].wait_send()


def partial_sums(orbitals, potential, deriv_blocks, levels, box_counts, neighbours):
    slots, coefs, w = orbitals.shape
    n = deriv_blocks.shape[1]
    nn = n * n
    pad = -(-nn // 16) * 16
    boxes = lax.axis_size("box")
    groups = lax.axis_size("orb")
    b = lax.axis_index("box")
    sgn = 1 - 2 * lax.rem(b, 2)
    live = (jnp.arange(slots, dtype=jnp.int32) < box_counts[0])
    scale = jnp.where(levels == 0, 0.5, jnp.where(levels == 1, 1.0, 2.0)).astype(F32)
    level_code = jnp.where(live, levels, -1)
    gid_own = b * slots + jnp.arange(slots, dtype=jnp.int32)
    ids = jnp.stack([neighbours[:, :, 0], jnp.broadcast_to(gid_own[:, None], (slots, 3)), neighbours[:, :, 1]], axis=2)
    table = jnp.concatenate([ids.reshape(slots, 9), level_code[:, None]], axis=1)
    before = lax.ppermute(table, "box", [(i, (i + 1) % boxes) for i in range(boxes)])
    after = lax.ppermute(table, "box", [(i, (i - 1) % boxes) for i in range(boxes)])
    table = jnp.concatenate([before, table, after], axis=0)
    code = table[:, 9:10]
    factor = jnp.where(code < 0, 0.0, jnp.where(code == 0, 0.5, jnp.where(code == 1, 1.0, 2.0))).astype(F32)
    ids_rows = jnp.repeat(table, n, axis=0)
    sc_rows = jnp.repeat(factor, n, axis=0)
    sources = jnp.stack([b, b + sgn, b - sgn, b - 2 * sgn, b + 2 * sgn])
    sources = (sources + boxes) % boxes
    gid = (sources[:, None] * slots + jnp.arange(slots, dtype=jnp.int32)[None, :]).reshape(-1)
    gid_cols = jnp.repeat(gid, n)[None, :]
    bt = jnp.tile(deriv_blocks.astype(F32), (1, 3 * slots, 5 * slots))
    pot = (potential * live[:, None]).astype(F32).reshape(slots, n, nn, 1)
    pot = jnp.pad(pot, ((0, 0), (0, 0), (0, pad - nn), (0, 0)))
    live_f = live.astype(F32)
    vm = pl.BlockSpec(memory_space=pltpu.VMEM)
    return pl.pallas_call(
        functools.partial(gram_kernel, n, pad, boxes, groups),
        out_shape=jax.ShapeDtypeStruct((groups * w, 2 * w), F32),
        in_specs=[vm, vm, vm, vm, vm, vm, pl.BlockSpec(memory_space=pltpu.SMEM)],
        out_specs=vm,
        scratch_shapes=[
            pltpu.VMEM((3, slots, coefs, w), BF16),
            pltpu.VMEM((4, slots, coefs, w), BF16),
            pltpu.VMEM((n, 10, pad, w), BF16),
            pltpu.VMEM((n, 2, pad, w), F32),
            pltpu.VMEM((slots, coefs, 3 * w), BF16),
            pltpu.VMEM((4 * pad, 10 * pad), BF16),
            pltpu.VMEM((n * 64, n * 160), BF16),
            pltpu.SemaphoreType.DMA((6,)),
            pltpu.SemaphoreType.DMA((3, 2)),
            pltpu.SemaphoreType.DMA((8,)),
            pltpu.SemaphoreType.DMA((4, 2)),
        ],
        compiler_params=pltpu.CompilerParams(collective_id=0, has_side_effects=True, vmem_limit_bytes=60 << 20),
        name="gram",
    )(orbitals, ids_rows, sc_rows, gid_cols, bt, pot, live_f)


def tail_kernel(zs, ys, p_ref, fock_ref, corr_ref, inv_ref, abuf, X, B1, Y, B2, fin, cpan, qpan, crow, qrow,
                pan_hi, pan_lo, sa, ra, s1, r1, s2, r2, sg1, rg1, sg2, rg2, sf, rf, sx, rx):
    b = lax.axis_index("box")
    o = lax.axis_index("orb")
    groups = lax.axis_size("orb")
    core = lax.rem(b, 2)
    chip = b // 2
    z = chip // ys
    y = lax.rem(chip, ys)
    w = corr_ref.shape[1]
    rows = corr_ref.shape[0]
    half = rows // 2
    total = zs * ys * 2 * rows

    def at(zz, yy):
        return ((zz * ys + yy) * 2 + core, o)

    partner = (chip * 2 + 1 - core, o)
    zpeer = [at(lax.rem(z + d, zs), y) for d in range(1, zs)]
    ypeer = [at(z, lax.rem(y + d, ys)) for d in range(1, ys)]
    xpeer = [(b, lax.rem(o + d, groups)) for d in range(1, groups)]
    barrier = pltpu.get_barrier_semaphore()
    peers = [partner] + zpeer + ypeer + xpeer
    for dev in peers:
        pl.semaphore_signal(barrier, inc=1, device_id=dev, device_id_type=MESH)
    pl.semaphore_wait(barrier, len(peers))
    started = []

    def send(src, dst, ssem, rsem, dev):
        copy = pltpu.make_async_remote_copy(src_ref=src, dst_ref=dst, send_sem=ssem, recv_sem=rsem,
                                            device_id=dev, device_id_type=MESH)
        copy.start()
        started.append(copy)
        return copy

    lanes = [pl.ds(0, w), pl.ds(w, w)]
    part = [pl.ds(0, half), pl.ds(half, half)]

    first = {}
    for f in range(2):
        for h in range(2):
            first[f, h] = send(p_ref.at[:, :, 1 - core, part[h], lanes[f]], abuf.at[f, h],
                               sa.at[f, h], ra.at[f, h], partner)

    def add_pair(f, h):
        first[f, h].wait_recv()
        X[f, h] = p_ref[:, :, core, part[h], lanes[f]] + abuf[f, h]

    def scatter_one(f, h):
        out = []
        for d in range(1, ys if h == 0 else zs):
            if h == 0:
                t = lax.rem(y + d, ys)
                src = X.at[f, h, :, t]
            else:
                t = lax.rem(z + d, zs)
                src = X.at[f, h, t]
            out.append(send(src, B1.at[f, h, d - 1], s1.at[f, h, d - 1], r1.at[f, h, d - 1],
                            (ypeer if h == 0 else zpeer)[d - 1]))
        return out

    def scatter_two(f, h, copies):
        for copy in copies:
            copy.wait_recv()
        acc = X[f, h, :, y] if h == 0 else X[f, h, z]
        for d in range(1, ys if h == 0 else zs):
            acc = acc + B1[f, h, d - 1]
        Y[f, h] = acc
        out = []
        for d in range(1, zs if h == 0 else ys):
            t = lax.rem(z + d, zs) if h == 0 else lax.rem(y + d, ys)
            out.append(send(Y.at[f, h, t], B2.at[f, h, d - 1], s2.at[f, h, d - 1], r2.at[f, h, d - 1],
                            (zpeer if h == 0 else ypeer)[d - 1]))
        return out

    def scatter_end(f, h, copies):
        for copy in copies:
            copy.wait_recv()
        acc = Y[f, h, z] if h == 0 else Y[f, h, y]
        for d in range(1, zs if h == 0 else ys):
            acc = acc + B2[f, h, d - 1]
        return acc

    def gather_one(g, pan, h):
        out = []
        for d in range(1, zs if h == 0 else ys):
            out.append(send(pan.at[z, y, core, part[h]], pan.at[z, y, core, part[h]],
                            sg1.at[g, h, d - 1], rg1.at[g, h, d - 1], (zpeer if h == 0 else ypeer)[d - 1]))
        return out

    def line(pan, h, k):
        return pan.at[:, k, core, part[h]] if h == 0 else pan.at[k, :, core, part[h]]

    def gather_two(g, pan, h, copies):
        for copy in copies:
            copy.wait_recv()
        mine = line(pan, h, y if h == 0 else z)
        out = []
        for d in range(1, ys if h == 0 else zs):
            out.append(send(mine, mine, sg2.at[g, h, d - 1], rg2.at[g, h, d - 1],
                            (ypeer if h == 0 else zpeer)[d - 1]))
        fwd = send(mine, mine, sf.at[g, h, 0], rf.at[g, h, 0], partner)
        return out, fwd

    def gather_end(g, pan, h, copies, fwd):
        out = [fwd]
        n_line = ys if h == 0 else zs
        for d, copy in enumerate(copies, 1):
            copy.wait_recv()
            k = lax.rem((y if h == 0 else z) - d + n_line, n_line)
            piece = line(pan, h, k)
            out.append(send(piece, piece, sf.at[g, h, d], rf.at[g, h, d], partner))
        return out

    def row_gather(g, row, src):
        out = []
        for d in range(1, groups):
            out.append(send(src, row.at[o], sx.at[g, d - 1], rx.at[g, d - 1], xpeer[d - 1]))
        return out

    one = {}
    two = {}
    for h in range(2):
        add_pair(0, h)
        one[0, h] = scatter_one(0, h)
    for h in range(2):
        add_pair(1, h)
    for h in range(2):
        two[0, h] = scatter_two(0, h, one[0, h])
    got = {}
    for h in range(2):
        piece = scatter_end(0, h, two[0, h])
        corr_ref[part[h], :] = piece
        cpan[z, y, core, part[h]] = piece
        crow[o, part[h]] = piece
        got[h] = gather_one(0, cpan, h)
    rows_c = row_gather(0, crow, cpan.at[z, y, core])
    for h in range(2):
        got[h] = gather_two(0, cpan, h, got[h])
    for h in range(2):
        one[1, h] = scatter_one(1, h)
    got = {h: gather_end(0, cpan, h, *got[h]) for h in range(2)}

    def columns(row, f):
        return jnp.concatenate([f(row[k]) for k in range(4)], axis=1)

    def product(left, panel):
        lhi, llo = split_two(left)
        for k in range(zs):
            hi, lo = split_two(panel(k))
            span = pl.ds(k * (total // zs), total // zs)
            pan_hi[span, :] = hi
            pan_lo[span, :] = lo
        big = jnp.dot(jnp.concatenate([lhi, llo], axis=0), pan_hi[...], preferred_element_type=F32)
        return big[0:rows] + big[rows:2 * rows] + jnp.dot(lhi, pan_lo[...], preferred_element_type=F32)

    def flat(pan, k):
        return pan[k].reshape(total // zs, w)

    for copy in rows_c:
        copy.wait_recv()
    for h in range(2):
        for copy in got[h]:
            copy.wait_recv()
    left = jnp.concatenate([crow[k] for k in range(4)], axis=1)
    q = product(left, lambda k: flat(cpan, k))
    qpan[z, y, core] = q
    qrow[o] = q
    for h in range(2):
        got[h] = gather_one(1, qpan, h)
    rows_q = row_gather(1, qrow, qpan.at[z, y, core])
    for h in range(2):
        got[h] = gather_two(1, qpan, h, got[h])
    for h in range(2):
        two[1, h] = scatter_two(1, h, one[1, h])
    got = {h: gather_end(1, qpan, h, *got[h]) for h in range(2)}
    for h in range(2):
        fock_ref[part[h], :] = scatter_end(1, h, two[1, h])
    for copy in rows_q:
        copy.wait_recv()
    for h in range(2):
        for copy in got[h]:
            copy.wait_recv()
    left = jnp.concatenate([1.5 * crow[k] - 0.5 * qrow[k] for k in range(4)], axis=1)

    def diagonal(count, start):
        r = lax.broadcasted_iota(jnp.int32, (count, w), 0) + start
        c = lax.broadcasted_iota(jnp.int32, (count, w), 1) + o * w
        return r == c

    def panel(k):
        step = total // zs
        square = 0.25 * flat(qpan, k) - 1.5 * flat(cpan, k)
        return square + jnp.where(diagonal(step, k * step), 2.25, 0.0)

    right = product(left, panel)
    turn = jnp.where(diagonal(rows, b * rows), 1.5, 0.0) - 0.5 * corr_ref[...]
    inv_ref[...] = 1.5 * turn - 0.5 * right
    for copy in started:
        copy.wait_send()


def tail(both):
    boxes = lax.axis_size("box")
    groups = lax.axis_size("orb")
    w = both.shape[1] // 2
    rows = both.shape[0] // boxes
    half = rows // 2
    zs = 1
    while 2 * zs * zs < boxes:
        zs += 1
    ys = boxes // 2 // zs
    total = both.shape[0]
    far = max(zs, ys) - 1
    vm = pl.BlockSpec(memory_space=pltpu.VMEM)
    out = jax.ShapeDtypeStruct((rows, w), F32)
    dma = pltpu.SemaphoreType.DMA
    return pl.pallas_call(
        functools.partial(tail_kernel, zs, ys),
        out_shape=(out, out, out),
        in_specs=[vm],
        out_specs=(vm, vm, vm),
        scratch_shapes=[
            pltpu.VMEM((2, 2, zs, ys, half, w), F32),
            pltpu.VMEM((2, 2, zs, ys, half, w), F32),
            pltpu.VMEM((2, 2, far, zs, half, w), F32),
            pltpu.VMEM((2, 2, zs, half, w), F32),
            pltpu.VMEM((2, 2, far, half, w), F32),
            pltpu.VMEM((8, 128), F32),
            pltpu.VMEM((zs, ys, 2, rows, w), F32),
            pltpu.VMEM((zs, ys, 2, rows, w), F32),
            pltpu.VMEM((groups, rows, w), F32),
            pltpu.VMEM((groups, rows, w), F32),
            pltpu.VMEM((total, w), BF16),
            pltpu.VMEM((total, w), BF16),
            dma((2, 2)), dma((2, 2)),
            dma((2, 2, far)), dma((2, 2, far)),
            dma((2, 2, far)), dma((2, 2, far)),
            dma((2, 2, far)), dma((2, 2, far)),
            dma((2, 2, far)), dma((2, 2, far)),
            dma((2, 2, far + 1)), dma((2, 2, far + 1)),
            dma((2, groups - 1)), dma((2, groups - 1)),
        ],
        compiler_params=pltpu.CompilerParams(collective_id=1, has_side_effects=True, vmem_limit_bytes=60 << 20),
        name="tail",
    )(both.reshape(zs, ys, 2, rows, 2 * w))


def body(orbitals, potential, deriv_blocks, levels, box_counts, neighbours):
    return tail(partial_sums(orbitals, potential, deriv_blocks, levels, box_counts, neighbours))


def solution(mesh):
    in_specs = (
        P("box", None, "orb"),
        P("box", None),
        P(),
        P("box"),
        P("box"),
        P("box", None, None),
    )
    out_specs = (P("box", "orb"), P("box", "orb"), P("box", "orb"))
    return jax.shard_map(body, mesh=mesh, in_specs=in_specs, out_specs=out_specs, check_vma=False)
```

```python
import functools

import jax
import jax.numpy as jnp
from jax import lax
from jax.experimental import pallas as pl
from jax.experimental.pallas import tpu as pltpu
from jax.sharding import PartitionSpec as P

MESH = pl.DeviceIdType.MESH
HIGH = lax.Precision.HIGHEST
F32 = jnp.float32
BF16 = jnp.bfloat16


def quotient(x, n):
    return jnp.floor((x + 0.5) * (1.0 / n))


def rows_and_cols(shape):
    r = lax.broadcasted_iota(jnp.int32, shape, 0).astype(F32)
    c = lax.broadcasted_iota(jnp.int32, shape, 1).astype(F32)
    return r, c


def split_two(x):
    hi = x.astype(BF16)
    return hi, (x - hi.astype(F32)).astype(BF16)


def hdot(a, b):
    return jnp.dot(a, b, precision=HIGH, preferred_element_type=F32)


def gram_kernel(n, pad, boxes, groups, a_ref, nb_ref, lev_ref, cnt_ref, pot_ref, db_ref, out_ref,
                gath, halo, SA, SB, SC, Wsc, R, m12a, m12b, m12c, m0a, m0b, m0c, tbl, prow, pcol,
                xs_sem, xr_sem, hs_sem, hr_sem, ts_sem, tr_sem):
    b = lax.axis_index("box")
    o = lax.axis_index("orb")
    sgn = 1 - 2 * lax.rem(b, 2)
    partner = b + sgn
    back1 = lax.rem(b - sgn + boxes, boxes)
    fwd2 = lax.rem(b + 2 * sgn + boxes, boxes)
    back2 = lax.rem(b - 2 * sgn + boxes, boxes)
    right = lax.rem(o + 1, groups)
    left = lax.rem(o + groups - 1, groups)
    nn = n * n
    w = a_ref.shape[2]

    shape = tbl.shape[1:]
    r = lax.broadcasted_iota(jnp.int32, shape, 0)
    c = lax.broadcasted_iota(jnp.int32, shape, 1)
    own = jnp.zeros(shape, jnp.int32)
    for k in range(2):
        mine = (r >= k * n) & (r < (k + 1) * n)
        for a in range(3):
            own = jnp.where(mine & (c == a * 3), nb_ref[k, a, 0], own)
            own = jnp.where(mine & (c == a * 3 + 1), b * 2 + k, own)
            own = jnp.where(mine & (c == a * 3 + 2), nb_ref[k, a, 1], own)
        code = jnp.where(cnt_ref[0] > k, lev_ref[k], -1)
        own = jnp.where(mine & (c == 9), code, own)
    tbl[0] = own

    barrier = pltpu.get_barrier_semaphore()
    for dev in ((b, right), (b, left), (partner, o), (back1, o), (fwd2, o), (back2, o)):
        pl.semaphore_signal(barrier, inc=1, device_id=dev, device_id_type=MESH)
    pl.semaphore_wait(barrier, 6)

    def remote(src, dst, ssem, rsem, dev):
        return pltpu.make_async_remote_copy(src_ref=src, dst_ref=dst, send_sem=ssem, recv_sem=rsem,
                                            device_id=dev, device_id_type=MESH)

    sends = {}
    for i, (k, q, dev) in enumerate(((0, 0, (b, right)), (1, 1, (b, left)), (1, 0, (b, right)), (0, 1, (b, left)))):
        sends[i] = remote(a_ref.at[k], gath.at[q, k], xs_sem.at[i], xr_sem.at[q, k], dev)
    xf0 = remote(gath.at[0, 0], gath.at[2, 0], xs_sem.at[4], xr_sem.at[2, 0], (b, right))
    xf1 = remote(gath.at[1, 1], gath.at[2, 1], xs_sem.at[5], xr_sem.at[2, 1], (b, left))
    h1 = [remote(a_ref.at[k], halo.at[1, k], hs_sem.at[k], hr_sem.at[1, k], (back1, o)) for k in range(2)]
    h2 = [remote(a_ref.at[k], halo.at[2, k], hs_sem.at[2 + k], hr_sem.at[2, k], (fwd2, o)) for k in range(2)]
    h0 = [remote(a_ref.at[k], halo.at[0, k], hs_sem.at[4 + k], hr_sem.at[0, k], (partner, o)) for k in range(2)]
    h3 = [remote(halo.at[1, k], halo.at[3, k], hs_sem.at[6 + k], hr_sem.at[3, k], (partner, o)) for k in range(2)]
    t1 = remote(tbl.at[0], tbl.at[1], ts_sem.at[0], tr_sem.at[0], (partner, o))
    t2 = remote(tbl.at[0], tbl.at[2], ts_sem.at[1], tr_sem.at[1], (back1, o))
    sends[0].start()
    sends[1].start()
    t2.start()
    h1[0].start()
    h2[0].start()
    t1.start()
    h0[0].start()
    h0[1].start()
    sends[2].start()
    sends[3].start()
    h1[1].start()
    h2[1].start()

    alive = [jnp.where(cnt_ref[0] > k, 1.0, 0.0) for k in range(2)]
    for k in range(2):
        R[k, :, 0:w] = (a_ref[k].astype(F32) * alive[k]).astype(BF16)

    def correlate(block, place):
        @pl.loop(0, w // 128)
        def _(i):
            cols = pl.ds(pl.multiple_of(i * 128, 128), 128)
            rows = pl.ds(pl.multiple_of(place * w + i * 128, 128), 128)
            total = jnp.zeros((128, w), F32)
            for k in range(2):
                total = total + lax.dot_general(block[k, :, cols], R[k, :, 0:w], (((0,), (0,)), ((), ())),
                                                preferred_element_type=F32)
            out_ref[rows, 0:w] = total

    def fock_part(block, place):
        @pl.loop(0, w // 128)
        def _(i):
            cols = pl.ds(pl.multiple_of(i * 128, 128), 128)
            rows = pl.ds(pl.multiple_of(place * w + i * 128, 128), 128)
            total = jnp.zeros((128, 2 * w), F32)
            for k in range(2):
                total = total + lax.dot_general(block[k, :, cols], R[k, :, w:3 * w], (((0,), (0,)), ((), ())),
                                                preferred_element_type=F32)
            out_ref[rows, w:2 * w] = total[:, 0:w] + total[:, w:2 * w]

    edge = nn // 16 * 16
    for S in (SA, SB, SC):
        S[:, :, edge:pad, :] = jnp.zeros((n, S.shape[1], pad - edge, w), BF16)

    def spread(block, S, q):
        for l in range(n):
            S[l, q, 0:nn, :] = block[l * nn:(l + 1) * nn, :]

    spread(a_ref.at[0], SA, 0)
    spread(a_ref.at[1], SA, 1)
    correlate(a_ref, o)

    prow[...] = jnp.zeros(prow.shape, F32)
    prow[0:2, 0:n * nn] = pot_ref[...]
    pcol[...] = prow[...].T

    order = [(b, 0), (b, 1), (partner, 0), (partner, 1), (back1, 0), (back2, 0), (fwd2, 0), (back1, 1), (back2, 1),
             (fwd2, 1)]
    shape = (2 * n, 10 * n)
    ci = lax.broadcasted_iota(jnp.int32, shape, 1)
    gid = jnp.zeros(shape, jnp.int32)
    for q, (dev, k) in enumerate(order):
        gid = jnp.where((ci >= q * n) & (ci < (q + 1) * n), dev * 2 + k, gid)
    r, c = rows_and_cols((2 * n, n))
    pick_r = jnp.where(r - n * quotient(r, n) == c, 1.0, 0.0)
    r, c = rows_and_cols((n, 10 * n))
    pick_c = jnp.where(c - n * quotient(c, n) == r, 1.0, 0.0)
    bt = [hdot(hdot(pick_r, db_ref[u].astype(F32)), pick_c) for u in range(3)]
    t1.wait_recv()
    t2.wait_recv()
    M = [jnp.zeros(shape, F32) for _ in range(3)]
    for d in range(3):
        code = tbl[d, 0:2 * n, 9:10]
        factor = jnp.where(code < 0, 0.0, jnp.where(code == 0, 0.5, jnp.where(code == 1, 1.0, 2.0)))
        for a in range(3):
            t = jnp.zeros(shape, F32)
            for u in range(3):
                t = t + jnp.where(tbl[d, 0:2 * n, a * 3 + u:a * 3 + u + 1] == gid, bt[u], 0.0)
            t = t * factor
            M[a] = M[a] + 0.5 * lax.dot_general(t[:, 0:2 * n], t, (((0,), (0,)), ((), ())), precision=HIGH,
                                                preferred_element_type=F32)
    half = 2 * pad
    r, c = rows_and_cols((half, 2 * n))
    rs = quotient(r, pad)
    rq = r - rs * pad
    ri1 = quotient(rq, n)
    ri2 = rq - ri1 * n
    ok = rq < nn
    cs = quotient(c, n)
    ci = c - cs * n
    L1 = jnp.where(ok & (cs == rs) & (ci == ri1), 1.0, 0.0)
    L2 = jnp.where(ok & (cs == rs) & (ci == ri2), 1.0, 0.0)
    LM1 = hdot(L1, M[1])
    LM2 = hdot(L2, M[2])
    r, c = rows_and_cols((n * 32, 2 * n))
    ri = quotient(r, 32)
    rs = quotient(r, 16) - 2 * ri
    cs = quotient(c, n)
    L0 = jnp.where((cs == rs) & ((c - cs * n) == ri), 1.0, 0.0)
    LM0 = hdot(L0, M[0])

    def expand(m12, m0, base, count):
        wide = count * pad
        r, c = rows_and_cols((10 * n, wide))
        cs = quotient(c, pad)
        cq = c - cs * pad
        cl1 = quotient(cq, n)
        cl2 = cq - cl1 * n
        ok = cq < nn
        rs = quotient(r, n)
        ri = r - rs * n
        ok = ok & (cs + base == rs)
        C1 = jnp.where(ok & (ri == cl1), 1.0, 0.0)
        C2 = jnp.where(ok & (ri == cl2), 1.0, 0.0)
        r, c = rows_and_cols((half, wide))
        rq = r - quotient(r, pad) * pad
        cq = c - quotient(c, pad) * pad
        ri1 = quotient(rq, n)
        cl1 = quotient(cq, n)
        same1 = ri1 == cl1
        same2 = (rq - ri1 * n) == (cq - cl1 * n)
        full = jnp.where(same2, hdot(LM1, C1), 0.0) + jnp.where(same1, hdot(LM2, C2), 0.0)
        hi, lo = split_two(full)
        m12[0:half, :] = hi
        m12[half:2 * half, :] = lo
        step = count * 16
        r, c = rows_and_cols((10 * n, n * step))
        cl = quotient(c, step)
        cs = quotient(c - cl * step, 16)
        rs = quotient(r, n)
        C0 = jnp.where((rs == cs + base) & ((r - rs * n) == cl), 1.0, 0.0)
        r, c = rows_and_cols((n * 32, n * step))
        same = (r - 16 * quotient(r, 16)) == (c - 16 * quotient(c, 16))
        full = jnp.where(same, hdot(LM0, C0), 0.0)
        hi, lo = split_two(full)
        m0[0:n * 32, :] = hi
        m0[n * 32:n * 64, :] = lo

    def apply(S, m12, m0, fresh):
        count = S.shape[1]

        @pl.loop(0, n)
        def _(i):
            got = jnp.dot(m12[...], S[i].reshape(count * pad, w), preferred_element_type=F32)
            got = (got[0:half] + got[half:2 * half]).reshape(2, pad, w)
            Wsc[i] = got if fresh else Wsc[i] + got

        @pl.loop(0, pad // 16)
        def _(i):
            rows = pl.ds(pl.multiple_of(i * 16, 16), 16)
            got = jnp.dot(m0[...], S[:, :, rows, :].reshape(n * count * 16, w), preferred_element_type=F32)
            Wsc[:, :, rows, :] = Wsc[:, :, rows, :] + (got[0:n * 32] + got[n * 32:n * 64]).reshape(n, 2, 16, w)

    expand(m12a, m0a, 0, 4)
    for k in range(2):
        h0[k].wait_recv()
        spread(halo.at[0, k], SA, 2 + k)
    apply(SA, m12a, m0a, True)
    expand(m12b, m0b, 4, 3)
    expand(m12c, m0c, 7, 3)

    sends[0].wait_recv()
    xf0.start()
    sends[1].wait_recv()
    xf1.start()
    h1[0].wait_recv()
    h3[0].start()
    spread(halo.at[1, 0], SB, 0)
    h2[0].wait_recv()
    spread(halo.at[2, 0], SB, 1)
    h3[0].wait_recv()
    spread(halo.at[3, 0], SB, 2)
    apply(SB, m12b, m0b, False)

    h1[1].wait_recv()
    h3[1].start()
    spread(halo.at[1, 1], SC, 0)
    h2[1].wait_recv()
    spread(halo.at[2, 1], SC, 1)
    h3[1].wait_recv()
    spread(halo.at[3, 1], SC, 2)
    apply(SC, m12c, m0c, False)

    for k in range(2):
        for l in range(n):
            full = Wsc[l, k] + (pcol[l * nn:l * nn + pad, k:k + 1] * alive[k]) * SA[l, k].astype(F32)
            hi, lo = split_two(full)
            R[k, l * nn:(l + 1) * nn, w:2 * w] = hi[0:nn]
            R[k, l * nn:(l + 1) * nn, 2 * w:3 * w] = lo[0:nn]

    sends[2].wait_recv()
    correlate(gath.at[0], left)
    sends[3].wait_recv()
    correlate(gath.at[1], right)
    fock_part(a_ref, o)
    fock_part(gath.at[0], left)
    fock_part(gath.at[1], right)
    xf0.wait_recv()
    xf1.wait_recv()
    far = lax.rem(o + 2, groups)
    correlate(gath.at[2], far)
    fock_part(gath.at[2], far)
    for i in range(4):
        sends[i].wait_send()
    xf0.wait_send()
    xf1.wait_send()
    t1.wait_send()
    t2.wait_send()
    for k in range(2):
        h0[k].wait_send()
        h1[k].wait_send()
        h2[k].wait_send()
        h3[k].wait_send()


def partial_sums(orbitals, potential, deriv_blocks, levels, box_counts, neighbours):
    slots, coefs, w = orbitals.shape
    n = deriv_blocks.shape[1]
    nn = n * n
    pad = -(-nn // 16) * 16
    boxes = lax.axis_size("box")
    groups = lax.axis_size("orb")
    vm = pl.BlockSpec(memory_space=pltpu.VMEM)
    sm = pl.BlockSpec(memory_space=pltpu.SMEM)
    column = -(-((n - 1) * nn + pad) // 128) * 128
    dma = pltpu.SemaphoreType.DMA
    return pl.pallas_call(
        functools.partial(gram_kernel, n, pad, boxes, groups),
        out_shape=jax.ShapeDtypeStruct((groups * w, 2 * w), F32),
        in_specs=[vm, sm, sm, sm, vm, vm],
        out_specs=vm,
        scratch_shapes=[
            pltpu.VMEM((3, slots, coefs, w), BF16),
            pltpu.VMEM((4, slots, coefs, w), BF16),
            pltpu.VMEM((n, 4, pad, w), BF16),
            pltpu.VMEM((n, 3, pad, w), BF16),
            pltpu.VMEM((n, 3, pad, w), BF16),
            pltpu.VMEM((n, 2, pad, w), F32),
            pltpu.VMEM((slots, coefs, 3 * w), BF16),
            pltpu.VMEM((4 * pad, 4 * pad), BF16),
            pltpu.VMEM((4 * pad, 3 * pad), BF16),
            pltpu.VMEM((4 * pad, 3 * pad), BF16),
            pltpu.VMEM((n * 64, n * 64), BF16),
            pltpu.VMEM((n * 64, n * 48), BF16),
            pltpu.VMEM((n * 64, n * 48), BF16),
            pltpu.VMEM((3, -(-slots * n // 8) * 8, 128), jnp.int32),
            pltpu.VMEM((8, column), F32),
            pltpu.VMEM((column, 8), F32),
            dma((6,)), dma((3, 2)), dma((8,)), dma((4, 2)), dma((2,)), dma((2,)),
        ],
        compiler_params=pltpu.CompilerParams(collective_id=0, has_side_effects=True, vmem_limit_bytes=60 << 20),
        name="gram",
    )(orbitals, neighbours, levels, box_counts, potential, deriv_blocks)


def tail_kernel(zs, ys, p_ref, fock_ref, corr_ref, inv_ref, abuf, X, B1, Y, B2, fin, cpan, qpan, crow, qrow,
                pan_hi, pan_lo, sa, ra, s1, r1, s2, r2, sg1, rg1, sg2, rg2, sf, rf, sx, rx):
    b = lax.axis_index("box")
    o = lax.axis_index("orb")
    groups = lax.axis_size("orb")
    core = lax.rem(b, 2)
    chip = b // 2
    z = chip // ys
    y = lax.rem(chip, ys)
    w = corr_ref.shape[1]
    rows = corr_ref.shape[0]
    half = rows // 2
    total = zs * ys * 2 * rows

    def at(zz, yy):
        return ((zz * ys + yy) * 2 + core, o)

    partner = (chip * 2 + 1 - core, o)
    zpeer = [at(lax.rem(z + d, zs), y) for d in range(1, zs)]
    ypeer = [at(z, lax.rem(y + d, ys)) for d in range(1, ys)]
    xpeer = [(b, lax.rem(o + d, groups)) for d in range(1, groups)]
    barrier = pltpu.get_barrier_semaphore()
    peers = [partner] + zpeer + ypeer + xpeer
    for dev in peers:
        pl.semaphore_signal(barrier, inc=1, device_id=dev, device_id_type=MESH)
    pl.semaphore_wait(barrier, len(peers))
    started = []

    def send(src, dst, ssem, rsem, dev):
        copy = pltpu.make_async_remote_copy(src_ref=src, dst_ref=dst, send_sem=ssem, recv_sem=rsem,
                                            device_id=dev, device_id_type=MESH)
        copy.start()
        started.append(copy)
        return copy

    lanes = [pl.ds(0, w), pl.ds(w, w)]
    part = [pl.ds(0, half), pl.ds(half, half)]

    first = {}
    for f in range(2):
        for h in range(2):
            first[f, h] = send(p_ref.at[:, :, 1 - core, part[h], lanes[f]], abuf.at[f, h],
                               sa.at[f, h], ra.at[f, h], partner)

    def add_pair(f, h):
        first[f, h].wait_recv()
        X[f, h] = p_ref[:, :, core, part[h], lanes[f]] + abuf[f, h]

    def scatter_one(f, h):
        out = []
        for d in range(1, ys if h == 0 else zs):
            if h == 0:
                t = lax.rem(y + d, ys)
                src = X.at[f, h, :, t]
            else:
                t = lax.rem(z + d, zs)
                src = X.at[f, h, t]
            out.append(send(src, B1.at[f, h, d - 1], s1.at[f, h, d - 1], r1.at[f, h, d - 1],
                            (ypeer if h == 0 else zpeer)[d - 1]))
        return out

    def scatter_two(f, h, copies):
        for copy in copies:
            copy.wait_recv()
        acc = X[f, h, :, y] if h == 0 else X[f, h, z]
        for d in range(1, ys if h == 0 else zs):
            acc = acc + B1[f, h, d - 1]
        Y[f, h] = acc
        out = []
        for d in range(1, zs if h == 0 else ys):
            t = lax.rem(z + d, zs) if h == 0 else lax.rem(y + d, ys)
            out.append(send(Y.at[f, h, t], B2.at[f, h, d - 1], s2.at[f, h, d - 1], r2.at[f, h, d - 1],
                            (zpeer if h == 0 else ypeer)[d - 1]))
        return out

    def scatter_end(f, h, copies):
        for copy in copies:
            copy.wait_recv()
        acc = Y[f, h, z] if h == 0 else Y[f, h, y]
        for d in range(1, zs if h == 0 else ys):
            acc = acc + B2[f, h, d - 1]
        return acc

    def gather_one(g, pan, h):
        out = []
        for d in range(1, zs if h == 0 else ys):
            out.append(send(pan.at[z, y, core, part[h]], pan.at[z, y, core, part[h]],
                            sg1.at[g, h, d - 1], rg1.at[g, h, d - 1], (zpeer if h == 0 else ypeer)[d - 1]))
        return out

    def line(pan, h, k):
        return pan.at[:, k, core, part[h]] if h == 0 else pan.at[k, :, core, part[h]]

    def gather_two(g, pan, h, copies):
        for copy in copies:
            copy.wait_recv()
        mine = line(pan, h, y if h == 0 else z)
        out = []
        for d in range(1, ys if h == 0 else zs):
            out.append(send(mine, mine, sg2.at[g, h, d - 1], rg2.at[g, h, d - 1],
                            (ypeer if h == 0 else zpeer)[d - 1]))
        fwd = send(mine, mine, sf.at[g, h, 0], rf.at[g, h, 0], partner)
        return out, fwd

    def gather_end(g, pan, h, copies, fwd):
        out = [fwd]
        n_line = ys if h == 0 else zs
        for d, copy in enumerate(copies, 1):
            copy.wait_recv()
            k = lax.rem((y if h == 0 else z) - d + n_line, n_line)
            piece = line(pan, h, k)
            out.append(send(piece, piece, sf.at[g, h, d], rf.at[g, h, d], partner))
        return out

    def row_gather(g, row, src):
        out = []
        for d in range(1, groups):
            out.append(send(src, row.at[o], sx.at[g, d - 1], rx.at[g, d - 1], xpeer[d - 1]))
        return out

    one = {}
    two = {}
    for h in range(2):
        add_pair(0, h)
        one[0, h] = scatter_one(0, h)
    for h in range(2):
        add_pair(1, h)
    for h in range(2):
        two[0, h] = scatter_two(0, h, one[0, h])
    got = {}
    for h in range(2):
        piece = scatter_end(0, h, two[0, h])
        corr_ref[part[h], :] = piece
        cpan[z, y, core, part[h]] = piece
        crow[o, part[h]] = piece
        got[h] = gather_one(0, cpan, h)
    rows_c = row_gather(0, crow, cpan.at[z, y, core])
    for h in range(2):
        got[h] = gather_two(0, cpan, h, got[h])
    for h in range(2):
        one[1, h] = scatter_one(1, h)
    got = {h: gather_end(0, cpan, h, *got[h]) for h in range(2)}

    def columns(row, f):
        return jnp.concatenate([f(row[k]) for k in range(4)], axis=1)

    def product(left, panel):
        lhi, llo = split_two(left)
        for k in range(zs):
            hi, lo = split_two(panel(k))
            span = pl.ds(k * (total // zs), total // zs)
            pan_hi[span, :] = hi
            pan_lo[span, :] = lo
        big = jnp.dot(jnp.concatenate([lhi, llo], axis=0), pan_hi[...], preferred_element_type=F32)
        return big[0:rows] + big[rows:2 * rows] + jnp.dot(lhi, pan_lo[...], preferred_element_type=F32)

    def flat(pan, k):
        return pan[k].reshape(total // zs, w)

    for copy in rows_c:
        copy.wait_recv()
    for h in range(2):
        for copy in got[h]:
            copy.wait_recv()
    left = jnp.concatenate([crow[k] for k in range(4)], axis=1)
    q = product(left, lambda k: flat(cpan, k))
    qpan[z, y, core] = q
    qrow[o] = q
    for h in range(2):
        got[h] = gather_one(1, qpan, h)
    rows_q = row_gather(1, qrow, qpan.at[z, y, core])
    for h in range(2):
        got[h] = gather_two(1, qpan, h, got[h])
    for h in range(2):
        two[1, h] = scatter_two(1, h, one[1, h])
    got = {h: gather_end(1, qpan, h, *got[h]) for h in range(2)}
    for h in range(2):
        fock_ref[part[h], :] = scatter_end(1, h, two[1, h])
    for copy in rows_q:
        copy.wait_recv()
    for h in range(2):
        for copy in got[h]:
            copy.wait_recv()
    left = jnp.concatenate([1.5 * crow[k] - 0.5 * qrow[k] for k in range(4)], axis=1)

    def diagonal(count, start):
        r = lax.broadcasted_iota(jnp.int32, (count, w), 0) + start
        c = lax.broadcasted_iota(jnp.int32, (count, w), 1) + o * w
        return r == c

    def panel(k):
        step = total // zs
        square = 0.25 * flat(qpan, k) - 1.5 * flat(cpan, k)
        return square + jnp.where(diagonal(step, k * step), 2.25, 0.0)

    right = product(left, panel)
    turn = jnp.where(diagonal(rows, b * rows), 1.5, 0.0) - 0.5 * corr_ref[...]
    inv_ref[...] = 1.5 * turn - 0.5 * right
    for copy in started:
        copy.wait_send()


def tail(both):
    boxes = lax.axis_size("box")
    groups = lax.axis_size("orb")
    w = both.shape[1] // 2
    rows = both.shape[0] // boxes
    half = rows // 2
    zs = 1
    while 2 * zs * zs < boxes:
        zs += 1
    ys = boxes // 2 // zs
    total = both.shape[0]
    far = max(zs, ys) - 1
    vm = pl.BlockSpec(memory_space=pltpu.VMEM)
    out = jax.ShapeDtypeStruct((rows, w), F32)
    dma = pltpu.SemaphoreType.DMA
    return pl.pallas_call(
        functools.partial(tail_kernel, zs, ys),
        out_shape=(out, out, out),
        in_specs=[vm],
        out_specs=(vm, vm, vm),
        scratch_shapes=[
            pltpu.VMEM((2, 2, zs, ys, half, w), F32),
            pltpu.VMEM((2, 2, zs, ys, half, w), F32),
            pltpu.VMEM((2, 2, far, zs, half, w), F32),
            pltpu.VMEM((2, 2, zs, half, w), F32),
            pltpu.VMEM((2, 2, far, half, w), F32),
            pltpu.VMEM((8, 128), F32),
            pltpu.VMEM((zs, ys, 2, rows, w), F32),
            pltpu.VMEM((zs, ys, 2, rows, w), F32),
            pltpu.VMEM((groups, rows, w), F32),
            pltpu.VMEM((groups, rows, w), F32),
            pltpu.VMEM((total, w), BF16),
            pltpu.VMEM((total, w), BF16),
            dma((2, 2)), dma((2, 2)),
            dma((2, 2, far)), dma((2, 2, far)),
            dma((2, 2, far)), dma((2, 2, far)),
            dma((2, 2, far)), dma((2, 2, far)),
            dma((2, 2, far)), dma((2, 2, far)),
            dma((2, 2, far + 1)), dma((2, 2, far + 1)),
            dma((2, groups - 1)), dma((2, groups - 1)),
        ],
        compiler_params=pltpu.CompilerParams(collective_id=1, has_side_effects=True, vmem_limit_bytes=60 << 20),
        name="tail",
    )(both.reshape(zs, ys, 2, rows, 2 * w))


def settle_kernel(*refs):
    for src, dst in zip(refs[:3], refs[3:]):
        dst[...] = src[...]


def settle(arrays):
    vm = pl.BlockSpec(memory_space=pltpu.VMEM)
    return pl.pallas_call(
        settle_kernel,
        out_shape=tuple(jax.ShapeDtypeStruct(a.shape, a.dtype) for a in arrays),
        in_specs=[vm] * 3,
        out_specs=(vm,) * 3,
        name="settle",
    )(*arrays)


def body(orbitals, potential, deriv_blocks, levels, box_counts, neighbours):
    return settle(tail(partial_sums(orbitals, potential, deriv_blocks, levels, box_counts, neighbours)))


def solution(mesh):
    in_specs = (
        P("box", None, "orb"),
        P("box", None),
        P(),
        P("box"),
        P("box"),
        P("box", None, None),
    )
    out_specs = (P("box", "orb"), P("box", "orb"), P("box", "orb"))
    return jax.shard_map(body, mesh=mesh, in_specs=in_specs, out_specs=out_specs, check_vma=False)
```

```python
import functools

import jax
import jax.numpy as jnp
from jax import lax
from jax.experimental import pallas as pl
from jax.experimental.pallas import tpu as pltpu
from jax.sharding import PartitionSpec as P

MESH = pl.DeviceIdType.MESH
HIGH = lax.Precision.HIGHEST
F32 = jnp.float32
BF16 = jnp.bfloat16


def quotient(x, n):
    return jnp.floor((x + 0.5) * (1.0 / n))


def rows_and_cols(shape):
    r = lax.broadcasted_iota(jnp.int32, shape, 0).astype(F32)
    c = lax.broadcasted_iota(jnp.int32, shape, 1).astype(F32)
    return r, c


def split_two(x):
    hi = x.astype(BF16)
    return hi, (x - hi.astype(F32)).astype(BF16)


def hdot(a, b):
    return jnp.dot(a, b, precision=HIGH, preferred_element_type=F32)


def whole_kernel(n, pad, zs, ys, a_ref, nb_ref, lev_ref, cnt_ref, pot_ref, db_ref, fock_ref, corr_ref, inv_ref,
                 gath, halo, SA, SB, SC, Wsc, R, m12a, m12b, m12c, m0a, m0b, m0c, tbl, prow, pcol,
                 p_ref, abuf, X, B1, Y, B2, cpan, qpan, crow, qrow, pan_hi, pan_lo,
                 xs_sem, xr_sem, hs_sem, hr_sem, ts_sem, tr_sem,
                 sa, ra, s1, r1, s2, r2, sg1, rg1, sg2, rg2, sf, rf, sx, rx):
    b = lax.axis_index("box")
    o = lax.axis_index("orb")
    boxes = lax.axis_size("box")
    groups = lax.axis_size("orb")
    core = lax.rem(b, 2)
    chip = b // 2
    z = chip // ys
    y = lax.rem(chip, ys)
    sgn = 1 - 2 * core
    mate = b + sgn
    back1 = lax.rem(b - sgn + boxes, boxes)
    fwd2 = lax.rem(b + 2 * sgn + boxes, boxes)
    back2 = lax.rem(b - 2 * sgn + boxes, boxes)
    right = lax.rem(o + 1, groups)
    left = lax.rem(o + groups - 1, groups)
    nn = n * n
    w = a_ref.shape[2]
    rows = corr_ref.shape[0]
    half_rows = rows // 2
    total_rows = zs * ys * 2 * rows

    def at(zz, yy):
        return ((zz * ys + yy) * 2 + core, o)

    partner = (mate, o)
    zpeer = [at(lax.rem(z + d, zs), y) for d in range(1, zs)]
    ypeer = [at(z, lax.rem(y + d, ys)) for d in range(1, ys)]
    xpeer = [(b, lax.rem(o + d, groups)) for d in range(1, groups)]

    shape = tbl.shape[1:]
    r = lax.broadcasted_iota(jnp.int32, shape, 0)
    c = lax.broadcasted_iota(jnp.int32, shape, 1)
    own = jnp.zeros(shape, jnp.int32)
    for k in range(2):
        mine = (r >= k * n) & (r < (k + 1) * n)
        for a in range(3):
            own = jnp.where(mine & (c == a * 3), nb_ref[k, 0, a], own)
            own = jnp.where(mine & (c == a * 3 + 1), b * 2 + k, own)
            own = jnp.where(mine & (c == a * 3 + 2), nb_ref[k, 1, a], own)
        code = jnp.where(cnt_ref[0] > k, lev_ref[k], -1)
        own = jnp.where(mine & (c == 9), code, own)
    tbl[0] = own

    barrier = pltpu.get_barrier_semaphore()
    peers = [partner, (back1, o), (fwd2, o), (back2, o)] + xpeer + ypeer + zpeer
    for dev in peers:
        pl.semaphore_signal(barrier, inc=1, device_id=dev, device_id_type=MESH)
    pl.semaphore_wait(barrier, len(peers))

    def remote(src, dst, ssem, rsem, dev):
        return pltpu.make_async_remote_copy(src_ref=src, dst_ref=dst, send_sem=ssem, recv_sem=rsem,
                                            device_id=dev, device_id_type=MESH)

    sends = {}
    for i, (k, q, dev) in enumerate(((0, 0, (b, right)), (1, 1, (b, left)), (1, 0, (b, right)), (0, 1, (b, left)))):
        sends[i] = remote(a_ref.at[k], gath.at[q, k], xs_sem.at[i], xr_sem.at[q, k], dev)
    xf0 = remote(gath.at[0, 0], gath.at[2, 0], xs_sem.at[4], xr_sem.at[2, 0], (b, right))
    xf1 = remote(gath.at[1, 1], gath.at[2, 1], xs_sem.at[5], xr_sem.at[2, 1], (b, left))
    h1 = [remote(a_ref.at[k], halo.at[1, k], hs_sem.at[k], hr_sem.at[1, k], (back1, o)) for k in range(2)]
    h2 = [remote(a_ref.at[k], halo.at[2, k], hs_sem.at[2 + k], hr_sem.at[2, k], (fwd2, o)) for k in range(2)]
    h0 = [remote(a_ref.at[k], halo.at[0, k], hs_sem.at[4 + k], hr_sem.at[0, k], partner) for k in range(2)]
    h3 = [remote(halo.at[1, k], halo.at[3, k], hs_sem.at[6 + k], hr_sem.at[3, k], partner) for k in range(2)]
    t1 = remote(tbl.at[0], tbl.at[1], ts_sem.at[0], tr_sem.at[0], partner)
    t2 = remote(tbl.at[0], tbl.at[2], ts_sem.at[1], tr_sem.at[1], (back1, o))
    sends[0].start()
    sends[1].start()
    t2.start()
    h1[0].start()
    h2[0].start()
    t1.start()
    h0[0].start()
    h0[1].start()
    sends[2].start()
    sends[3].start()
    h1[1].start()
    h2[1].start()

    alive = [jnp.where(cnt_ref[0] > k, 1.0, 0.0) for k in range(2)]
    for k in range(2):
        R[k, :, 0:w] = (a_ref[k].astype(F32) * alive[k]).astype(BF16)

    def correlate(block, place):
        total = jnp.zeros((w, w), F32)
        for k in range(2):
            total = total + lax.dot_general(block[k], R[k, :, 0:w], (((0,), (0,)), ((), ())),
                                            preferred_element_type=F32)
        p_ref[0, place] = total.reshape(ys, 2, rows, w)

    def fock_part(block, place):
        total = jnp.zeros((w, 2 * w), F32)
        for k in range(2):
            total = total + lax.dot_general(block[k], R[k, :, w:3 * w], (((0,), (0,)), ((), ())),
                                            preferred_element_type=F32)
        p_ref[1, place] = (total[:, 0:w] + total[:, w:2 * w]).reshape(ys, 2, rows, w)

    edge = nn // 16 * 16
    for S in (SA, SB, SC):
        S[:, :, edge:pad, :] = jnp.zeros((n, S.shape[1], pad - edge, w), BF16)

    def spread(block, S, q):
        for l in range(n):
            S[l, q, 0:nn, :] = block[l * nn:(l + 1) * nn, :]

    spread(a_ref.at[0], SA, 0)
    spread(a_ref.at[1], SA, 1)
    correlate(a_ref, o)

    prow[...] = jnp.zeros(prow.shape, F32)
    prow[0:2, 0:n * nn] = pot_ref[...]
    pcol[...] = prow[...].T

    order = [(b, 0), (b, 1), (mate, 0), (mate, 1), (back1, 0), (back2, 0), (fwd2, 0), (back1, 1), (back2, 1),
             (fwd2, 1)]
    shape = (2 * n, 10 * n)
    ci = lax.broadcasted_iota(jnp.int32, shape, 1)
    gid = jnp.zeros(shape, jnp.int32)
    for q, (dev, k) in enumerate(order):
        gid = jnp.where((ci >= q * n) & (ci < (q + 1) * n), dev * 2 + k, gid)
    r, c = rows_and_cols((2 * n, n))
    pick_r = jnp.where(r - n * quotient(r, n) == c, 1.0, 0.0)
    r, c = rows_and_cols((n, 10 * n))
    pick_c = jnp.where(c - n * quotient(c, n) == r, 1.0, 0.0)
    bt = [hdot(hdot(pick_r, db_ref[:, u, :].astype(F32)), pick_c) for u in range(3)]
    t1.wait_recv()
    t2.wait_recv()
    M = [jnp.zeros(shape, F32) for _ in range(3)]
    for d in range(3):
        code = tbl[d, 0:2 * n, 9:10]
        factor = jnp.where(code < 0, 0.0, jnp.where(code == 0, 0.5, jnp.where(code == 1, 1.0, 2.0)))
        for a in range(3):
            t = jnp.zeros(shape, F32)
            for u in range(3):
                t = t + jnp.where(tbl[d, 0:2 * n, a * 3 + u:a * 3 + u + 1] == gid, bt[u], 0.0)
            t = t * factor
            M[a] = M[a] + 0.5 * lax.dot_general(t[:, 0:2 * n], t, (((0,), (0,)), ((), ())), precision=HIGH,
                                                preferred_element_type=F32)
    half = 2 * pad
    r, c = rows_and_cols((half, 2 * n))
    rs = quotient(r, pad)
    rq = r - rs * pad
    ri1 = quotient(rq, n)
    ri2 = rq - ri1 * n
    ok = rq < nn
    cs = quotient(c, n)
    ci = c - cs * n
    L1 = jnp.where(ok & (cs == rs) & (ci == ri1), 1.0, 0.0)
    L2 = jnp.where(ok & (cs == rs) & (ci == ri2), 1.0, 0.0)
    LM1 = hdot(L1, M[1])
    LM2 = hdot(L2, M[2])
    r, c = rows_and_cols((n * 32, 2 * n))
    ri = quotient(r, 32)
    rs = quotient(r, 16) - 2 * ri
    cs = quotient(c, n)
    L0 = jnp.where((cs == rs) & ((c - cs * n) == ri), 1.0, 0.0)
    LM0 = hdot(L0, M[0])

    def expand(m12, m0, base, count):
        wide = count * pad
        r, c = rows_and_cols((10 * n, wide))
        cs = quotient(c, pad)
        cq = c - cs * pad
        cl1 = quotient(cq, n)
        cl2 = cq - cl1 * n
        ok = cq < nn
        rs = quotient(r, n)
        ri = r - rs * n
        ok = ok & (cs + base == rs)
        C1 = jnp.where(ok & (ri == cl1), 1.0, 0.0)
        C2 = jnp.where(ok & (ri == cl2), 1.0, 0.0)
        r, c = rows_and_cols((half, wide))
        rq = r - quotient(r, pad) * pad
        cq = c - quotient(c, pad) * pad
        ri1 = quotient(rq, n)
        cl1 = quotient(cq, n)
        same1 = ri1 == cl1
        same2 = (rq - ri1 * n) == (cq - cl1 * n)
        full = jnp.where(same2, hdot(LM1, C1), 0.0) + jnp.where(same1, hdot(LM2, C2), 0.0)
        hi, lo = split_two(full)
        m12[0:half, :] = hi
        m12[half:2 * half, :] = lo
        step = count * 16
        r, c = rows_and_cols((10 * n, n * step))
        cl = quotient(c, step)
        cs = quotient(c - cl * step, 16)
        rs = quotient(r, n)
        C0 = jnp.where((rs == cs + base) & ((r - rs * n) == cl), 1.0, 0.0)
        r, c = rows_and_cols((n * 32, n * step))
        same = (r - 16 * quotient(r, 16)) == (c - 16 * quotient(c, 16))
        full = jnp.where(same, hdot(LM0, C0), 0.0)
        hi, lo = split_two(full)
        m0[0:n * 32, :] = hi
        m0[n * 32:n * 64, :] = lo

    def apply(S, m12, m0, fresh):
        count = S.shape[1]

        @pl.loop(0, n)
        def _(i):
            got = jnp.dot(m12[...], S[i].reshape(count * pad, w), preferred_element_type=F32)
            got = (got[0:half] + got[half:2 * half]).reshape(2, pad, w)
            Wsc[i] = got if fresh else Wsc[i] + got

        @pl.loop(0, pad // 16)
        def _(i):
            rows = pl.ds(pl.multiple_of(i * 16, 16), 16)
            got = jnp.dot(m0[...], S[:, :, rows, :].reshape(n * count * 16, w), preferred_element_type=F32)
            Wsc[:, :, rows, :] = Wsc[:, :, rows, :] + (got[0:n * 32] + got[n * 32:n * 64]).reshape(n, 2, 16, w)

    expand(m12a, m0a, 0, 4)
    for k in range(2):
        h0[k].wait_recv()
        spread(halo.at[0, k], SA, 2 + k)
    apply(SA, m12a, m0a, True)
    expand(m12b, m0b, 4, 3)
    expand(m12c, m0c, 7, 3)

    sends[0].wait_recv()
    xf0.start()
    sends[1].wait_recv()
    xf1.start()
    h1[0].wait_recv()
    h3[0].start()
    spread(halo.at[1, 0], SB, 0)
    h2[0].wait_recv()
    spread(halo.at[2, 0], SB, 1)
    h3[0].wait_recv()
    spread(halo.at[3, 0], SB, 2)
    apply(SB, m12b, m0b, False)

    h1[1].wait_recv()
    h3[1].start()
    spread(halo.at[1, 1], SC, 0)
    h2[1].wait_recv()
    spread(halo.at[2, 1], SC, 1)
    h3[1].wait_recv()
    spread(halo.at[3, 1], SC, 2)
    apply(SC, m12c, m0c, False)

    for k in range(2):
        for l in range(n):
            full = Wsc[l, k] + (pcol[l * nn:l * nn + pad, k:k + 1] * alive[k]) * SA[l, k].astype(F32)
            hi, lo = split_two(full)
            R[k, l * nn:(l + 1) * nn, w:2 * w] = hi[0:nn]
            R[k, l * nn:(l + 1) * nn, 2 * w:3 * w] = lo[0:nn]

    sends[2].wait_recv()
    correlate(gath.at[0], left)
    sends[3].wait_recv()
    correlate(gath.at[1], right)
    fock_part(a_ref, o)
    fock_part(gath.at[0], left)
    fock_part(gath.at[1], right)
    xf0.wait_recv()
    xf1.wait_recv()
    far = lax.rem(o + 2, groups)
    correlate(gath.at[2], far)
    started = []

    def send(src, dst, ssem, rsem, dev):
        copy = pltpu.make_async_remote_copy(src_ref=src, dst_ref=dst, send_sem=ssem, recv_sem=rsem,
                                            device_id=dev, device_id_type=MESH)
        copy.start()
        started.append(copy)
        return copy

    part = [pl.ds(0, half_rows), pl.ds(half_rows, half_rows)]

    first = {}

    def pair_exchange(f):
        for h in range(2):
            first[f, h] = send(p_ref.at[f, :, :, 1 - core, part[h]], abuf.at[f, h], sa.at[f, h], ra.at[f, h], partner)

    def add_pair(f, h):
        first[f, h].wait_recv()
        X[f, h] = p_ref[f, :, :, core, part[h]] + abuf[f, h]

    def scatter_one(f, h):
        out = []
        for d in range(1, ys if h == 0 else zs):
            if h == 0:
                t = lax.rem(y + d, ys)
                src = X.at[f, h, :, t]
            else:
                t = lax.rem(z + d, zs)
                src = X.at[f, h, t]
            out.append(send(src, B1.at[f, h, d - 1], s1.at[f, h, d - 1], r1.at[f, h, d - 1],
                            (ypeer if h == 0 else zpeer)[d - 1]))
        return out

    def scatter_two(f, h, copies):
        for copy in copies:
            copy.wait_recv()
        acc = X[f, h, :, y] if h == 0 else X[f, h, z]
        for d in range(1, ys if h == 0 else zs):
            acc = acc + B1[f, h, d - 1]
        Y[f, h] = acc
        out = []
        for d in range(1, zs if h == 0 else ys):
            t = lax.rem(z + d, zs) if h == 0 else lax.rem(y + d, ys)
            out.append(send(Y.at[f, h, t], B2.at[f, h, d - 1], s2.at[f, h, d - 1], r2.at[f, h, d - 1],
                            (zpeer if h == 0 else ypeer)[d - 1]))
        return out

    def scatter_end(f, h, copies):
        for copy in copies:
            copy.wait_recv()
        acc = Y[f, h, z] if h == 0 else Y[f, h, y]
        for d in range(1, zs if h == 0 else ys):
            acc = acc + B2[f, h, d - 1]
        return acc

    def gather_one(g, pan, h):
        out = []
        for d in range(1, zs if h == 0 else ys):
            out.append(send(pan.at[z, y, core, part[h]], pan.at[z, y, core, part[h]],
                            sg1.at[g, h, d - 1], rg1.at[g, h, d - 1], (zpeer if h == 0 else ypeer)[d - 1]))
        return out

    def line(pan, h, k):
        return pan.at[:, k, core, part[h]] if h == 0 else pan.at[k, :, core, part[h]]

    def gather_two(g, pan, h, copies):
        for copy in copies:
            copy.wait_recv()
        mine = line(pan, h, y if h == 0 else z)
        out = []
        for d in range(1, ys if h == 0 else zs):
            out.append(send(mine, mine, sg2.at[g, h, d - 1], rg2.at[g, h, d - 1],
                            (ypeer if h == 0 else zpeer)[d - 1]))
        fwd = send(mine, mine, sf.at[g, h, 0], rf.at[g, h, 0], partner)
        return out, fwd

    def gather_end(g, pan, h, copies, fwd):
        out = [fwd]
        n_line = ys if h == 0 else zs
        for d, copy in enumerate(copies, 1):
            copy.wait_recv()
            k = lax.rem((y if h == 0 else z) - d + n_line, n_line)
            piece = line(pan, h, k)
            out.append(send(piece, piece, sf.at[g, h, d], rf.at[g, h, d], partner))
        return out

    def row_gather(g, row, src):
        out = []
        for d in range(1, groups):
            out.append(send(src, row.at[o], sx.at[g, d - 1], rx.at[g, d - 1], xpeer[d - 1]))
        return out

    pair_exchange(0)
    fock_part(gath.at[2], far)
    pair_exchange(1)
    one = {}
    two = {}
    for h in range(2):
        add_pair(0, h)
        one[0, h] = scatter_one(0, h)
    for h in range(2):
        add_pair(1, h)
    for h in range(2):
        two[0, h] = scatter_two(0, h, one[0, h])
    got = {}
    for h in range(2):
        piece = scatter_end(0, h, two[0, h])
        corr_ref[part[h], :] = piece
        cpan[z, y, core, part[h]] = piece
        crow[o, part[h]] = piece
        got[h] = gather_one(0, cpan, h)
    rows_c = row_gather(0, crow, cpan.at[z, y, core])
    for h in range(2):
        got[h] = gather_two(0, cpan, h, got[h])
    for h in range(2):
        one[1, h] = scatter_one(1, h)
    got = {h: gather_end(0, cpan, h, *got[h]) for h in range(2)}

    def product(left, panel):
        lhi, llo = split_two(left)
        for k in range(zs):
            hi, lo = split_two(panel(k))
            span = pl.ds(k * (total_rows // zs), total_rows // zs)
            pan_hi[span, :] = hi
            pan_lo[span, :] = lo
        big = jnp.dot(jnp.concatenate([lhi, llo], axis=0), pan_hi[...], preferred_element_type=F32)
        return big[0:rows] + big[rows:2 * rows] + jnp.dot(lhi, pan_lo[...], preferred_element_type=F32)

    def flat(pan, k):
        return pan[k].reshape(total_rows // zs, w)

    for copy in rows_c:
        copy.wait_recv()
    for h in range(2):
        for copy in got[h]:
            copy.wait_recv()
    left = jnp.concatenate([crow[k] for k in range(groups)], axis=1)
    q = product(left, lambda k: flat(cpan, k))
    qpan[z, y, core] = q
    qrow[o] = q
    for h in range(2):
        got[h] = gather_one(1, qpan, h)
    rows_q = row_gather(1, qrow, qpan.at[z, y, core])
    for h in range(2):
        got[h] = gather_two(1, qpan, h, got[h])
    for h in range(2):
        two[1, h] = scatter_two(1, h, one[1, h])
    got = {h: gather_end(1, qpan, h, *got[h]) for h in range(2)}
    for h in range(2):
        fock_ref[part[h], :] = scatter_end(1, h, two[1, h])
    for copy in rows_q:
        copy.wait_recv()
    for h in range(2):
        for copy in got[h]:
            copy.wait_recv()
    left = jnp.concatenate([1.5 * crow[k] - 0.5 * qrow[k] for k in range(groups)], axis=1)

    def diagonal(count, start):
        r = lax.broadcasted_iota(jnp.int32, (count, w), 0) + start
        c = lax.broadcasted_iota(jnp.int32, (count, w), 1) + o * w
        return r == c

    def panel(k):
        step = total_rows // zs
        square = 0.25 * flat(qpan, k) - 1.5 * flat(cpan, k)
        return square + jnp.where(diagonal(step, k * step), 2.25, 0.0)

    right = product(left, panel)
    turn = jnp.where(diagonal(rows, b * rows), 1.5, 0.0) - 0.5 * corr_ref[...]
    inv_ref[...] = 1.5 * turn - 0.5 * right
    for copy in started:
        copy.wait_send()
    for i in range(4):
        sends[i].wait_send()
    xf0.wait_send()
    xf1.wait_send()
    t1.wait_send()
    t2.wait_send()
    for k in range(2):
        h0[k].wait_send()
        h1[k].wait_send()
        h2[k].wait_send()
        h3[k].wait_send()


def whole(orbitals, potential, deriv_blocks, levels, box_counts, neighbours):
    slots, coefs, w = orbitals.shape
    n = deriv_blocks.shape[1]
    nn = n * n
    pad = -(-nn // 16) * 16
    boxes = lax.axis_size("box")
    groups = lax.axis_size("orb")
    zs = 1
    while 2 * zs * zs < boxes:
        zs += 1
    ys = boxes // 2 // zs
    total = groups * w
    rows = total // boxes
    half = rows // 2
    far = max(zs, ys) - 1
    vm = pl.BlockSpec(memory_space=pltpu.VMEM)
    sm = pl.BlockSpec(memory_space=pltpu.SMEM)
    column = -(-((n - 1) * nn + pad) // 128) * 128
    dma = pltpu.SemaphoreType.DMA
    out = jax.ShapeDtypeStruct((rows, w), F32)
    return pl.pallas_call(
        functools.partial(whole_kernel, n, pad, zs, ys),
        out_shape=(out, out, out),
        in_specs=[vm, sm, sm, sm, vm, vm],
        out_specs=(vm, vm, vm),
        scratch_shapes=[
            pltpu.VMEM((3, slots, coefs, w), BF16),
            pltpu.VMEM((4, slots, coefs, w), BF16),
            pltpu.VMEM((n, 4, pad, w), BF16),
            pltpu.VMEM((n, 3, pad, w), BF16),
            pltpu.VMEM((n, 3, pad, w), BF16),
            pltpu.VMEM((n, 2, pad, w), F32),
            pltpu.VMEM((slots, coefs, 3 * w), BF16),
            pltpu.VMEM((4 * pad, 4 * pad), BF16),
            pltpu.VMEM((4 * pad, 3 * pad), BF16),
            pltpu.VMEM((4 * pad, 3 * pad), BF16),
            pltpu.VMEM((n * 64, n * 64), BF16),
            pltpu.VMEM((n * 64, n * 48), BF16),
            pltpu.VMEM((n * 64, n * 48), BF16),
            pltpu.VMEM((3, -(-slots * n // 8) * 8, 128), jnp.int32),
            pltpu.VMEM((8, column), F32),
            pltpu.VMEM((column, 8), F32),
            pltpu.VMEM((2, groups, total // groups // (2 * rows), 2, rows, w), F32),
            pltpu.VMEM((2, 2, zs, ys, half, w), F32),
            pltpu.VMEM((2, 2, zs, ys, half, w), F32),
            pltpu.VMEM((2, 2, far, zs, half, w), F32),
            pltpu.VMEM((2, 2, zs, half, w), F32),
            pltpu.VMEM((2, 2, far, half, w), F32),
            pltpu.VMEM((zs, ys, 2, rows, w), F32),
            pltpu.VMEM((zs, ys, 2, rows, w), F32),
            pltpu.VMEM((groups, rows, w), F32),
            pltpu.VMEM((groups, rows, w), F32),
            pltpu.VMEM((total, w), BF16),
            pltpu.VMEM((total, w), BF16),
            dma((6,)), dma((3, 2)), dma((8,)), dma((4, 2)), dma((2,)), dma((2,)),
            dma((2, 2)), dma((2, 2)),
            dma((2, 2, far)), dma((2, 2, far)),
            dma((2, 2, far)), dma((2, 2, far)),
            dma((2, 2, far)), dma((2, 2, far)),
            dma((2, 2, far)), dma((2, 2, far)),
            dma((2, 2, far + 1)), dma((2, 2, far + 1)),
            dma((2, groups - 1)), dma((2, groups - 1)),
        ],
        compiler_params=pltpu.CompilerParams(collective_id=0, has_side_effects=True, vmem_limit_bytes=63 << 20),
        name="whole",
    )(orbitals, jnp.transpose(neighbours, (0, 2, 1)), levels, box_counts, potential,
      jnp.transpose(deriv_blocks, (1, 0, 2)))


def settle_kernel(*refs):
    for src, dst in zip(refs[:3], refs[3:]):
        dst[...] = src[...]


def settle(arrays):
    vm = pl.BlockSpec(memory_space=pltpu.VMEM)
    return pl.pallas_call(
        settle_kernel,
        out_shape=tuple(jax.ShapeDtypeStruct(a.shape, a.dtype) for a in arrays),
        in_specs=[vm] * 3,
        out_specs=(vm,) * 3,
        name="settle",
    )(*arrays)


def body(orbitals, potential, deriv_blocks, levels, box_counts, neighbours):
    return settle(whole(orbitals, potential, deriv_blocks, levels, box_counts, neighbours))


def solution(mesh):
    in_specs = (
        P("box", None, "orb"),
        P("box", None),
        P(),
        P("box"),
        P("box"),
        P("box", None, None),
    )
    out_specs = (P("box", "orb"), P("box", "orb"), P("box", "orb"))
    return jax.shard_map(body, mesh=mesh, in_specs=in_specs, out_specs=out_specs, check_vma=False)
```

```python
import functools

import jax
import jax.numpy as jnp
from jax import lax
from jax.experimental import pallas as pl
from jax.experimental.pallas import tpu as pltpu
from jax.sharding import PartitionSpec as P

MESH = pl.DeviceIdType.MESH
HIGH = lax.Precision.HIGHEST
F32 = jnp.float32
BF16 = jnp.bfloat16


def quotient(x, n):
    return jnp.floor((x + 0.5) * (1.0 / n))


def rows_and_cols(shape):
    r = lax.broadcasted_iota(jnp.int32, shape, 0).astype(F32)
    c = lax.broadcasted_iota(jnp.int32, shape, 1).astype(F32)
    return r, c


def split_two(x):
    hi = x.astype(BF16)
    return hi, (x - hi.astype(F32)).astype(BF16)


def hdot(a, b):
    return jnp.dot(a, b, precision=HIGH, preferred_element_type=F32)


def whole_kernel(n, pad, zs, ys, a_ref, nb_ref, lev_ref, cnt_ref, pot_ref, db_ref, fock_ref, corr_ref, inv_ref,
                 gath, halo, SA, SB, SC, Wsc, R, m12a, m12b, m12c, m0a, m0b, m0c, tbl, prow, pcol,
                 p_ref, abuf0, X0, B1a, B1b, Ya, Yb, B2a, B2b, abuf, X, B1, Y, B2, cpan, qpan, crow, qrow, pan_hi, pan_lo,
                 xs_sem, xr_sem, hs_sem, hr_sem, ts_sem, tr_sem,
                 sa0, ra0, s1a, r1a, s1b, r1b, s2a, r2a, s2b, r2b, g1a_s, g1a_r, g1b_s, g1b_r, g2a_s, g2a_r,
                 g2b_s, g2b_r, fa_s, fa_r, fb_s, fb_r,
                 sa, ra, s1, r1, s2, r2, sg1, rg1, sg2, rg2, sf, rf, sx, rx):
    b = lax.axis_index("box")
    o = lax.axis_index("orb")
    boxes = lax.axis_size("box")
    groups = lax.axis_size("orb")
    core = lax.rem(b, 2)
    chip = b // 2
    z = chip // ys
    y = lax.rem(chip, ys)
    sgn = 1 - 2 * core
    mate = b + sgn
    back1 = lax.rem(b - sgn + boxes, boxes)
    fwd2 = lax.rem(b + 2 * sgn + boxes, boxes)
    back2 = lax.rem(b - 2 * sgn + boxes, boxes)
    right = lax.rem(o + 1, groups)
    left = lax.rem(o + groups - 1, groups)
    nn = n * n
    w = a_ref.shape[2]
    rows = corr_ref.shape[0]
    half_rows = rows // 2
    total_rows = zs * ys * 2 * rows

    def at(zz, yy):
        return ((zz * ys + yy) * 2 + core, o)

    partner = (mate, o)
    zpeer = [at(lax.rem(z + d, zs), y) for d in range(1, zs)]
    ypeer = [at(z, lax.rem(y + d, ys)) for d in range(1, ys)]
    xpeer = [(b, lax.rem(o + d, groups)) for d in range(1, groups)]

    shape = tbl.shape[1:]
    r = lax.broadcasted_iota(jnp.int32, shape, 0)
    c = lax.broadcasted_iota(jnp.int32, shape, 1)
    own = jnp.zeros(shape, jnp.int32)
    for k in range(2):
        mine = (r >= k * n) & (r < (k + 1) * n)
        for a in range(3):
            own = jnp.where(mine & (c == a * 3), nb_ref[k, 0, a], own)
            own = jnp.where(mine & (c == a * 3 + 1), b * 2 + k, own)
            own = jnp.where(mine & (c == a * 3 + 2), nb_ref[k, 1, a], own)
        code = jnp.where(cnt_ref[0] > k, lev_ref[k], -1)
        own = jnp.where(mine & (c == 9), code, own)
    tbl[0] = own

    barrier = pltpu.get_barrier_semaphore()
    peers = [partner, (back1, o), (fwd2, o), (back2, o)] + xpeer + ypeer + zpeer
    for dev in peers:
        pl.semaphore_signal(barrier, inc=1, device_id=dev, device_id_type=MESH)
    pl.semaphore_wait(barrier, len(peers))

    def remote(src, dst, ssem, rsem, dev):
        return pltpu.make_async_remote_copy(src_ref=src, dst_ref=dst, send_sem=ssem, recv_sem=rsem,
                                            device_id=dev, device_id_type=MESH)

    sends = {}
    for i, (k, q, dev) in enumerate(((0, 0, (b, right)), (1, 1, (b, left)), (1, 0, (b, right)), (0, 1, (b, left)))):
        sends[i] = remote(a_ref.at[k], gath.at[q, k], xs_sem.at[i], xr_sem.at[q, k], dev)
    xf0 = remote(gath.at[0, 0], gath.at[2, 0], xs_sem.at[4], xr_sem.at[2, 0], (b, right))
    xf1 = remote(gath.at[1, 1], gath.at[2, 1], xs_sem.at[5], xr_sem.at[2, 1], (b, left))
    h1 = [remote(a_ref.at[k], halo.at[1, k], hs_sem.at[k], hr_sem.at[1, k], (back1, o)) for k in range(2)]
    h2 = [remote(a_ref.at[k], halo.at[2, k], hs_sem.at[2 + k], hr_sem.at[2, k], (fwd2, o)) for k in range(2)]
    h0 = [remote(a_ref.at[k], halo.at[0, k], hs_sem.at[4 + k], hr_sem.at[0, k], partner) for k in range(2)]
    h3 = [remote(halo.at[1, k], halo.at[3, k], hs_sem.at[6 + k], hr_sem.at[3, k], partner) for k in range(2)]
    t1 = remote(tbl.at[0], tbl.at[1], ts_sem.at[0], tr_sem.at[0], partner)
    t2 = remote(tbl.at[0], tbl.at[2], ts_sem.at[1], tr_sem.at[1], (back1, o))
    sends[0].start()
    sends[1].start()
    t2.start()
    h1[0].start()
    h2[0].start()
    t1.start()
    h0[0].start()
    h0[1].start()
    sends[2].start()
    sends[3].start()
    h1[1].start()
    h2[1].start()

    alive = [jnp.where(cnt_ref[0] > k, 1.0, 0.0) for k in range(2)]
    for k in range(2):
        R[k, :, 0:w] = (a_ref[k].astype(F32) * alive[k]).astype(BF16)

    def correlate(block, place):
        total = jnp.zeros((w, w), F32)
        for k in range(2):
            total = total + lax.dot_general(block[k], R[k, :, 0:w], (((0,), (0,)), ((), ())),
                                            preferred_element_type=F32)
        p_ref[0, place] = total.reshape(ys, 2, rows, w)

    def fock_part(block, place):
        total = jnp.zeros((w, 2 * w), F32)
        for k in range(2):
            total = total + lax.dot_general(block[k], R[k, :, w:3 * w], (((0,), (0,)), ((), ())),
                                            preferred_element_type=F32)
        p_ref[1, place] = (total[:, 0:w] + total[:, w:2 * w]).reshape(ys, 2, rows, w)

    edge = nn // 16 * 16
    for S in (SA, SB, SC):
        S[:, :, edge:pad, :] = jnp.zeros((n, S.shape[1], pad - edge, w), BF16)

    def spread(block, S, q):
        for l in range(n):
            S[l, q, 0:nn, :] = block[l * nn:(l + 1) * nn, :]

    spread(a_ref.at[0], SA, 0)
    spread(a_ref.at[1], SA, 1)
    started = []

    def send(src, dst, ssem, rsem, dev):
        copy = pltpu.make_async_remote_copy(src_ref=src, dst_ref=dst, send_sem=ssem, recv_sem=rsem,
                                            device_id=dev, device_id_type=MESH)
        copy.start()
        started.append(copy)
        return copy

    part = [pl.ds(0, half_rows), pl.ds(half_rows, half_rows)]

    order_z = [o, left, right, lax.rem(o + 2, groups)]
    last = order_z[3]
    low, high = part
    pairs = {}
    one_a = {}
    two_a = {}

    def ahead(i):
        return lax.rem(order_z[i] - z + zs, zs)

    def behind(i):
        return lax.rem(z - order_z[i] + zs, zs)

    def pair_send(i):
        zp = order_z[i]
        pairs[i] = send(p_ref.at[0, zp, :, 1 - core], abuf0.at[zp], sa0.at[i], ra0.at[i], partner)

    def pair_add(i):
        zp = order_z[i]
        pairs[i].wait_recv()
        X0[zp] = p_ref[0, zp, :, core] + abuf0[zp]

    def c_one(i):
        zp = order_z[i]
        for d in range(1, ys):
            one_a[i, d] = send(X0.at[zp, lax.rem(y + d, ys), low], B1a.at[i, d - 1], s1a.at[i, d - 1],
                               r1a.at[i, d - 1], ypeer[d - 1])
        e = ahead(i)

        @pl.when(e > 0)
        def _():
            remote(X0.at[zp, :, high], B1b.at[e - 1], s1b.at[e - 1], r1b.at[e - 1], at(zp, y)).start()

    def c_two_a(i):
        zp = order_z[i]
        acc = X0[zp, y, low]
        for d in range(1, ys):
            one_a[i, d].wait_recv()
            acc = acc + B1a[i, d - 1]
        Ya[zp] = acc
        e = ahead(i)

        @pl.when(e > 0)
        def _():
            remote(Ya.at[zp], B2a.at[e - 1], s2a.at[e - 1], r2a.at[e - 1], at(zp, y)).start()

    def c_two_b():
        for e in range(1, zs):
            remote(B1b.at[e - 1], B1b.at[e - 1], s1b.at[e - 1], r1b.at[e - 1], partner).wait_recv()
        acc = X0[z, :, high]
        for e in range(1, zs):
            acc = acc + B1b[e - 1]
        Yb[...] = acc
        for d in range(1, ys):
            remote(Yb.at[lax.rem(y + d, ys)], B2b.at[d - 1], s2b.at[d - 1], r2b.at[d - 1], ypeer[d - 1]).start()

    def c_end():
        piece = Ya[z]
        for e in range(1, zs):
            remote(B2a.at[e - 1], B2a.at[e - 1], s2a.at[e - 1], r2a.at[e - 1], partner).wait_recv()
            piece = piece + B2a[e - 1]
        corr_ref[low, :] = piece
        cpan[z, y, core, low] = piece
        crow[o, low] = piece
        for e in range(1, zs):
            spot = cpan.at[z, y, core, low]
            remote(spot, spot, g1a_s.at[e - 1], g1a_r.at[e - 1], zpeer[e - 1]).start()
        piece = Yb[y]
        for d in range(1, ys):
            remote(B2b.at[d - 1], B2b.at[d - 1], s2b.at[d - 1], r2b.at[d - 1], partner).wait_recv()
            piece = piece + B2b[d - 1]
        corr_ref[high, :] = piece
        cpan[z, y, core, high] = piece
        crow[o, high] = piece
        for d in range(1, ys):
            spot = cpan.at[z, y, core, high]
            remote(spot, spot, g1b_s.at[d - 1], g1b_r.at[d - 1], ypeer[d - 1]).start()
        for d in range(1, groups):
            remote(cpan.at[z, y, core], crow.at[o], sx.at[0, d - 1], rx.at[0, d - 1], xpeer[d - 1]).start()

    def g_two_a(i):
        zp = order_z[i]
        spot = cpan.at[zp, y, core, low]
        e = behind(i)

        @pl.when(e > 0)
        def _():
            remote(spot, spot, g1a_s.at[e - 1], g1a_r.at[e - 1], partner).wait_recv()

        for d in range(1, ys):
            two_a[i, d] = send(spot, spot, g2a_s.at[i, d - 1], g2a_r.at[i, d - 1], ypeer[d - 1])

    def g_end_a(i):
        for d in range(1, ys):
            two_a[i, d].wait_recv()
        column = cpan.at[order_z[i], :, core, low]
        return send(column, column, fa_s.at[i], fa_r.at[i], partner)

    def g_two_b():
        for d in range(1, ys):
            spot = cpan.at[z, y, core, high]
            remote(spot, spot, g1b_s.at[d - 1], g1b_r.at[d - 1], partner).wait_recv()
        column = cpan.at[z, :, core, high]
        for e in range(1, zs):
            remote(column, column, g2b_s.at[e - 1], g2b_r.at[e - 1], zpeer[e - 1]).start()
        remote(column, column, fb_s.at[0], fb_r.at[0], partner).start()

    def g_end_b(i):
        e = behind(i)
        column = cpan.at[order_z[i], :, core, high]

        @pl.when(e > 0)
        def _():
            remote(column, column, g2b_s.at[e - 1], g2b_r.at[e - 1], partner).wait_recv()
            remote(column, column, fb_s.at[e], fb_r.at[e], partner).start()

    correlate(a_ref, o)
    pair_send(0)

    prow[...] = jnp.zeros(prow.shape, F32)
    prow[0:2, 0:n * nn] = pot_ref[...]
    pcol[...] = prow[...].T

    order = [(b, 0), (b, 1), (mate, 0), (mate, 1), (back1, 0), (back2, 0), (fwd2, 0), (back1, 1), (back2, 1),
             (fwd2, 1)]
    shape = (2 * n, 10 * n)
    ci = lax.broadcasted_iota(jnp.int32, shape, 1)
    gid = jnp.zeros(shape, jnp.int32)
    for q, (dev, k) in enumerate(order):
        gid = jnp.where((ci >= q * n) & (ci < (q + 1) * n), dev * 2 + k, gid)
    r, c = rows_and_cols((2 * n, n))
    pick_r = jnp.where(r - n * quotient(r, n) == c, 1.0, 0.0)
    r, c = rows_and_cols((n, 10 * n))
    pick_c = jnp.where(c - n * quotient(c, n) == r, 1.0, 0.0)
    bt = [hdot(hdot(pick_r, db_ref[:, u, :].astype(F32)), pick_c) for u in range(3)]
    t1.wait_recv()
    t2.wait_recv()
    M = [jnp.zeros(shape, F32) for _ in range(3)]
    for d in range(3):
        code = tbl[d, 0:2 * n, 9:10]
        factor = jnp.where(code < 0, 0.0, jnp.where(code == 0, 0.5, jnp.where(code == 1, 1.0, 2.0)))
        for a in range(3):
            t = jnp.zeros(shape, F32)
            for u in range(3):
                t = t + jnp.where(tbl[d, 0:2 * n, a * 3 + u:a * 3 + u + 1] == gid, bt[u], 0.0)
            t = t * factor
            M[a] = M[a] + 0.5 * lax.dot_general(t[:, 0:2 * n], t, (((0,), (0,)), ((), ())), precision=HIGH,
                                                preferred_element_type=F32)
    half = 2 * pad
    r, c = rows_and_cols((half, 2 * n))
    rs = quotient(r, pad)
    rq = r - rs * pad
    ri1 = quotient(rq, n)
    ri2 = rq - ri1 * n
    ok = rq < nn
    cs = quotient(c, n)
    ci = c - cs * n
    L1 = jnp.where(ok & (cs == rs) & (ci == ri1), 1.0, 0.0)
    L2 = jnp.where(ok & (cs == rs) & (ci == ri2), 1.0, 0.0)
    LM1 = hdot(L1, M[1])
    LM2 = hdot(L2, M[2])
    r, c = rows_and_cols((n * 32, 2 * n))
    ri = quotient(r, 32)
    rs = quotient(r, 16) - 2 * ri
    cs = quotient(c, n)
    L0 = jnp.where((cs == rs) & ((c - cs * n) == ri), 1.0, 0.0)
    LM0 = hdot(L0, M[0])

    def expand(m12, m0, base, count):
        wide = count * pad
        r, c = rows_and_cols((10 * n, wide))
        cs = quotient(c, pad)
        cq = c - cs * pad
        cl1 = quotient(cq, n)
        cl2 = cq - cl1 * n
        ok = cq < nn
        rs = quotient(r, n)
        ri = r - rs * n
        ok = ok & (cs + base == rs)
        C1 = jnp.where(ok & (ri == cl1), 1.0, 0.0)
        C2 = jnp.where(ok & (ri == cl2), 1.0, 0.0)
        r, c = rows_and_cols((half, wide))
        rq = r - quotient(r, pad) * pad
        cq = c - quotient(c, pad) * pad
        ri1 = quotient(rq, n)
        cl1 = quotient(cq, n)
        same1 = ri1 == cl1
        same2 = (rq - ri1 * n) == (cq - cl1 * n)
        full = jnp.where(same2, hdot(LM1, C1), 0.0) + jnp.where(same1, hdot(LM2, C2), 0.0)
        hi, lo = split_two(full)
        m12[0:half, :] = hi
        m12[half:2 * half, :] = lo
        step = count * 16
        r, c = rows_and_cols((10 * n, n * step))
        cl = quotient(c, step)
        cs = quotient(c - cl * step, 16)
        rs = quotient(r, n)
        C0 = jnp.where((rs == cs + base) & ((r - rs * n) == cl), 1.0, 0.0)
        r, c = rows_and_cols((n * 32, n * step))
        same = (r - 16 * quotient(r, 16)) == (c - 16 * quotient(c, 16))
        full = jnp.where(same, hdot(LM0, C0), 0.0)
        hi, lo = split_two(full)
        m0[0:n * 32, :] = hi
        m0[n * 32:n * 64, :] = lo

    def apply_inner(S, m12, fresh):
        count = S.shape[1]

        @pl.loop(0, n)
        def _(i):
            got = jnp.dot(m12[...], S[i].reshape(count * pad, w), preferred_element_type=F32)
            got = (got[0:half] + got[half:2 * half]).reshape(2, pad, w)
            Wsc[i] = got if fresh else Wsc[i] + got

    def apply_outer(S, m0):
        count = S.shape[1]

        @pl.loop(0, pad // 16)
        def _(i):
            rows = pl.ds(pl.multiple_of(i * 16, 16), 16)
            got = jnp.dot(m0[...], S[:, :, rows, :].reshape(n * count * 16, w), preferred_element_type=F32)
            Wsc[:, :, rows, :] = Wsc[:, :, rows, :] + (got[0:n * 32] + got[n * 32:n * 64]).reshape(n, 2, 16, w)

    expand(m12a, m0a, 0, 4)
    for k in range(2):
        h0[k].wait_recv()
        spread(halo.at[0, k], SA, 2 + k)
    apply_inner(SA, m12a, True)
    apply_outer(SA, m0a)
    expand(m12b, m0b, 4, 3)
    expand(m12c, m0c, 7, 3)

    sends[0].wait_recv()
    xf0.start()
    sends[1].wait_recv()
    xf1.start()
    h1[0].wait_recv()
    h3[0].start()
    spread(halo.at[1, 0], SB, 0)
    h2[0].wait_recv()
    spread(halo.at[2, 0], SB, 1)
    h3[0].wait_recv()
    spread(halo.at[3, 0], SB, 2)
    apply_inner(SB, m12b, False)
    apply_outer(SB, m0b)

    h1[1].wait_recv()
    h3[1].start()
    sends[2].wait_recv()
    correlate(gath.at[0], left)
    pair_send(1)
    sends[3].wait_recv()
    correlate(gath.at[1], right)
    pair_send(2)
    spread(halo.at[1, 1], SC, 0)
    h2[1].wait_recv()
    spread(halo.at[2, 1], SC, 1)
    h3[1].wait_recv()
    spread(halo.at[3, 1], SC, 2)
    apply_inner(SC, m12c, False)
    for i in range(3):
        pair_add(i)
        c_one(i)
    apply_outer(SC, m0c)

    for k in range(2):
        for l in range(n):
            full = Wsc[l, k] + (pcol[l * nn:l * nn + pad, k:k + 1] * alive[k]) * SA[l, k].astype(F32)
            hi, lo = split_two(full)
            R[k, l * nn:(l + 1) * nn, w:2 * w] = hi[0:nn]
            R[k, l * nn:(l + 1) * nn, 2 * w:3 * w] = lo[0:nn]

    fock_part(a_ref, o)
    fock_part(gath.at[0], left)
    for i in range(3):
        c_two_a(i)
    pl.when(z != last)(c_two_b)
    fock_part(gath.at[1], right)
    pl.when(z != last)(c_end)
    xf0.wait_recv()
    xf1.wait_recv()
    correlate(gath.at[2], last)
    pair_send(3)
    fock_part(gath.at[2], last)

    first = {}

    for h in range(2):
        first[0, h] = send(p_ref.at[1, :, :, 1 - core, part[h]], abuf.at[0, h], sa.at[0, h], ra.at[0, h], partner)
    pair_add(3)
    c_one(3)
    for i in range(3):
        g_two_a(i)
    pl.when(z != last)(g_two_b)
    c_two_a(3)
    pl.when(z == last)(c_two_b)

    def add_pair(f, h):
        first[f, h].wait_recv()
        X[f, h] = p_ref[1, :, :, core, part[h]] + abuf[f, h]

    def scatter_one(f, h):
        out = []
        for d in range(1, ys if h == 0 else zs):
            if h == 0:
                t = lax.rem(y + d, ys)
                src = X.at[f, h, :, t]
            else:
                t = lax.rem(z + d, zs)
                src = X.at[f, h, t]
            out.append(send(src, B1.at[f, h, d - 1], s1.at[f, h, d - 1], r1.at[f, h, d - 1],
                            (ypeer if h == 0 else zpeer)[d - 1]))
        return out

    def scatter_two(f, h, copies):
        for copy in copies:
            copy.wait_recv()
        acc = X[f, h, :, y] if h == 0 else X[f, h, z]
        for d in range(1, ys if h == 0 else zs):
            acc = acc + B1[f, h, d - 1]
        Y[f, h] = acc
        out = []
        for d in range(1, zs if h == 0 else ys):
            t = lax.rem(z + d, zs) if h == 0 else lax.rem(y + d, ys)
            out.append(send(Y.at[f, h, t], B2.at[f, h, d - 1], s2.at[f, h, d - 1], r2.at[f, h, d - 1],
                            (zpeer if h == 0 else ypeer)[d - 1]))
        return out

    def scatter_end(f, h, copies):
        for copy in copies:
            copy.wait_recv()
        acc = Y[f, h, z] if h == 0 else Y[f, h, y]
        for d in range(1, zs if h == 0 else ys):
            acc = acc + B2[f, h, d - 1]
        return acc

    def gather_one(g, pan, h):
        out = []
        for d in range(1, zs if h == 0 else ys):
            out.append(send(pan.at[z, y, core, part[h]], pan.at[z, y, core, part[h]],
                            sg1.at[g, h, d - 1], rg1.at[g, h, d - 1], (zpeer if h == 0 else ypeer)[d - 1]))
        return out

    def line(pan, h, k):
        return pan.at[:, k, core, part[h]] if h == 0 else pan.at[k, :, core, part[h]]

    def gather_two(g, pan, h, copies):
        for copy in copies:
            copy.wait_recv()
        mine = line(pan, h, y if h == 0 else z)
        out = []
        for d in range(1, ys if h == 0 else zs):
            out.append(send(mine, mine, sg2.at[g, h, d - 1], rg2.at[g, h, d - 1],
                            (ypeer if h == 0 else zpeer)[d - 1]))
        fwd = send(mine, mine, sf.at[g, h, 0], rf.at[g, h, 0], partner)
        return out, fwd

    def gather_end(g, pan, h, copies, fwd):
        out = [fwd]
        n_line = ys if h == 0 else zs
        for d, copy in enumerate(copies, 1):
            copy.wait_recv()
            k = lax.rem((y if h == 0 else z) - d + n_line, n_line)
            piece = line(pan, h, k)
            out.append(send(piece, piece, sf.at[g, h, d], rf.at[g, h, d], partner))
        return out

    def row_gather(g, row, src):
        out = []
        for d in range(1, groups):
            out.append(send(src, row.at[o], sx.at[g, d - 1], rx.at[g, d - 1], xpeer[d - 1]))
        return out

    for h in range(2):
        add_pair(0, h)
    pl.when(z == last)(c_end)
    forwards = []
    for i in range(3):
        forwards.append(g_end_a(i))
        g_end_b(i)
    g_two_a(3)
    pl.when(z == last)(g_two_b)
    one = {}
    two = {}
    got = {}
    for h in range(2):
        one[0, h] = scatter_one(0, h)
    forwards.append(g_end_a(3))
    g_end_b(3)

    def product(left, panel):
        lhi, llo = split_two(left)
        for k in range(zs):
            hi, lo = split_two(panel(k))
            span = pl.ds(k * (total_rows // zs), total_rows // zs)
            pan_hi[span, :] = hi
            pan_lo[span, :] = lo
        big = jnp.dot(jnp.concatenate([lhi, llo], axis=0), pan_hi[...], preferred_element_type=F32)
        return big[0:rows] + big[rows:2 * rows] + jnp.dot(lhi, pan_lo[...], preferred_element_type=F32)

    def flat(pan, k):
        return pan[k].reshape(total_rows // zs, w)

    for d in range(1, groups):
        remote(crow.at[0], crow.at[0], sx.at[0, d - 1], rx.at[0, d - 1], partner).wait_recv()
    for copy in forwards:
        copy.wait_recv()
    for e in range(zs):
        column = cpan.at[0, :, core, high]
        remote(column, column, fb_s.at[e], fb_r.at[e], partner).wait_recv()
    row_c = jnp.concatenate([crow[k] for k in range(groups)], axis=1)
    q = product(row_c, lambda k: flat(cpan, k))
    qpan[z, y, core] = q
    qrow[o] = q
    for h in range(2):
        got[h] = gather_one(0, qpan, h)
    rows_q = row_gather(1, qrow, qpan.at[z, y, core])
    for h in range(2):
        got[h] = gather_two(0, qpan, h, got[h])
    for h in range(2):
        two[0, h] = scatter_two(0, h, one[0, h])
    got = {h: gather_end(0, qpan, h, *got[h]) for h in range(2)}
    for h in range(2):
        fock_ref[part[h], :] = scatter_end(0, h, two[0, h])
    for copy in rows_q:
        copy.wait_recv()
    for h in range(2):
        for copy in got[h]:
            copy.wait_recv()
    left = jnp.concatenate([1.5 * crow[k] - 0.5 * qrow[k] for k in range(groups)], axis=1)

    def diagonal(count, start):
        r = lax.broadcasted_iota(jnp.int32, (count, w), 0) + start
        c = lax.broadcasted_iota(jnp.int32, (count, w), 1) + o * w
        return r == c

    def panel(k):
        step = total_rows // zs
        square = 0.25 * flat(qpan, k) - 1.5 * flat(cpan, k)
        return square + jnp.where(diagonal(step, k * step), 2.25, 0.0)

    right = product(left, panel)
    turn = jnp.where(diagonal(rows, b * rows), 1.5, 0.0) - 0.5 * corr_ref[...]
    inv_ref[...] = 1.5 * turn - 0.5 * right
    for e in range(1, zs):
        for ref, sem in ((B1b.at[e - 1], s1b), (B2a.at[e - 1], s2a), (cpan.at[0, y, core, low], g1a_s),
                         (cpan.at[0, :, core, high], g2b_s)):
            remote(ref, ref, sem.at[e - 1], r1b.at[e - 1], partner).wait_send()
    for d in range(1, ys):
        for ref, sem in ((B2b.at[d - 1], s2b), (cpan.at[0, y, core, high], g1b_s)):
            remote(ref, ref, sem.at[d - 1], r2b.at[d - 1], partner).wait_send()
    for e in range(zs):
        column = cpan.at[0, :, core, high]
        remote(column, column, fb_s.at[e], fb_r.at[e], partner).wait_send()
    for d in range(1, groups):
        remote(crow.at[0], crow.at[0], sx.at[0, d - 1], rx.at[0, d - 1], partner).wait_send()
    for copy in started:
        copy.wait_send()
    for i in range(4):
        sends[i].wait_send()
    xf0.wait_send()
    xf1.wait_send()
    t1.wait_send()
    t2.wait_send()
    for k in range(2):
        h0[k].wait_send()
        h1[k].wait_send()
        h2[k].wait_send()
        h3[k].wait_send()


def whole(orbitals, potential, deriv_blocks, levels, box_counts, neighbours):
    slots, coefs, w = orbitals.shape
    n = deriv_blocks.shape[1]
    nn = n * n
    pad = -(-nn // 16) * 16
    boxes = lax.axis_size("box")
    groups = lax.axis_size("orb")
    zs = groups
    ys = boxes // 2 // zs
    fy = max(ys - 1, 1)
    total = groups * w
    rows = total // boxes
    half = rows // 2
    far = max(zs, ys) - 1
    vm = pl.BlockSpec(memory_space=pltpu.VMEM)
    sm = pl.BlockSpec(memory_space=pltpu.SMEM)
    column = -(-((n - 1) * nn + pad) // 128) * 128
    dma = pltpu.SemaphoreType.DMA
    out = jax.ShapeDtypeStruct((rows, w), F32)
    return pl.pallas_call(
        functools.partial(whole_kernel, n, pad, zs, ys),
        out_shape=(out, out, out),
        in_specs=[vm, sm, sm, sm, vm, vm],
        out_specs=(vm, vm, vm),
        scratch_shapes=[
            pltpu.VMEM((3, slots, coefs, w), BF16),
            pltpu.VMEM((4, slots, coefs, w), BF16),
            pltpu.VMEM((n, 4, pad, w), BF16),
            pltpu.VMEM((n, 3, pad, w), BF16),
            pltpu.VMEM((n, 3, pad, w), BF16),
            pltpu.VMEM((n, 2, pad, w), F32),
            pltpu.VMEM((slots, coefs, 3 * w), BF16),
            pltpu.VMEM((4 * pad, 4 * pad), BF16),
            pltpu.VMEM((4 * pad, 3 * pad), BF16),
            pltpu.VMEM((4 * pad, 3 * pad), BF16),
            pltpu.VMEM((n * 64, n * 64), BF16),
            pltpu.VMEM((n * 64, n * 48), BF16),
            pltpu.VMEM((n * 64, n * 48), BF16),
            pltpu.VMEM((3, -(-slots * n // 8) * 8, 128), jnp.int32),
            pltpu.VMEM((8, column), F32),
            pltpu.VMEM((column, 8), F32),
            pltpu.VMEM((2, groups, total // groups // (2 * rows), 2, rows, w), F32),
            pltpu.VMEM((zs, ys, rows, w), F32),
            pltpu.VMEM((zs, ys, rows, w), F32),
            pltpu.VMEM((zs, fy, half, w), F32),
            pltpu.VMEM((zs - 1, ys, half, w), F32),
            pltpu.VMEM((zs, half, w), F32),
            pltpu.VMEM((ys, half, w), F32),
            pltpu.VMEM((zs - 1, half, w), F32),
            pltpu.VMEM((fy, half, w), F32),
            pltpu.VMEM((1, 2, zs, ys, half, w), F32),
            pltpu.VMEM((1, 2, zs, ys, half, w), F32),
            pltpu.VMEM((1, 2, far, zs, half, w), F32),
            pltpu.VMEM((1, 2, zs, half, w), F32),
            pltpu.VMEM((1, 2, far, half, w), F32),
            pltpu.VMEM((zs, ys, 2, rows, w), F32),
            pltpu.VMEM((zs, ys, 2, rows, w), F32),
            pltpu.VMEM((groups, rows, w), F32),
            pltpu.VMEM((groups, rows, w), F32),
            pltpu.VMEM((total, w), BF16),
            pltpu.VMEM((total, w), BF16),
            dma((6,)), dma((3, 2)), dma((8,)), dma((4, 2)), dma((2,)), dma((2,)),
            dma((zs,)), dma((zs,)),
            dma((zs, fy)), dma((zs, fy)), dma((zs - 1,)), dma((zs - 1,)),
            dma((zs - 1,)), dma((zs - 1,)), dma((fy,)), dma((fy,)),
            dma((zs - 1,)), dma((zs - 1,)), dma((fy,)), dma((fy,)),
            dma((zs, fy)), dma((zs, fy)), dma((zs - 1,)), dma((zs - 1,)),
            dma((zs,)), dma((zs,)), dma((zs,)), dma((zs,)),
            dma((1, 2)), dma((1, 2)),
            dma((1, 2, far)), dma((1, 2, far)),
            dma((1, 2, far)), dma((1, 2, far)),
            dma((1, 2, far)), dma((1, 2, far)),
            dma((1, 2, far)), dma((1, 2, far)),
            dma((1, 2, far + 1)), dma((1, 2, far + 1)),
            dma((2, groups - 1)), dma((2, groups - 1)),
        ],
        compiler_params=pltpu.CompilerParams(collective_id=0, has_side_effects=True, vmem_limit_bytes=63 << 20),
        name="whole",
    )(orbitals, jnp.transpose(neighbours, (0, 2, 1)), levels, box_counts, potential,
      jnp.transpose(deriv_blocks, (1, 0, 2)))


def settle_kernel(*refs):
    for src, dst in zip(refs[:3], refs[3:]):
        dst[...] = src[...]


def settle(arrays):
    vm = pl.BlockSpec(memory_space=pltpu.VMEM)
    return pl.pallas_call(
        settle_kernel,
        out_shape=tuple(jax.ShapeDtypeStruct(a.shape, a.dtype) for a in arrays),
        in_specs=[vm] * 3,
        out_specs=(vm,) * 3,
        name="settle",
    )(*arrays)


def body(orbitals, potential, deriv_blocks, levels, box_counts, neighbours):
    return settle(whole(orbitals, potential, deriv_blocks, levels, box_counts, neighbours))


def solution(mesh):
    in_specs = (
        P("box", None, "orb"),
        P("box", None),
        P(),
        P("box"),
        P("box"),
        P("box", None, None),
    )
    out_specs = (P("box", "orb"), P("box", "orb"), P("box", "orb"))
    return jax.shard_map(body, mesh=mesh, in_specs=in_specs, out_specs=out_specs, check_vma=False)
```

```python
import functools

import jax
import jax.numpy as jnp
from jax import lax
from jax.experimental import pallas as pl
from jax.experimental.pallas import tpu as pltpu
from jax.sharding import PartitionSpec as P

MESH = pl.DeviceIdType.MESH
HIGH = lax.Precision.HIGHEST
F32 = jnp.float32
BF16 = jnp.bfloat16


def quotient(x, n):
    return jnp.floor((x + 0.5) * (1.0 / n))


def rows_and_cols(shape):
    r = lax.broadcasted_iota(jnp.int32, shape, 0).astype(F32)
    c = lax.broadcasted_iota(jnp.int32, shape, 1).astype(F32)
    return r, c


def split_two(x):
    hi = x.astype(BF16)
    return hi, (x - hi.astype(F32)).astype(BF16)


def hdot(a, b):
    return jnp.dot(a, b, precision=HIGH, preferred_element_type=F32)


def whole_kernel(n, pad, zs, ys, a_hbm, nb_ref, lev_ref, cnt_ref, pot_ref, db_ref, fock_ref, corr_ref, inv_ref,
                 a_ref, in_sem, gath, halo, SA, SB, SC, Wsc, R, m12a, m12b, m12c, m0a, m0b, m0c, tbl, prow, pcol,
                 p_ref, abuf0, X0, B1a, B1b, Ya, Yb, B2a, B2b, BL1, YL, BL2, abuf, X, B1, Y, B2,
                 cpan, crow, urow, pan_hi, pan_lo,
                 xs_sem, xr_sem, hs_sem, hr_sem, ts_sem, tr_sem,
                 sa0, ra0, s1a, r1a, s1b, r1b, s2a, r2a, s2b, r2b, g1a_s, g1a_r, g1b_s, g1b_r, g2a_s, g2a_r,
                 g2b_s, g2b_r, fa_s, fa_r, fb_s, fb_r, sl1, rl1, sl2, rl2, gl_s, gl_r, gm_s, gm_r, gf_s, gf_r,
                 sa, ra, s1, r1, s2, r2, sx, rx):
    b = lax.axis_index("box")
    o = lax.axis_index("orb")
    boxes = lax.axis_size("box")
    groups = lax.axis_size("orb")
    core = lax.rem(b, 2)
    chip = b // 2
    z = chip // ys
    y = lax.rem(chip, ys)
    sgn = 1 - 2 * core
    mate = b + sgn
    back1 = lax.rem(b - sgn + boxes, boxes)
    fwd2 = lax.rem(b + 2 * sgn + boxes, boxes)
    back2 = lax.rem(b - 2 * sgn + boxes, boxes)
    right = lax.rem(o + 1, groups)
    left = lax.rem(o + groups - 1, groups)
    nn = n * n
    w = a_ref.shape[2]
    rows = corr_ref.shape[0]
    half_rows = rows // 2
    total_rows = zs * ys * 2 * rows

    def at(zz, yy):
        return ((zz * ys + yy) * 2 + core, o)

    partner = (mate, o)
    zpeer = [at(lax.rem(z + d, zs), y) for d in range(1, zs)]
    ypeer = [at(z, lax.rem(y + d, ys)) for d in range(1, ys)]
    xpeer = [(b, lax.rem(o + d, groups)) for d in range(1, groups)]

    fetch = pltpu.make_async_copy(a_hbm, a_ref, in_sem)
    fetch.start()

    shape = tbl.shape[1:]
    r = lax.broadcasted_iota(jnp.int32, shape, 0)
    c = lax.broadcasted_iota(jnp.int32, shape, 1)
    own = jnp.zeros(shape, jnp.int32)
    for k in range(2):
        mine = (r >= k * n) & (r < (k + 1) * n)
        for a in range(3):
            own = jnp.where(mine & (c == a * 3), nb_ref[k, 0, a], own)
            own = jnp.where(mine & (c == a * 3 + 1), b * 2 + k, own)
            own = jnp.where(mine & (c == a * 3 + 2), nb_ref[k, 1, a], own)
        code = jnp.where(cnt_ref[0] > k, lev_ref[k], -1)
        own = jnp.where(mine & (c == 9), code, own)
    tbl[0] = own

    barrier = pltpu.get_barrier_semaphore()
    peers = [partner, (back1, o), (fwd2, o), (back2, o)] + xpeer + ypeer + zpeer
    for dev in peers:
        pl.semaphore_signal(barrier, inc=1, device_id=dev, device_id_type=MESH)
    pl.semaphore_wait(barrier, len(peers))

    def remote(src, dst, ssem, rsem, dev):
        return pltpu.make_async_remote_copy(src_ref=src, dst_ref=dst, send_sem=ssem, recv_sem=rsem,
                                            device_id=dev, device_id_type=MESH)

    sends = {}
    for i, (k, q, dev) in enumerate(((0, 0, (b, right)), (1, 1, (b, left)), (1, 0, (b, right)), (0, 1, (b, left)))):
        sends[i] = remote(a_hbm.at[k], gath.at[q, k], xs_sem.at[i], xr_sem.at[q, k], dev)
    xf0 = remote(gath.at[0, 0], gath.at[2, 0], xs_sem.at[4], xr_sem.at[2, 0], (b, right))
    xf1 = remote(gath.at[1, 1], gath.at[2, 1], xs_sem.at[5], xr_sem.at[2, 1], (b, left))
    h1 = [remote(a_hbm.at[k], halo.at[1, k], hs_sem.at[k], hr_sem.at[1, k], (back1, o)) for k in range(2)]
    h2 = [remote(a_hbm.at[k], halo.at[2, k], hs_sem.at[2 + k], hr_sem.at[2, k], (fwd2, o)) for k in range(2)]
    h0 = [remote(a_hbm.at[k], halo.at[0, k], hs_sem.at[4 + k], hr_sem.at[0, k], partner) for k in range(2)]
    h3 = [remote(halo.at[1, k], halo.at[3, k], hs_sem.at[6 + k], hr_sem.at[3, k], partner) for k in range(2)]
    t1 = remote(tbl.at[0], tbl.at[1], ts_sem.at[0], tr_sem.at[0], partner)
    t2 = remote(tbl.at[0], tbl.at[2], ts_sem.at[1], tr_sem.at[1], (back1, o))
    sends[0].start()
    sends[1].start()
    t2.start()
    h1[0].start()
    h2[0].start()
    t1.start()
    h0[0].start()
    h0[1].start()
    sends[2].start()
    sends[3].start()
    h1[1].start()
    h2[1].start()

    fetch.wait()

    alive = [jnp.where(cnt_ref[0] > k, 1.0, 0.0) for k in range(2)]
    for k in range(2):
        R[k, :, 0:w] = (a_ref[k].astype(F32) * alive[k]).astype(BF16)

    def correlate(block, place):
        total = jnp.zeros((w, w), F32)
        for k in range(2):
            total = total + lax.dot_general(block[k], R[k, :, 0:w], (((0,), (0,)), ((), ())),
                                            preferred_element_type=F32)
        p_ref[0, place] = total.reshape(ys, 2, rows, w)

    def fock_part(block, place):
        total = jnp.zeros((w, 2 * w), F32)
        for k in range(2):
            total = total + lax.dot_general(block[k], R[k, :, w:3 * w], (((0,), (0,)), ((), ())),
                                            preferred_element_type=F32)
        p_ref[1, place] = (total[:, 0:w] + total[:, w:2 * w]).reshape(ys, 2, rows, w)

    edge = nn // 16 * 16
    for S in (SA, SB, SC):
        S[:, :, edge:pad, :] = jnp.zeros((n, S.shape[1], pad - edge, w), BF16)

    def spread(block, S, q):
        for l in range(n):
            S[l, q, 0:nn, :] = block[l * nn:(l + 1) * nn, :]

    spread(a_ref.at[0], SA, 0)
    spread(a_ref.at[1], SA, 1)
    started = []

    def send(src, dst, ssem, rsem, dev):
        copy = pltpu.make_async_remote_copy(src_ref=src, dst_ref=dst, send_sem=ssem, recv_sem=rsem,
                                            device_id=dev, device_id_type=MESH)
        copy.start()
        started.append(copy)
        return copy

    part = [pl.ds(0, half_rows), pl.ds(half_rows, half_rows)]

    order_z = [o, left, right, lax.rem(o + 2, groups)]
    last = order_z[3]
    low, high = part
    pairs = {}
    one_a = {}
    two_a = {}

    def ahead(i):
        return lax.rem(order_z[i] - z + zs, zs)

    def behind(i):
        return lax.rem(z - order_z[i] + zs, zs)

    def pair_send(i):
        zp = order_z[i]
        pairs[i] = send(p_ref.at[0, zp, :, 1 - core], abuf0.at[zp], sa0.at[i], ra0.at[i], partner)

    def pair_add(i):
        zp = order_z[i]
        pairs[i].wait_recv()
        X0[zp] = p_ref[0, zp, :, core] + abuf0[zp]

    def c_one(i):
        zp = order_z[i]
        for d in range(1, ys):
            one_a[i, d] = send(X0.at[zp, lax.rem(y + d, ys), low], B1a.at[i, d - 1], s1a.at[i, d - 1],
                               r1a.at[i, d - 1], ypeer[d - 1])
        e = ahead(i)

        @pl.when(e > 0)
        def _():
            remote(X0.at[zp, :, high], B1b.at[e - 1], s1b.at[e - 1], r1b.at[e - 1], at(zp, y)).start()

    def c_two_a(i):
        zp = order_z[i]
        acc = X0[zp, y, low]
        for d in range(1, ys):
            one_a[i, d].wait_recv()
            acc = acc + B1a[i, d - 1]
        Ya[zp] = acc
        e = ahead(i)

        @pl.when(e > 0)
        def _():
            remote(Ya.at[zp], B2a.at[e - 1], s2a.at[e - 1], r2a.at[e - 1], at(zp, y)).start()

    def c_two_b():
        for e in range(1, zs):
            remote(B1b.at[e - 1], B1b.at[e - 1], s1b.at[e - 1], r1b.at[e - 1], partner).wait_recv()
        acc = X0[z, :, high]
        for e in range(1, zs):
            acc = acc + B1b[e - 1]
        Yb[...] = acc
        for d in range(1, ys):
            remote(Yb.at[lax.rem(y + d, ys)], B2b.at[d - 1], s2b.at[d - 1], r2b.at[d - 1], ypeer[d - 1]).start()

    def c_end():
        piece = Ya[z]
        for e in range(1, zs):
            remote(B2a.at[e - 1], B2a.at[e - 1], s2a.at[e - 1], r2a.at[e - 1], partner).wait_recv()
            piece = piece + B2a[e - 1]
        corr_ref[low, :] = piece
        cpan[z, y, core, low] = piece
        crow[o, low] = piece
        for e in range(1, zs):
            spot = cpan.at[z, y, core, low]
            remote(spot, spot, g1a_s.at[e - 1], g1a_r.at[e - 1], zpeer[e - 1]).start()
        piece = Yb[y]
        for d in range(1, ys):
            remote(B2b.at[d - 1], B2b.at[d - 1], s2b.at[d - 1], r2b.at[d - 1], partner).wait_recv()
            piece = piece + B2b[d - 1]
        corr_ref[high, :] = piece
        cpan[z, y, core, high] = piece
        crow[o, high] = piece
        for d in range(1, ys):
            spot = cpan.at[z, y, core, high]
            remote(spot, spot, g1b_s.at[d - 1], g1b_r.at[d - 1], ypeer[d - 1]).start()
        for d in range(1, groups):
            remote(cpan.at[z, y, core], crow.at[o], sx.at[0, d - 1], rx.at[0, d - 1], xpeer[d - 1]).start()

    def late_one():
        out = []
        for d in range(1, ys):
            out.append(send(X0.at[last, lax.rem(y + d, ys)], BL1.at[d - 1], sl1.at[d - 1], rl1.at[d - 1], ypeer[d - 1]))
        return out

    def late_two(copies):
        acc = X0[last, y]
        for d, copy in enumerate(copies):
            copy.wait_recv()
            acc = acc + BL1[d]
        YL[...] = acc
        e = ahead(3)

        @pl.when(e > 0)
        def _():
            remote(YL, BL2.at[e - 1], sl2.at[e - 1], rl2.at[e - 1], at(last, y)).start()

    def late_end():
        piece = YL[...]
        for e in range(1, zs):
            remote(BL2.at[e - 1], BL2.at[e - 1], sl2.at[e - 1], rl2.at[e - 1], partner).wait_recv()
            piece = piece + BL2[e - 1]
        corr_ref[...] = piece
        cpan[z, y, core] = piece
        crow[o] = piece
        spot = cpan.at[z, y, core]
        for e in range(1, zs):
            remote(spot, spot, gl_s.at[e - 1], gl_r.at[e - 1], zpeer[e - 1]).start()
        for d in range(1, groups):
            remote(spot, crow.at[o], sx.at[0, d - 1], rx.at[0, d - 1], xpeer[d - 1]).start()

    def late_spread():
        spot = cpan.at[last, y, core]
        e = behind(3)

        @pl.when(e > 0)
        def _():
            remote(spot, spot, gl_s.at[e - 1], gl_r.at[e - 1], partner).wait_recv()

        out = []
        for d in range(1, ys):
            out.append(send(spot, spot, gm_s.at[d - 1], gm_r.at[d - 1], ypeer[d - 1]))
        return out

    def late_forward(copies):
        for copy in copies:
            copy.wait_recv()
        column = cpan.at[last, :, core]
        return send(column, column, gf_s.at[0], gf_r.at[0], partner)

    def g_two_a(i):
        zp = order_z[i]
        spot = cpan.at[zp, y, core, low]
        e = behind(i)

        @pl.when(e > 0)
        def _():
            remote(spot, spot, g1a_s.at[e - 1], g1a_r.at[e - 1], partner).wait_recv()

        for d in range(1, ys):
            two_a[i, d] = send(spot, spot, g2a_s.at[i, d - 1], g2a_r.at[i, d - 1], ypeer[d - 1])

    def g_end_a(i):
        for d in range(1, ys):
            two_a[i, d].wait_recv()
        column = cpan.at[order_z[i], :, core, low]
        return send(column, column, fa_s.at[i], fa_r.at[i], partner)

    def g_two_b():
        for d in range(1, ys):
            spot = cpan.at[z, y, core, high]
            remote(spot, spot, g1b_s.at[d - 1], g1b_r.at[d - 1], partner).wait_recv()
        column = cpan.at[z, :, core, high]
        for e in range(1, zs):
            remote(column, column, g2b_s.at[e - 1], g2b_r.at[e - 1], zpeer[e - 1]).start()
        remote(column, column, fb_s.at[0], fb_r.at[0], partner).start()

    def g_end_b(i):
        e = behind(i)
        column = cpan.at[order_z[i], :, core, high]

        @pl.when(e > 0)
        def _():
            remote(column, column, g2b_s.at[e - 1], g2b_r.at[e - 1], partner).wait_recv()
            remote(column, column, fb_s.at[e], fb_r.at[e], partner).start()

    correlate(a_ref, o)
    pair_send(0)

    prow[...] = jnp.zeros(prow.shape, F32)
    prow[0:2, 0:n * nn] = pot_ref[...]
    pcol[...] = prow[...].T

    order = [(b, 0), (b, 1), (mate, 0), (mate, 1), (back1, 0), (back2, 0), (fwd2, 0), (back1, 1), (back2, 1),
             (fwd2, 1)]
    shape = (2 * n, 10 * n)
    ci = lax.broadcasted_iota(jnp.int32, shape, 1)
    gid = jnp.zeros(shape, jnp.int32)
    for q, (dev, k) in enumerate(order):
        gid = jnp.where((ci >= q * n) & (ci < (q + 1) * n), dev * 2 + k, gid)
    r, c = rows_and_cols((2 * n, n))
    pick_r = jnp.where(r - n * quotient(r, n) == c, 1.0, 0.0)
    r, c = rows_and_cols((n, 10 * n))
    pick_c = jnp.where(c - n * quotient(c, n) == r, 1.0, 0.0)
    bt = [hdot(hdot(pick_r, db_ref[:, u, :].astype(F32)), pick_c) for u in range(3)]
    t1.wait_recv()
    t2.wait_recv()
    M = [jnp.zeros(shape, F32) for _ in range(3)]
    for d in range(3):
        code = tbl[d, 0:2 * n, 9:10]
        factor = jnp.where(code < 0, 0.0, jnp.where(code == 0, 0.5, jnp.where(code == 1, 1.0, 2.0)))
        for a in range(3):
            t = jnp.zeros(shape, F32)
            for u in range(3):
                t = t + jnp.where(tbl[d, 0:2 * n, a * 3 + u:a * 3 + u + 1] == gid, bt[u], 0.0)
            t = t * factor
            M[a] = M[a] + 0.5 * lax.dot_general(t[:, 0:2 * n], t, (((0,), (0,)), ((), ())), precision=HIGH,
                                                preferred_element_type=F32)
    half = 2 * pad
    r, c = rows_and_cols((half, 2 * n))
    rs = quotient(r, pad)
    rq = r - rs * pad
    ri1 = quotient(rq, n)
    ri2 = rq - ri1 * n
    ok = rq < nn
    cs = quotient(c, n)
    ci = c - cs * n
    L1 = jnp.where(ok & (cs == rs) & (ci == ri1), 1.0, 0.0)
    L2 = jnp.where(ok & (cs == rs) & (ci == ri2), 1.0, 0.0)
    LM1 = hdot(L1, M[1])
    LM2 = hdot(L2, M[2])
    r, c = rows_and_cols((n * 32, 2 * n))
    ri = quotient(r, 32)
    rs = quotient(r, 16) - 2 * ri
    cs = quotient(c, n)
    L0 = jnp.where((cs == rs) & ((c - cs * n) == ri), 1.0, 0.0)
    LM0 = hdot(L0, M[0])

    def expand(m12, m0, base, count):
        wide = count * pad
        r, c = rows_and_cols((10 * n, wide))
        cs = quotient(c, pad)
        cq = c - cs * pad
        cl1 = quotient(cq, n)
        cl2 = cq - cl1 * n
        ok = cq < nn
        rs = quotient(r, n)
        ri = r - rs * n
        ok = ok & (cs + base == rs)
        C1 = jnp.where(ok & (ri == cl1), 1.0, 0.0)
        C2 = jnp.where(ok & (ri == cl2), 1.0, 0.0)
        r, c = rows_and_cols((half, wide))
        rq = r - quotient(r, pad) * pad
        cq = c - quotient(c, pad) * pad
        ri1 = quotient(rq, n)
        cl1 = quotient(cq, n)
        same1 = ri1 == cl1
        same2 = (rq - ri1 * n) == (cq - cl1 * n)
        full = jnp.where(same2, hdot(LM1, C1), 0.0) + jnp.where(same1, hdot(LM2, C2), 0.0)
        hi, lo = split_two(full)
        m12[0:half, :] = hi
        m12[half:2 * half, :] = lo
        step = count * 16
        r, c = rows_and_cols((10 * n, n * step))
        cl = quotient(c, step)
        cs = quotient(c - cl * step, 16)
        rs = quotient(r, n)
        C0 = jnp.where((rs == cs + base) & ((r - rs * n) == cl), 1.0, 0.0)
        r, c = rows_and_cols((n * 32, n * step))
        same = (r - 16 * quotient(r, 16)) == (c - 16 * quotient(c, 16))
        full = jnp.where(same, hdot(LM0, C0), 0.0)
        hi, lo = split_two(full)
        m0[0:n * 32, :] = hi
        m0[n * 32:n * 64, :] = lo

    def apply_inner(S, m12, fresh):
        count = S.shape[1]

        @pl.loop(0, n)
        def _(i):
            got = jnp.dot(m12[...], S[i].reshape(count * pad, w), preferred_element_type=F32)
            got = (got[0:half] + got[half:2 * half]).reshape(2, pad, w)
            Wsc[i] = got if fresh else Wsc[i] + got

    def apply_outer(S, m0):
        count = S.shape[1]

        @pl.loop(0, pad // 16)
        def _(i):
            rows = pl.ds(pl.multiple_of(i * 16, 16), 16)
            got = jnp.dot(m0[...], S[:, :, rows, :].reshape(n * count * 16, w), preferred_element_type=F32)
            Wsc[:, :, rows, :] = Wsc[:, :, rows, :] + (got[0:n * 32] + got[n * 32:n * 64]).reshape(n, 2, 16, w)

    expand(m12a, m0a, 0, 4)
    for k in range(2):
        h0[k].wait_recv()
        spread(halo.at[0, k], SA, 2 + k)
    apply_inner(SA, m12a, True)
    apply_outer(SA, m0a)
    expand(m12b, m0b, 4, 3)
    expand(m12c, m0c, 7, 3)

    sends[0].wait_recv()
    xf0.start()
    sends[1].wait_recv()
    xf1.start()
    h1[0].wait_recv()
    h3[0].start()
    spread(halo.at[1, 0], SB, 0)
    h2[0].wait_recv()
    spread(halo.at[2, 0], SB, 1)
    h3[0].wait_recv()
    spread(halo.at[3, 0], SB, 2)
    apply_inner(SB, m12b, False)
    apply_outer(SB, m0b)

    h1[1].wait_recv()
    h3[1].start()
    sends[2].wait_recv()
    correlate(gath.at[0], left)
    pair_send(1)
    sends[3].wait_recv()
    correlate(gath.at[1], right)
    pair_send(2)
    spread(halo.at[1, 1], SC, 0)
    h2[1].wait_recv()
    spread(halo.at[2, 1], SC, 1)
    h3[1].wait_recv()
    spread(halo.at[3, 1], SC, 2)
    apply_inner(SC, m12c, False)
    for i in range(3):
        pair_add(i)
        c_one(i)
    apply_outer(SC, m0c)

    for k in range(2):
        for l in range(n):
            full = Wsc[l, k] + (pcol[l * nn:l * nn + pad, k:k + 1] * alive[k]) * SA[l, k].astype(F32)
            hi, lo = split_two(full)
            R[k, l * nn:(l + 1) * nn, w:2 * w] = hi[0:nn]
            R[k, l * nn:(l + 1) * nn, 2 * w:3 * w] = lo[0:nn]

    fock_part(a_ref, o)
    fock_part(gath.at[0], left)
    for i in range(3):
        c_two_a(i)
    pl.when(z != last)(c_two_b)
    fock_part(gath.at[1], right)
    pl.when(z != last)(c_end)
    xf0.wait_recv()
    xf1.wait_recv()
    correlate(gath.at[2], last)
    pair_send(3)
    pair_add(3)
    late = late_one()
    fock_part(gath.at[2], last)

    first = {}

    for h in range(2):
        first[0, h] = send(p_ref.at[1, :, :, 1 - core, part[h]], abuf.at[0, h], sa.at[0, h], ra.at[0, h], partner)
    for i in range(3):
        g_two_a(i)
    pl.when(z != last)(g_two_b)
    late_two(late)

    def add_pair(f, h):
        first[f, h].wait_recv()
        X[f, h] = p_ref[1, :, :, core, part[h]] + abuf[f, h]

    def scatter_one(f, h):
        out = []
        for d in range(1, ys if h == 0 else zs):
            if h == 0:
                t = lax.rem(y + d, ys)
                src = X.at[f, h, :, t]
            else:
                t = lax.rem(z + d, zs)
                src = X.at[f, h, t]
            out.append(send(src, B1.at[f, h, d - 1], s1.at[f, h, d - 1], r1.at[f, h, d - 1],
                            (ypeer if h == 0 else zpeer)[d - 1]))
        return out

    def scatter_two(f, h, copies):
        for copy in copies:
            copy.wait_recv()
        acc = X[f, h, :, y] if h == 0 else X[f, h, z]
        for d in range(1, ys if h == 0 else zs):
            acc = acc + B1[f, h, d - 1]
        Y[f, h] = acc
        out = []
        for d in range(1, zs if h == 0 else ys):
            t = lax.rem(z + d, zs) if h == 0 else lax.rem(y + d, ys)
            out.append(send(Y.at[f, h, t], B2.at[f, h, d - 1], s2.at[f, h, d - 1], r2.at[f, h, d - 1],
                            (zpeer if h == 0 else ypeer)[d - 1]))
        return out

    def scatter_end(f, h, copies):
        for copy in copies:
            copy.wait_recv()
        acc = Y[f, h, z] if h == 0 else Y[f, h, y]
        for d in range(1, zs if h == 0 else ys):
            acc = acc + B2[f, h, d - 1]
        return acc

    for h in range(2):
        add_pair(0, h)
    forwards = []
    for i in range(3):
        forwards.append(g_end_a(i))
        g_end_b(i)
    pl.when(z == last)(late_end)
    late = late_spread()
    one = {}
    two = {}
    for h in range(2):
        one[0, h] = scatter_one(0, h)
    forwards.append(late_forward(late))

    def diagonal(count, start):
        r = lax.broadcasted_iota(jnp.int32, (count, w), 0) + start
        c = lax.broadcasted_iota(jnp.int32, (count, w), 1) + o * w
        return r == c

    def product(left):
        lhi, llo = split_two(left)
        big = jnp.dot(jnp.concatenate([lhi, llo], axis=0), pan_hi[...], preferred_element_type=F32)
        return big[0:rows] + big[rows:2 * rows] + jnp.dot(lhi, pan_lo[...], preferred_element_type=F32)

    def row_gather(g, value):
        urow[g, o] = value
        out = []
        for d in range(1, groups):
            out.append(send(urow.at[g, o], urow.at[g, o], sx.at[g + 1, d - 1], rx.at[g + 1, d - 1], xpeer[d - 1]))
        return out

    def whole_row(ref):
        return jnp.concatenate([ref[k] for k in range(groups)], axis=1)

    step = total_rows // zs

    def turn_panel(k):
        block = jnp.where(diagonal(step, k * step), 1.5, 0.0) - 0.5 * cpan[k].reshape(step, w)
        hi, lo = split_two(block)
        span = pl.ds(k * step, step)
        pan_hi[span, :] = hi
        pan_lo[span, :] = lo

    for d in range(1, groups):
        remote(crow.at[0], crow.at[0], sx.at[0, d - 1], rx.at[0, d - 1], partner).wait_recv()
    for copy in forwards:
        copy.wait_recv()
    for i in range(3):
        column = cpan.at[0, :, core, high]
        e = behind(i)
        remote(column, column, fb_s.at[e], fb_r.at[e], partner).wait_recv()
    for k in range(zs):
        turn_panel(k)
    moved = row_gather(0, product(whole_row(crow)))
    for h in range(2):
        two[0, h] = scatter_two(0, h, one[0, h])
    for copy in moved:
        copy.wait_recv()
    moved = row_gather(1, product(whole_row(urow.at[0])))
    for h in range(2):
        fock_ref[part[h], :] = scatter_end(0, h, two[0, h])
    for copy in moved:
        copy.wait_recv()
    right = product(whole_row(urow.at[1]))
    turn = jnp.where(diagonal(rows, b * rows), 1.5, 0.0) - 0.5 * corr_ref[...]
    inv_ref[...] = 1.5 * turn - 0.5 * right
    def sent(ref, sem):
        remote(ref, ref, sem, rl1.at[0], partner).wait_send()

    for i in range(3):
        e = ahead(i)

        @pl.when(e > 0)
        def _():
            sent(B1b.at[e - 1], s1b.at[e - 1])
            sent(B2a.at[e - 1], s2a.at[e - 1])

    @pl.when(z != last)
    def _():
        sent(YL, sl2.at[ahead(3) - 1])
        for e in range(1, zs):
            sent(cpan.at[0, 0, core, low], g1a_s.at[e - 1])
            sent(cpan.at[0, :, core, high], g2b_s.at[e - 1])
        for d in range(1, ys):
            sent(B2b.at[d - 1], s2b.at[d - 1])
            sent(cpan.at[0, 0, core, high], g1b_s.at[d - 1])

    @pl.when(z == last)
    def _():
        for e in range(1, zs):
            sent(cpan.at[0, 0, core], gl_s.at[e - 1])

    for i in range(3):
        sent(cpan.at[0, :, core, high], fb_s.at[behind(i)])
    for d in range(1, groups):
        sent(crow.at[0], sx.at[0, d - 1])
    for copy in started:
        copy.wait_send()
    for i in range(4):
        sends[i].wait_send()
    xf0.wait_send()
    xf1.wait_send()
    t1.wait_send()
    t2.wait_send()
    for k in range(2):
        h0[k].wait_send()
        h1[k].wait_send()
        h2[k].wait_send()
        h3[k].wait_send()


def whole(orbitals, potential, deriv_blocks, levels, box_counts, neighbours):
    slots, coefs, w = orbitals.shape
    n = deriv_blocks.shape[1]
    nn = n * n
    pad = -(-nn // 16) * 16
    boxes = lax.axis_size("box")
    groups = lax.axis_size("orb")
    zs = groups
    ys = boxes // 2 // zs
    fy = max(ys - 1, 1)
    total = groups * w
    rows = total // boxes
    half = rows // 2
    far = max(zs, ys) - 1
    vm = pl.BlockSpec(memory_space=pltpu.VMEM)
    sm = pl.BlockSpec(memory_space=pltpu.SMEM)
    column = -(-((n - 1) * nn + pad) // 128) * 128
    dma = pltpu.SemaphoreType.DMA
    out = jax.ShapeDtypeStruct((rows, w), F32)
    return pl.pallas_call(
        functools.partial(whole_kernel, n, pad, zs, ys),
        out_shape=(out, out, out),
        in_specs=[pl.BlockSpec(memory_space=pl.ANY), sm, sm, sm, vm, vm],
        out_specs=(vm, vm, vm),
        scratch_shapes=[
            pltpu.VMEM((slots, coefs, w), BF16),
            dma(()),
            pltpu.VMEM((3, slots, coefs, w), BF16),
            pltpu.VMEM((4, slots, coefs, w), BF16),
            pltpu.VMEM((n, 4, pad, w), BF16),
            pltpu.VMEM((n, 3, pad, w), BF16),
            pltpu.VMEM((n, 3, pad, w), BF16),
            pltpu.VMEM((n, 2, pad, w), F32),
            pltpu.VMEM((slots, coefs, 3 * w), BF16),
            pltpu.VMEM((4 * pad, 4 * pad), BF16),
            pltpu.VMEM((4 * pad, 3 * pad), BF16),
            pltpu.VMEM((4 * pad, 3 * pad), BF16),
            pltpu.VMEM((n * 64, n * 64), BF16),
            pltpu.VMEM((n * 64, n * 48), BF16),
            pltpu.VMEM((n * 64, n * 48), BF16),
            pltpu.VMEM((3, -(-slots * n // 8) * 8, 128), jnp.int32),
            pltpu.VMEM((8, column), F32),
            pltpu.VMEM((column, 8), F32),
            pltpu.VMEM((2, groups, total // groups // (2 * rows), 2, rows, w), F32),
            pltpu.VMEM((zs, ys, rows, w), F32),
            pltpu.VMEM((zs, ys, rows, w), F32),
            pltpu.VMEM((zs, fy, half, w), F32),
            pltpu.VMEM((zs - 1, ys, half, w), F32),
            pltpu.VMEM((zs, half, w), F32),
            pltpu.VMEM((ys, half, w), F32),
            pltpu.VMEM((zs - 1, half, w), F32),
            pltpu.VMEM((fy, half, w), F32),
            pltpu.VMEM((fy, rows, w), F32),
            pltpu.VMEM((rows, w), F32),
            pltpu.VMEM((zs - 1, rows, w), F32),
            pltpu.VMEM((1, 2, zs, ys, half, w), F32),
            pltpu.VMEM((1, 2, zs, ys, half, w), F32),
            pltpu.VMEM((1, 2, far, zs, half, w), F32),
            pltpu.VMEM((1, 2, zs, half, w), F32),
            pltpu.VMEM((1, 2, far, half, w), F32),
            pltpu.VMEM((zs, ys, 2, rows, w), F32),
            pltpu.VMEM((groups, rows, w), F32),
            pltpu.VMEM((2, groups, rows, w), F32),
            pltpu.VMEM((total, w), BF16),
            pltpu.VMEM((total, w), BF16),
            dma((6,)), dma((3, 2)), dma((8,)), dma((4, 2)), dma((2,)), dma((2,)),
            dma((zs,)), dma((zs,)),
            dma((zs, fy)), dma((zs, fy)), dma((zs - 1,)), dma((zs - 1,)),
            dma((zs - 1,)), dma((zs - 1,)), dma((fy,)), dma((fy,)),
            dma((zs - 1,)), dma((zs - 1,)), dma((fy,)), dma((fy,)),
            dma((zs, fy)), dma((zs, fy)), dma((zs - 1,)), dma((zs - 1,)),
            dma((zs,)), dma((zs,)), dma((zs,)), dma((zs,)),
            dma((fy,)), dma((fy,)), dma((zs - 1,)), dma((zs - 1,)),
            dma((zs - 1,)), dma((zs - 1,)), dma((fy,)), dma((fy,)), dma((1,)), dma((1,)),
            dma((1, 2)), dma((1, 2)),
            dma((1, 2, far)), dma((1, 2, far)),
            dma((1, 2, far)), dma((1, 2, far)),
            dma((3, groups - 1)), dma((3, groups - 1)),
        ],
        compiler_params=pltpu.CompilerParams(collective_id=0, has_side_effects=True, vmem_limit_bytes=63 << 20),
        name="whole",
    )(orbitals, jnp.transpose(neighbours, (0, 2, 1)), levels, box_counts, potential,
      jnp.transpose(deriv_blocks, (1, 0, 2)))


def settle_kernel(*refs):
    for src, dst in zip(refs[:3], refs[3:]):
        dst[...] = src[...]


def settle(arrays):
    vm = pl.BlockSpec(memory_space=pltpu.VMEM)
    return pl.pallas_call(
        settle_kernel,
        out_shape=tuple(jax.ShapeDtypeStruct(a.shape, a.dtype) for a in arrays),
        in_specs=[vm] * 3,
        out_specs=(vm,) * 3,
        name="settle",
    )(*arrays)


def body(orbitals, potential, deriv_blocks, levels, box_counts, neighbours):
    return settle(whole(orbitals, potential, deriv_blocks, levels, box_counts, neighbours))


def solution(mesh):
    in_specs = (
        P("box", None, "orb"),
        P("box", None),
        P(),
        P("box"),
        P("box"),
        P("box", None, None),
    )
    out_specs = (P("box", "orb"), P("box", "orb"), P("box", "orb"))
    return jax.shard_map(body, mesh=mesh, in_specs=in_specs, out_specs=out_specs, check_vma=False)
```

```python
import functools

import jax
import jax.numpy as jnp
from jax import lax
from jax.experimental import pallas as pl
from jax.experimental.pallas import tpu as pltpu
from jax.sharding import PartitionSpec as P

MESH = pl.DeviceIdType.MESH
HIGH = lax.Precision.HIGHEST
F32 = jnp.float32
BF16 = jnp.bfloat16


def quotient(x, n):
    return jnp.floor((x + 0.5) * (1.0 / n))


def rows_and_cols(shape):
    r = lax.broadcasted_iota(jnp.int32, shape, 0).astype(F32)
    c = lax.broadcasted_iota(jnp.int32, shape, 1).astype(F32)
    return r, c


def split_two(x):
    hi = x.astype(BF16)
    return hi, (x - hi.astype(F32)).astype(BF16)


def hdot(a, b):
    return jnp.dot(a, b, precision=HIGH, preferred_element_type=F32)


def whole_kernel(n, pad, zs, ys, a_hbm, nb_ref, lev_ref, cnt_ref, pot_ref, db_ref, fock_ref, corr_ref, inv_ref,
                 a_ref, in_sem, gath, halo, SA, SB, SC, Wsc, R, m12a, m12b, m12c, m0a, m0b, m0c, tbl, prow, pcol,
                 p_ref, abuf0, X0, B1a, B1b, Ya, Yb, B2a, B2b, BL1, YL, BL2, abuf, X, B1, Y, B2,
                 cpan, crow, urow, pan_hi, pan_lo,
                 xs_sem, xr_sem, hs_sem, hr_sem, ts_sem, tr_sem,
                 sa0, ra0, s1a, r1a, s1b, r1b, s2a, r2a, s2b, r2b, ga_s, ga_r, gb_s, gb_r, gf_s, gf_r,
                 sl1, rl1, sl2, rl2,
                 sa, ra, s1, r1, s2, r2, sx, rx, su, ru):
    b = lax.axis_index("box")
    o = lax.axis_index("orb")
    boxes = lax.axis_size("box")
    groups = lax.axis_size("orb")
    core = lax.rem(b, 2)
    chip = b // 2
    z = chip // ys
    y = lax.rem(chip, ys)
    sgn = 1 - 2 * core
    mate = b + sgn
    back1 = lax.rem(b - sgn + boxes, boxes)
    fwd2 = lax.rem(b + 2 * sgn + boxes, boxes)
    back2 = lax.rem(b - 2 * sgn + boxes, boxes)
    right = lax.rem(o + 1, groups)
    left = lax.rem(o + groups - 1, groups)
    nn = n * n
    w = a_ref.shape[2]
    rows = corr_ref.shape[0]
    half_rows = rows // 2
    total_rows = zs * ys * 2 * rows

    def at(zz, yy):
        return ((zz * ys + yy) * 2 + core, o)

    partner = (mate, o)
    zpeer = [at(lax.rem(z + d, zs), y) for d in range(1, zs)]
    ypeer = [at(z, lax.rem(y + d, ys)) for d in range(1, ys)]
    xpeer = [(b, lax.rem(o + d, groups)) for d in range(1, groups)]

    fetch = pltpu.make_async_copy(a_hbm, a_ref, in_sem)
    fetch.start()

    shape = tbl.shape[1:]
    r = lax.broadcasted_iota(jnp.int32, shape, 0)
    c = lax.broadcasted_iota(jnp.int32, shape, 1)
    own = jnp.zeros(shape, jnp.int32)
    for k in range(2):
        mine = (r >= k * n) & (r < (k + 1) * n)
        for a in range(3):
            own = jnp.where(mine & (c == a * 3), nb_ref[k, 0, a], own)
            own = jnp.where(mine & (c == a * 3 + 1), b * 2 + k, own)
            own = jnp.where(mine & (c == a * 3 + 2), nb_ref[k, 1, a], own)
        code = jnp.where(cnt_ref[0] > k, lev_ref[k], -1)
        own = jnp.where(mine & (c == 9), code, own)
    tbl[0] = own

    barrier = pltpu.get_barrier_semaphore()
    peers = [partner, (back1, o), (fwd2, o), (back2, o)] + xpeer + ypeer + zpeer
    for dev in peers:
        pl.semaphore_signal(barrier, inc=1, device_id=dev, device_id_type=MESH)
    pl.semaphore_wait(barrier, len(peers))

    def remote(src, dst, ssem, rsem, dev):
        return pltpu.make_async_remote_copy(src_ref=src, dst_ref=dst, send_sem=ssem, recv_sem=rsem,
                                            device_id=dev, device_id_type=MESH)

    sends = {}
    for i, (k, q, dev) in enumerate(((0, 0, (b, right)), (1, 1, (b, left)), (1, 0, (b, right)), (0, 1, (b, left)))):
        sends[i] = remote(a_hbm.at[k], gath.at[q, k], xs_sem.at[i], xr_sem.at[q, k], dev)
    xf0 = remote(gath.at[0, 0], gath.at[2, 0], xs_sem.at[4], xr_sem.at[2, 0], (b, right))
    xf1 = remote(gath.at[1, 1], gath.at[2, 1], xs_sem.at[5], xr_sem.at[2, 1], (b, left))
    h1 = [remote(a_hbm.at[k], halo.at[1, k], hs_sem.at[k], hr_sem.at[1, k], (back1, o)) for k in range(2)]
    h2 = [remote(a_hbm.at[k], halo.at[2, k], hs_sem.at[2 + k], hr_sem.at[2, k], (fwd2, o)) for k in range(2)]
    h0 = [remote(a_hbm.at[k], halo.at[0, k], hs_sem.at[4 + k], hr_sem.at[0, k], partner) for k in range(2)]
    h3 = [remote(halo.at[1, k], halo.at[3, k], hs_sem.at[6 + k], hr_sem.at[3, k], partner) for k in range(2)]
    t1 = remote(tbl.at[0], tbl.at[1], ts_sem.at[0], tr_sem.at[0], partner)
    t2 = remote(tbl.at[0], tbl.at[2], ts_sem.at[1], tr_sem.at[1], (back1, o))
    sends[0].start()
    sends[1].start()
    t2.start()
    h1[0].start()
    h2[0].start()
    t1.start()
    h0[0].start()
    h0[1].start()
    sends[2].start()
    sends[3].start()
    h1[1].start()
    h2[1].start()

    fetch.wait()

    alive = [jnp.where(cnt_ref[0] > k, 1.0, 0.0) for k in range(2)]
    for k in range(2):
        R[k, :, 0:w] = (a_ref[k].astype(F32) * alive[k]).astype(BF16)

    def correlate(block, place):
        total = jnp.zeros((w, w), F32)
        for k in range(2):
            total = total + lax.dot_general(block[k], R[k, :, 0:w], (((0,), (0,)), ((), ())),
                                            preferred_element_type=F32)
        p_ref[0, place] = total.reshape(ys, 2, rows, w)

    def fock_part(block, place):
        total = jnp.zeros((w, 2 * w), F32)
        for k in range(2):
            total = total + lax.dot_general(block[k], R[k, :, w:3 * w], (((0,), (0,)), ((), ())),
                                            preferred_element_type=F32)
        p_ref[1, place] = (total[:, 0:w] + total[:, w:2 * w]).reshape(ys, 2, rows, w)

    edge = nn // 16 * 16
    for S in (SA, SB, SC):
        S[:, :, edge:pad, :] = jnp.zeros((n, S.shape[1], pad - edge, w), BF16)

    def spread(block, S, q):
        for l in range(n):
            S[l, q, 0:nn, :] = block[l * nn:(l + 1) * nn, :]

    spread(a_ref.at[0], SA, 0)
    spread(a_ref.at[1], SA, 1)
    started = []

    def send(src, dst, ssem, rsem, dev):
        copy = pltpu.make_async_remote_copy(src_ref=src, dst_ref=dst, send_sem=ssem, recv_sem=rsem,
                                            device_id=dev, device_id_type=MESH)
        copy.start()
        started.append(copy)
        return copy

    part = [pl.ds(0, half_rows), pl.ds(half_rows, half_rows)]

    order_z = [o, left, right, lax.rem(o + 2, groups)]
    last = order_z[3]
    low, high = part
    pairs = {}
    one_a = {}

    def ahead(i):
        return lax.rem(order_z[i] - z + zs, zs)

    def behind(i):
        return lax.rem(z - order_z[i] + zs, zs)

    def pair_send(i):
        zp = order_z[i]
        pairs[i] = send(p_ref.at[0, zp, :, 1 - core], abuf0.at[zp], sa0.at[i], ra0.at[i], partner)

    def pair_add(i):
        zp = order_z[i]
        pairs[i].wait_recv()
        X0[zp] = p_ref[0, zp, :, core] + abuf0[zp]

    def c_one(i):
        zp = order_z[i]
        for d in range(1, ys):
            one_a[i, d] = send(X0.at[zp, lax.rem(y + d, ys), low], B1a.at[i, d - 1], s1a.at[i, d - 1],
                               r1a.at[i, d - 1], ypeer[d - 1])
        e = ahead(i)

        @pl.when(e > 0)
        def _():
            remote(X0.at[zp, :, high], B1b.at[e - 1], s1b.at[e - 1], r1b.at[e - 1], at(zp, y)).start()

    def c_two_a(i):
        zp = order_z[i]
        acc = X0[zp, y, low]
        for d in range(1, ys):
            one_a[i, d].wait_recv()
            acc = acc + B1a[i, d - 1]
        Ya[zp] = acc
        e = ahead(i)

        @pl.when(e > 0)
        def _():
            remote(Ya.at[zp], B2a.at[e - 1], s2a.at[e - 1], r2a.at[e - 1], at(zp, y)).start()

    def c_two_b():
        for e in range(1, zs):
            remote(B1b.at[e - 1], B1b.at[e - 1], s1b.at[e - 1], r1b.at[e - 1], partner).wait_recv()
        acc = X0[z, :, high]
        for e in range(1, zs):
            acc = acc + B1b[e - 1]
        Yb[...] = acc
        for d in range(1, ys):
            remote(Yb.at[lax.rem(y + d, ys)], B2b.at[d - 1], s2b.at[d - 1], r2b.at[d - 1], ypeer[d - 1]).start()

    def publish():
        spot = cpan.at[z, y, core]
        for e in range(1, zs):
            remote(spot, spot, ga_s.at[e - 1], ga_r.at[e - 1], zpeer[e - 1]).start()
        for d in range(1, ys):
            remote(spot, spot, gb_s.at[z, d - 1], gb_r.at[z, d - 1], ypeer[d - 1]).start()
        for d in range(1, groups):
            remote(spot, crow.at[o], sx.at[0, d - 1], rx.at[0, d - 1], xpeer[d - 1]).start()

    def c_end():
        piece = Ya[z]
        for e in range(1, zs):
            remote(B2a.at[e - 1], B2a.at[e - 1], s2a.at[e - 1], r2a.at[e - 1], partner).wait_recv()
            piece = piece + B2a[e - 1]
        corr_ref[low, :] = piece
        cpan[z, y, core, low] = piece
        crow[o, low] = piece
        piece = Yb[y]
        for d in range(1, ys):
            remote(B2b.at[d - 1], B2b.at[d - 1], s2b.at[d - 1], r2b.at[d - 1], partner).wait_recv()
            piece = piece + B2b[d - 1]
        corr_ref[high, :] = piece
        cpan[z, y, core, high] = piece
        crow[o, high] = piece
        publish()

    def g_two(i):
        zp = order_z[i]
        spot = cpan.at[zp, y, core]
        e = behind(i)

        @pl.when(e > 0)
        def _():
            remote(spot, spot, ga_s.at[e - 1], ga_r.at[e - 1], partner).wait_recv()
            for d in range(1, ys):
                remote(spot, spot, gb_s.at[zp, d - 1], gb_r.at[zp, d - 1], ypeer[d - 1]).start()

    def g_end(i):
        zp = order_z[i]
        spot = cpan.at[zp, y, core]
        for d in range(1, ys):
            remote(spot, spot, gb_s.at[zp, d - 1], gb_r.at[zp, d - 1], partner).wait_recv()
        column = cpan.at[zp, :, core]
        return send(column, column, gf_s.at[i], gf_r.at[i], partner)

    def late_one():
        out = []
        for d in range(1, ys):
            out.append(send(X0.at[last, lax.rem(y + d, ys)], BL1.at[d - 1], sl1.at[d - 1], rl1.at[d - 1], ypeer[d - 1]))
        return out

    def late_two(copies):
        acc = X0[last, y]
        for d, copy in enumerate(copies):
            copy.wait_recv()
            acc = acc + BL1[d]
        YL[...] = acc
        e = ahead(3)

        @pl.when(e > 0)
        def _():
            remote(YL, BL2.at[e - 1], sl2.at[e - 1], rl2.at[e - 1], at(last, y)).start()

    def late_end():
        piece = YL[...]
        for e in range(1, zs):
            remote(BL2.at[e - 1], BL2.at[e - 1], sl2.at[e - 1], rl2.at[e - 1], partner).wait_recv()
            piece = piece + BL2[e - 1]
        corr_ref[...] = piece
        cpan[z, y, core] = piece
        crow[o] = piece
        publish()

    correlate(a_ref, o)
    pair_send(0)

    prow[...] = jnp.zeros(prow.shape, F32)
    prow[0:2, 0:n * nn] = pot_ref[...]
    pcol[...] = prow[...].T

    order = [(b, 0), (b, 1), (mate, 0), (mate, 1), (back1, 0), (back2, 0), (fwd2, 0), (back1, 1), (back2, 1),
             (fwd2, 1)]
    shape = (2 * n, 10 * n)
    ci = lax.broadcasted_iota(jnp.int32, shape, 1)
    gid = jnp.zeros(shape, jnp.int32)
    for q, (dev, k) in enumerate(order):
        gid = jnp.where((ci >= q * n) & (ci < (q + 1) * n), dev * 2 + k, gid)
    r, c = rows_and_cols((2 * n, n))
    pick_r = jnp.where(r - n * quotient(r, n) == c, 1.0, 0.0)
    r, c = rows_and_cols((n, 10 * n))
    pick_c = jnp.where(c - n * quotient(c, n) == r, 1.0, 0.0)
    bt = [hdot(hdot(pick_r, db_ref[:, u, :].astype(F32)), pick_c) for u in range(3)]
    t1.wait_recv()
    t2.wait_recv()
    M = [jnp.zeros(shape, F32) for _ in range(3)]
    for d in range(3):
        code = tbl[d, 0:2 * n, 9:10]
        factor = jnp.where(code < 0, 0.0, jnp.where(code == 0, 0.5, jnp.where(code == 1, 1.0, 2.0)))
        for a in range(3):
            t = jnp.zeros(shape, F32)
            for u in range(3):
                t = t + jnp.where(tbl[d, 0:2 * n, a * 3 + u:a * 3 + u + 1] == gid, bt[u], 0.0)
            t = t * factor
            M[a] = M[a] + 0.5 * lax.dot_general(t[:, 0:2 * n], t, (((0,), (0,)), ((), ())), precision=HIGH,
                                                preferred_element_type=F32)
    half = 2 * pad
    r, c = rows_and_cols((half, 2 * n))
    rs = quotient(r, pad)
    rq = r - rs * pad
    ri1 = quotient(rq, n)
    ri2 = rq - ri1 * n
    ok = rq < nn
    cs = quotient(c, n)
    ci = c - cs * n
    L1 = jnp.where(ok & (cs == rs) & (ci == ri1), 1.0, 0.0)
    L2 = jnp.where(ok & (cs == rs) & (ci == ri2), 1.0, 0.0)
    LM1 = hdot(L1, M[1])
    LM2 = hdot(L2, M[2])
    r, c = rows_and_cols((n * 32, 2 * n))
    ri = quotient(r, 32)
    rs = quotient(r, 16) - 2 * ri
    cs = quotient(c, n)
    L0 = jnp.where((cs == rs) & ((c - cs * n) == ri), 1.0, 0.0)
    LM0 = hdot(L0, M[0])

    def expand(m12, m0, base, count):
        wide = count * pad
        r, c = rows_and_cols((10 * n, wide))
        cs = quotient(c, pad)
        cq = c - cs * pad
        cl1 = quotient(cq, n)
        cl2 = cq - cl1 * n
        ok = cq < nn
        rs = quotient(r, n)
        ri = r - rs * n
        ok = ok & (cs + base == rs)
        C1 = jnp.where(ok & (ri == cl1), 1.0, 0.0)
        C2 = jnp.where(ok & (ri == cl2), 1.0, 0.0)
        r, c = rows_and_cols((half, wide))
        rq = r - quotient(r, pad) * pad
        cq = c - quotient(c, pad) * pad
        ri1 = quotient(rq, n)
        cl1 = quotient(cq, n)
        same1 = ri1 == cl1
        same2 = (rq - ri1 * n) == (cq - cl1 * n)
        full = jnp.where(same2, hdot(LM1, C1), 0.0) + jnp.where(same1, hdot(LM2, C2), 0.0)
        hi, lo = split_two(full)
        m12[0:half, :] = hi
        m12[half:2 * half, :] = lo
        step = count * 16
        r, c = rows_and_cols((10 * n, n * step))
        cl = quotient(c, step)
        cs = quotient(c - cl * step, 16)
        rs = quotient(r, n)
        C0 = jnp.where((rs == cs + base) & ((r - rs * n) == cl), 1.0, 0.0)
        r, c = rows_and_cols((n * 32, n * step))
        same = (r - 16 * quotient(r, 16)) == (c - 16 * quotient(c, 16))
        full = jnp.where(same, hdot(LM0, C0), 0.0)
        hi, lo = split_two(full)
        m0[0:n * 32, :] = hi
        m0[n * 32:n * 64, :] = lo

    def apply_inner(S, m12, fresh):
        count = S.shape[1]

        @pl.loop(0, n)
        def _(i):
            got = jnp.dot(m12[...], S[i].reshape(count * pad, w), preferred_element_type=F32)
            got = (got[0:half] + got[half:2 * half]).reshape(2, pad, w)
            Wsc[i] = got if fresh else Wsc[i] + got

    def apply_outer(S, m0):
        count = S.shape[1]

        @pl.loop(0, pad // 16)
        def _(i):
            rows = pl.ds(pl.multiple_of(i * 16, 16), 16)
            got = jnp.dot(m0[...], S[:, :, rows, :].reshape(n * count * 16, w), preferred_element_type=F32)
            Wsc[:, :, rows, :] = Wsc[:, :, rows, :] + (got[0:n * 32] + got[n * 32:n * 64]).reshape(n, 2, 16, w)

    expand(m12a, m0a, 0, 4)
    for k in range(2):
        h0[k].wait_recv()
        spread(halo.at[0, k], SA, 2 + k)
    apply_inner(SA, m12a, True)
    apply_outer(SA, m0a)
    expand(m12b, m0b, 4, 3)
    expand(m12c, m0c, 7, 3)

    sends[0].wait_recv()
    xf0.start()
    sends[1].wait_recv()
    xf1.start()
    h1[0].wait_recv()
    h3[0].start()
    spread(halo.at[1, 0], SB, 0)
    h2[0].wait_recv()
    spread(halo.at[2, 0], SB, 1)
    h3[0].wait_recv()
    spread(halo.at[3, 0], SB, 2)
    apply_inner(SB, m12b, False)
    apply_outer(SB, m0b)

    h1[1].wait_recv()
    h3[1].start()
    sends[2].wait_recv()
    correlate(gath.at[0], left)
    pair_send(1)
    sends[3].wait_recv()
    correlate(gath.at[1], right)
    pair_send(2)
    spread(halo.at[1, 1], SC, 0)
    h2[1].wait_recv()
    spread(halo.at[2, 1], SC, 1)
    h3[1].wait_recv()
    spread(halo.at[3, 1], SC, 2)
    apply_inner(SC, m12c, False)
    for i in range(3):
        pair_add(i)
        c_one(i)
    apply_outer(SC, m0c)

    for k in range(2):
        for l in range(n):
            full = Wsc[l, k] + (pcol[l * nn:l * nn + pad, k:k + 1] * alive[k]) * SA[l, k].astype(F32)
            hi, lo = split_two(full)
            R[k, l * nn:(l + 1) * nn, w:2 * w] = hi[0:nn]
            R[k, l * nn:(l + 1) * nn, 2 * w:3 * w] = lo[0:nn]

    fock_part(a_ref, o)
    fock_part(gath.at[0], left)
    for i in range(3):
        c_two_a(i)
    pl.when(z != last)(c_two_b)
    xf0.wait_recv()
    xf1.wait_recv()
    correlate(gath.at[2], last)
    pair_send(3)
    fock_part(gath.at[1], right)
    pair_add(3)
    late = late_one()
    pl.when(z != last)(c_end)
    fock_part(gath.at[2], last)

    first = {}

    for h in range(2):
        first[0, h] = send(p_ref.at[1, :, :, 1 - core, part[h]], abuf.at[0, h], sa.at[0, h], ra.at[0, h], partner)
    late_two(late)
    for i in range(3):
        g_two(i)

    def add_pair(f, h):
        first[f, h].wait_recv()
        X[f, h] = p_ref[1, :, :, core, part[h]] + abuf[f, h]

    def scatter_one(f, h):
        out = []
        for d in range(1, ys if h == 0 else zs):
            if h == 0:
                t = lax.rem(y + d, ys)
                src = X.at[f, h, :, t]
            else:
                t = lax.rem(z + d, zs)
                src = X.at[f, h, t]
            out.append(send(src, B1.at[f, h, d - 1], s1.at[f, h, d - 1], r1.at[f, h, d - 1],
                            (ypeer if h == 0 else zpeer)[d - 1]))
        return out

    def scatter_two(f, h, copies):
        for copy in copies:
            copy.wait_recv()
        acc = X[f, h, :, y] if h == 0 else X[f, h, z]
        for d in range(1, ys if h == 0 else zs):
            acc = acc + B1[f, h, d - 1]
        Y[f, h] = acc
        out = []
        for d in range(1, zs if h == 0 else ys):
            t = lax.rem(z + d, zs) if h == 0 else lax.rem(y + d, ys)
            out.append(send(Y.at[f, h, t], B2.at[f, h, d - 1], s2.at[f, h, d - 1], r2.at[f, h, d - 1],
                            (zpeer if h == 0 else ypeer)[d - 1]))
        return out

    def scatter_end(f, h, copies):
        for copy in copies:
            copy.wait_recv()
        acc = Y[f, h, z] if h == 0 else Y[f, h, y]
        for d in range(1, zs if h == 0 else ys):
            acc = acc + B2[f, h, d - 1]
        return acc

    one = {}
    two = {}
    for h in range(2):
        add_pair(0, h)
    pl.when(z == last)(late_end)
    forwards = [g_end(i) for i in range(3)]
    g_two(3)
    for h in range(2):
        one[0, h] = scatter_one(0, h)
    forwards.append(g_end(3))

    def diagonal(count, start):
        r = lax.broadcasted_iota(jnp.int32, (count, w), 0) + start
        c = lax.broadcasted_iota(jnp.int32, (count, w), 1) + o * w
        return r == c

    def product(left):
        lhi, llo = split_two(left)
        both = jnp.concatenate([lhi.astype(F32), llo.astype(F32)], axis=0).astype(BF16)
        big = jnp.dot(both, pan_hi[...], preferred_element_type=F32)
        return big[0:half_rows] + big[half_rows:rows] + jnp.dot(lhi, pan_lo[...], preferred_element_type=F32)

    def row_gather(g, h, value):
        urow[g, h, o] = value
        out = []
        for d in range(1, groups):
            out.append(send(urow.at[g, h, o], urow.at[g, h, o], su.at[g, h, d - 1], ru.at[g, h, d - 1], xpeer[d - 1]))
        return out

    def arrived(copies):
        for copy in copies:
            copy.wait_recv()

    step = total_rows // zs

    def turn_panel(k):
        block = jnp.where(diagonal(step, k * step), 1.5, 0.0) - 0.5 * cpan[k].reshape(step, w)
        hi, lo = split_two(block)
        span = pl.ds(k * step, step)
        pan_hi[span, :] = hi
        pan_lo[span, :] = lo

    for d in range(1, groups):
        remote(crow.at[0], crow.at[0], sx.at[0, d - 1], rx.at[0, d - 1], partner).wait_recv()
    for copy in forwards:
        copy.wait_recv()
    for k in range(zs):
        turn_panel(k)
    moved = {}
    for h in range(2):
        row = jnp.concatenate([crow[k, part[h]] for k in range(groups)], axis=1)
        moved[0, h] = row_gather(0, h, product(row))
    for h in range(2):
        arrived(moved[0, h])
        row = jnp.concatenate([urow[0, h, k] for k in range(groups)], axis=1)
        moved[1, h] = row_gather(1, h, product(row))
    for h in range(2):
        two[0, h] = scatter_two(0, h, one[0, h])
    for h in range(2):
        arrived(moved[1, h])
        row = jnp.concatenate([urow[1, h, k] for k in range(groups)], axis=1)
        right = product(row)
        turn = jnp.where(diagonal(half_rows, b * rows + h * half_rows), 1.5, 0.0) - 0.5 * corr_ref[part[h], :]
        inv_ref[part[h], :] = 1.5 * turn - 0.5 * right
    for h in range(2):
        fock_ref[part[h], :] = scatter_end(0, h, two[0, h])

    def sent(ref, sem):
        remote(ref, ref, sem, rl1.at[0], partner).wait_send()

    for i in range(3):
        e = ahead(i)

        @pl.when(e > 0)
        def _():
            sent(B1b.at[e - 1], s1b.at[e - 1])
            sent(B2a.at[e - 1], s2a.at[e - 1])

    @pl.when(z != last)
    def _():
        sent(YL, sl2.at[ahead(3) - 1])
        for d in range(1, ys):
            sent(B2b.at[d - 1], s2b.at[d - 1])

    for e in range(1, zs):
        sent(cpan.at[0, 0, core], ga_s.at[e - 1])
    for zp in range(zs):
        for d in range(1, ys):
            sent(cpan.at[0, 0, core], gb_s.at[zp, d - 1])
    for d in range(1, groups):
        sent(crow.at[0], sx.at[0, d - 1])
    for copy in started:
        copy.wait_send()
    for i in range(4):
        sends[i].wait_send()
    xf0.wait_send()
    xf1.wait_send()
    t1.wait_send()
    t2.wait_send()
    for k in range(2):
        h0[k].wait_send()
        h1[k].wait_send()
        h2[k].wait_send()
        h3[k].wait_send()


def whole(orbitals, potential, deriv_blocks, levels, box_counts, neighbours):
    slots, coefs, w = orbitals.shape
    n = deriv_blocks.shape[1]
    nn = n * n
    pad = -(-nn // 16) * 16
    boxes = lax.axis_size("box")
    groups = lax.axis_size("orb")
    zs = groups
    ys = boxes // 2 // zs
    fy = max(ys - 1, 1)
    total = groups * w
    rows = total // boxes
    half = rows // 2
    far = max(zs, ys) - 1
    vm = pl.BlockSpec(memory_space=pltpu.VMEM)
    sm = pl.BlockSpec(memory_space=pltpu.SMEM)
    column = -(-((n - 1) * nn + pad) // 128) * 128
    dma = pltpu.SemaphoreType.DMA
    out = jax.ShapeDtypeStruct((rows, w), F32)
    return pl.pallas_call(
        functools.partial(whole_kernel, n, pad, zs, ys),
        out_shape=(out, out, out),
        in_specs=[pl.BlockSpec(memory_space=pl.ANY), sm, sm, sm, vm, vm],
        out_specs=(vm, vm, vm),
        scratch_shapes=[
            pltpu.VMEM((slots, coefs, w), BF16),
            dma(()),
            pltpu.VMEM((3, slots, coefs, w), BF16),
            pltpu.VMEM((4, slots, coefs, w), BF16),
            pltpu.VMEM((n, 4, pad, w), BF16),
            pltpu.VMEM((n, 3, pad, w), BF16),
            pltpu.VMEM((n, 3, pad, w), BF16),
            pltpu.VMEM((n, 2, pad, w), F32),
            pltpu.VMEM((slots, coefs, 3 * w), BF16),
            pltpu.VMEM((4 * pad, 4 * pad), BF16),
            pltpu.VMEM((4 * pad, 3 * pad), BF16),
            pltpu.VMEM((4 * pad, 3 * pad), BF16),
            pltpu.VMEM((n * 64, n * 64), BF16),
            pltpu.VMEM((n * 64, n * 48), BF16),
            pltpu.VMEM((n * 64, n * 48), BF16),
            pltpu.VMEM((3, -(-slots * n // 8) * 8, 128), jnp.int32),
            pltpu.VMEM((8, column), F32),
            pltpu.VMEM((column, 8), F32),
            pltpu.VMEM((2, groups, total // groups // (2 * rows), 2, rows, w), F32),
            pltpu.VMEM((zs, ys, rows, w), F32),
            pltpu.VMEM((zs, ys, rows, w), F32),
            pltpu.VMEM((zs, fy, half, w), F32),
            pltpu.VMEM((zs - 1, ys, half, w), F32),
            pltpu.VMEM((zs, half, w), F32),
            pltpu.VMEM((ys, half, w), F32),
            pltpu.VMEM((zs - 1, half, w), F32),
            pltpu.VMEM((fy, half, w), F32),
            pltpu.VMEM((fy, rows, w), F32),
            pltpu.VMEM((rows, w), F32),
            pltpu.VMEM((zs - 1, rows, w), F32),
            pltpu.VMEM((1, 2, zs, ys, half, w), F32),
            pltpu.VMEM((1, 2, zs, ys, half, w), F32),
            pltpu.VMEM((1, 2, far, zs, half, w), F32),
            pltpu.VMEM((1, 2, zs, half, w), F32),
            pltpu.VMEM((1, 2, far, half, w), F32),
            pltpu.VMEM((zs, ys, 2, rows, w), F32),
            pltpu.VMEM((groups, rows, w), F32),
            pltpu.VMEM((2, 2, groups, half, w), F32),
            pltpu.VMEM((total, w), BF16),
            pltpu.VMEM((total, w), BF16),
            dma((6,)), dma((3, 2)), dma((8,)), dma((4, 2)), dma((2,)), dma((2,)),
            dma((zs,)), dma((zs,)),
            dma((zs, fy)), dma((zs, fy)), dma((zs - 1,)), dma((zs - 1,)),
            dma((zs - 1,)), dma((zs - 1,)), dma((fy,)), dma((fy,)),
            dma((zs - 1,)), dma((zs - 1,)), dma((zs, fy)), dma((zs, fy)), dma((zs,)), dma((zs,)),
            dma((fy,)), dma((fy,)), dma((zs - 1,)), dma((zs - 1,)),
            dma((1, 2)), dma((1, 2)),
            dma((1, 2, far)), dma((1, 2, far)),
            dma((1, 2, far)), dma((1, 2, far)),
            dma((1, groups - 1)), dma((1, groups - 1)),
            dma((2, 2, groups - 1)), dma((2, 2, groups - 1)),
        ],
        compiler_params=pltpu.CompilerParams(collective_id=0, has_side_effects=True, vmem_limit_bytes=63 << 20),
        name="whole",
    )(orbitals, jnp.transpose(neighbours, (0, 2, 1)), levels, box_counts, potential,
      jnp.transpose(deriv_blocks, (1, 0, 2)))


def settle_kernel(*refs):
    for src, dst in zip(refs[:3], refs[3:]):
        dst[...] = src[...]


def settle(arrays):
    vm = pl.BlockSpec(memory_space=pltpu.VMEM)
    return pl.pallas_call(
        settle_kernel,
        out_shape=tuple(jax.ShapeDtypeStruct(a.shape, a.dtype) for a in arrays),
        in_specs=[vm] * 3,
        out_specs=(vm,) * 3,
        name="settle",
    )(*arrays)


def body(orbitals, potential, deriv_blocks, levels, box_counts, neighbours):
    return settle(whole(orbitals, potential, deriv_blocks, levels, box_counts, neighbours))


def solution(mesh):
    in_specs = (
        P("box", None, "orb"),
        P("box", None),
        P(),
        P("box"),
        P("box"),
        P("box", None, None),
    )
    out_specs = (P("box", "orb"), P("box", "orb"), P("box", "orb"))
    return jax.shard_map(body, mesh=mesh, in_specs=in_specs, out_specs=out_specs, check_vma=False)
```

```python
import functools

import jax
import jax.numpy as jnp
from jax import lax
from jax.experimental import pallas as pl
from jax.experimental.pallas import tpu as pltpu
from jax.sharding import PartitionSpec as P

MESH = pl.DeviceIdType.MESH
HIGH = lax.Precision.HIGHEST
F32 = jnp.float32
BF16 = jnp.bfloat16


def quotient(x, n):
    return jnp.floor((x + 0.5) * (1.0 / n))


def rows_and_cols(shape):
    r = lax.broadcasted_iota(jnp.int32, shape, 0).astype(F32)
    c = lax.broadcasted_iota(jnp.int32, shape, 1).astype(F32)
    return r, c


def split_two(x):
    hi = x.astype(BF16)
    return hi, (x - hi.astype(F32)).astype(BF16)


def hdot(a, b):
    return jnp.dot(a, b, precision=HIGH, preferred_element_type=F32)


def whole_kernel(n, pad, zs, ys, a_hbm, nb_ref, lev_ref, cnt_ref, pot_ref, db_ref, fock_ref, corr_ref, inv_ref,
                 a_ref, in_sem, gath, halo, SA, SB, SC, Wsc, R, m12a, m12b, m12c, m0a, m0b, m0c, tbl, prow, pcol,
                 p_ref, abuf0, X0, B1a, B1b, Ya, Yb, B2a, B2b, BL1, YL, BL2, abuf, X, B1, Y, B2,
                 cpan, crow, urow, pan_hi, pan_lo,
                 xs_sem, xr_sem, hs_sem, hr_sem, ts_sem, tr_sem,
                 sa0, ra0, s1a, r1a, s1b, r1b, s2a, r2a, s2b, r2b, ga_s, ga_r, gb_s, gb_r, gf_s, gf_r,
                 sl1, rl1, sl2, rl2,
                 sa, ra, s1, r1, s2, r2, sx, rx, su, ru):
    b = lax.axis_index("box")
    o = lax.axis_index("orb")
    boxes = lax.axis_size("box")
    groups = lax.axis_size("orb")
    core = lax.rem(b, 2)
    chip = b // 2
    z = chip // ys
    y = lax.rem(chip, ys)
    sgn = 1 - 2 * core
    mate = b + sgn
    back1 = lax.rem(b - sgn + boxes, boxes)
    fwd2 = lax.rem(b + 2 * sgn + boxes, boxes)
    back2 = lax.rem(b - 2 * sgn + boxes, boxes)
    right = lax.rem(o + 1, groups)
    left = lax.rem(o + groups - 1, groups)
    nn = n * n
    w = a_ref.shape[2]
    rows = corr_ref.shape[0]
    half_rows = rows // 2
    total_rows = zs * ys * 2 * rows

    def at(zz, yy):
        return ((zz * ys + yy) * 2 + core, o)

    partner = (mate, o)
    zpeer = [at(lax.rem(z + d, zs), y) for d in range(1, zs)]
    ypeer = [at(z, lax.rem(y + d, ys)) for d in range(1, ys)]
    xpeer = [(b, lax.rem(o + d, groups)) for d in range(1, groups)]

    fetch = pltpu.make_async_copy(a_hbm, a_ref, in_sem)
    fetch.start()

    shape = tbl.shape[1:]
    r = lax.broadcasted_iota(jnp.int32, shape, 0)
    c = lax.broadcasted_iota(jnp.int32, shape, 1)
    own = jnp.zeros(shape, jnp.int32)
    for k in range(2):
        mine = (r >= k * n) & (r < (k + 1) * n)
        for a in range(3):
            own = jnp.where(mine & (c == a * 3), nb_ref[k, 0, a], own)
            own = jnp.where(mine & (c == a * 3 + 1), b * 2 + k, own)
            own = jnp.where(mine & (c == a * 3 + 2), nb_ref[k, 1, a], own)
        code = jnp.where(cnt_ref[0] > k, lev_ref[k], -1)
        own = jnp.where(mine & (c == 9), code, own)
    tbl[0] = own

    barrier = pltpu.get_barrier_semaphore()
    peers = [partner, (back1, o), (fwd2, o), (back2, o)] + xpeer + ypeer + zpeer
    for dev in peers:
        pl.semaphore_signal(barrier, inc=1, device_id=dev, device_id_type=MESH)
    pl.semaphore_wait(barrier, len(peers))

    def remote(src, dst, ssem, rsem, dev):
        return pltpu.make_async_remote_copy(src_ref=src, dst_ref=dst, send_sem=ssem, recv_sem=rsem,
                                            device_id=dev, device_id_type=MESH)

    sends = {}
    for i, (k, q, dev) in enumerate(((0, 0, (b, right)), (1, 1, (b, left)), (1, 0, (b, right)), (0, 1, (b, left)))):
        sends[i] = remote(a_hbm.at[k], gath.at[q, k], xs_sem.at[i], xr_sem.at[q, k], dev)
    xf0 = remote(gath.at[0, 0], gath.at[2, 0], xs_sem.at[4], xr_sem.at[2, 0], (b, right))
    xf1 = remote(gath.at[1, 1], gath.at[2, 1], xs_sem.at[5], xr_sem.at[2, 1], (b, left))
    h1 = [remote(a_hbm.at[k], halo.at[1, k], hs_sem.at[k], hr_sem.at[1, k], (back1, o)) for k in range(2)]
    h2 = [remote(a_hbm.at[k], halo.at[2, k], hs_sem.at[2 + k], hr_sem.at[2, k], (fwd2, o)) for k in range(2)]
    h0 = [remote(a_hbm.at[k], halo.at[0, k], hs_sem.at[4 + k], hr_sem.at[0, k], partner) for k in range(2)]
    h3 = [remote(halo.at[1, k], halo.at[3, k], hs_sem.at[6 + k], hr_sem.at[3, k], partner) for k in range(2)]
    t1 = remote(tbl.at[0], tbl.at[1], ts_sem.at[0], tr_sem.at[0], partner)
    t2 = remote(tbl.at[0], tbl.at[2], ts_sem.at[1], tr_sem.at[1], (back1, o))
    sends[0].start()
    sends[1].start()
    t2.start()
    h1[0].start()
    h2[0].start()
    t1.start()
    h0[0].start()
    h0[1].start()
    sends[2].start()
    sends[3].start()
    h1[1].start()
    h2[1].start()

    fetch.wait()

    alive = [jnp.where(cnt_ref[0] > k, 1.0, 0.0) for k in range(2)]
    for k in range(2):
        R[k, :, 0:w] = (a_ref[k].astype(F32) * alive[k]).astype(BF16)

    def correlate(block, place):
        total = jnp.zeros((w, w), F32)
        for k in range(2):
            total = total + lax.dot_general(block[k], R[k, :, 0:w], (((0,), (0,)), ((), ())),
                                            preferred_element_type=F32)
        p_ref[0, place] = total.reshape(ys, 2, rows, w)

    def fock_part(block, place):
        total = jnp.zeros((w, 2 * w), F32)
        for k in range(2):
            total = total + lax.dot_general(block[k], R[k, :, w:3 * w], (((0,), (0,)), ((), ())),
                                            preferred_element_type=F32)
        p_ref[1, place] = (total[:, 0:w] + total[:, w:2 * w]).reshape(ys, 2, rows, w)

    edge = nn // 16 * 16
    for S in (SA, SB, SC):
        S[:, :, edge:pad, :] = jnp.zeros((n, S.shape[1], pad - edge, w), BF16)

    def spread(block, S, q):
        for l in range(n):
            S[l, q, 0:nn, :] = block[l * nn:(l + 1) * nn, :]

    spread(a_ref.at[0], SA, 0)
    spread(a_ref.at[1], SA, 1)
    started = []

    def send(src, dst, ssem, rsem, dev):
        copy = pltpu.make_async_remote_copy(src_ref=src, dst_ref=dst, send_sem=ssem, recv_sem=rsem,
                                            device_id=dev, device_id_type=MESH)
        copy.start()
        started.append(copy)
        return copy

    part = [pl.ds(0, half_rows), pl.ds(half_rows, half_rows)]

    order_z = [o, left, right, lax.rem(o + 2, groups)]
    last = order_z[3]
    low, high = part
    pairs = {}
    one_a = {}

    def ahead(i):
        return lax.rem(order_z[i] - z + zs, zs)

    def behind(i):
        return lax.rem(z - order_z[i] + zs, zs)

    def pair_send(i):
        zp = order_z[i]
        pairs[i] = send(p_ref.at[0, zp, :, 1 - core], abuf0.at[zp], sa0.at[i], ra0.at[i], partner)

    def pair_add(i):
        zp = order_z[i]
        pairs[i].wait_recv()
        X0[zp] = p_ref[0, zp, :, core] + abuf0[zp]

    def c_one(i):
        zp = order_z[i]
        for d in range(1, ys):
            one_a[i, d] = send(X0.at[zp, lax.rem(y + d, ys), low], B1a.at[i, d - 1], s1a.at[i, d - 1],
                               r1a.at[i, d - 1], ypeer[d - 1])
        e = ahead(i)

        @pl.when(e > 0)
        def _():
            remote(X0.at[zp, :, high], B1b.at[e - 1], s1b.at[e - 1], r1b.at[e - 1], at(zp, y)).start()

    def c_two_a(i):
        zp = order_z[i]
        acc = X0[zp, y, low]
        for d in range(1, ys):
            one_a[i, d].wait_recv()
            acc = acc + B1a[i, d - 1]
        Ya[zp] = acc
        e = ahead(i)

        @pl.when(e > 0)
        def _():
            remote(Ya.at[zp], B2a.at[e - 1], s2a.at[e - 1], r2a.at[e - 1], at(zp, y)).start()

    def c_two_b():
        for e in range(1, zs):
            remote(B1b.at[e - 1], B1b.at[e - 1], s1b.at[e - 1], r1b.at[e - 1], partner).wait_recv()
        acc = X0[z, :, high]
        for e in range(1, zs):
            acc = acc + B1b[e - 1]
        Yb[...] = acc
        for d in range(1, ys):
            remote(Yb.at[lax.rem(y + d, ys)], B2b.at[d - 1], s2b.at[d - 1], r2b.at[d - 1], ypeer[d - 1]).start()

    def publish():
        spot = cpan.at[z, y, core]
        for e in range(1, zs):
            remote(spot, spot, ga_s.at[e - 1], ga_r.at[e - 1], zpeer[e - 1]).start()
        for d in range(1, ys):
            remote(spot, spot, gb_s.at[z, d - 1], gb_r.at[z, d - 1], ypeer[d - 1]).start()
        for d in range(1, groups):
            remote(spot, crow.at[o], sx.at[0, d - 1], rx.at[0, d - 1], xpeer[d - 1]).start()

    def c_end():
        piece = Ya[z]
        for e in range(1, zs):
            remote(B2a.at[e - 1], B2a.at[e - 1], s2a.at[e - 1], r2a.at[e - 1], partner).wait_recv()
            piece = piece + B2a[e - 1]
        corr_ref[low, :] = piece
        cpan[z, y, core, low] = piece
        crow[o, low] = piece
        piece = Yb[y]
        for d in range(1, ys):
            remote(B2b.at[d - 1], B2b.at[d - 1], s2b.at[d - 1], r2b.at[d - 1], partner).wait_recv()
            piece = piece + B2b[d - 1]
        corr_ref[high, :] = piece
        cpan[z, y, core, high] = piece
        crow[o, high] = piece
        publish()

    def g_two(i):
        zp = order_z[i]
        spot = cpan.at[zp, y, core]
        e = behind(i)

        @pl.when(e > 0)
        def _():
            remote(spot, spot, ga_s.at[e - 1], ga_r.at[e - 1], partner).wait_recv()
            for d in range(1, ys):
                remote(spot, spot, gb_s.at[zp, d - 1], gb_r.at[zp, d - 1], ypeer[d - 1]).start()

    def g_end(i):
        zp = order_z[i]
        spot = cpan.at[zp, y, core]
        for d in range(1, ys):
            remote(spot, spot, gb_s.at[zp, d - 1], gb_r.at[zp, d - 1], partner).wait_recv()
        column = cpan.at[zp, :, core]
        return send(column, column, gf_s.at[i], gf_r.at[i], partner)

    def late_one():
        out = []
        for d in range(1, ys):
            out.append(send(X0.at[last, lax.rem(y + d, ys)], BL1.at[d - 1], sl1.at[d - 1], rl1.at[d - 1], ypeer[d - 1]))
        return out

    def late_two(copies):
        acc = X0[last, y]
        for d, copy in enumerate(copies):
            copy.wait_recv()
            acc = acc + BL1[d]
        YL[...] = acc
        for e in range(1, zs):
            remote(YL, BL2.at[e - 1], sl2.at[e - 1], rl2.at[e - 1], zpeer[e - 1]).start()

    def late_end():
        piece = YL[...]
        for e in range(1, zs):
            remote(BL2.at[e - 1], BL2.at[e - 1], sl2.at[e - 1], rl2.at[e - 1], partner).wait_recv()
            piece = piece + BL2[e - 1]
        cpan[last, y, core] = piece
        spot = cpan.at[last, y, core]
        for d in range(1, ys):
            remote(spot, spot, gb_s.at[last, d - 1], gb_r.at[last, d - 1], ypeer[d - 1]).start()

        @pl.when(z == last)
        def _():
            corr_ref[...] = piece
            crow[o] = piece
            for d in range(1, groups):
                remote(spot, crow.at[o], sx.at[0, d - 1], rx.at[0, d - 1], xpeer[d - 1]).start()

    correlate(a_ref, o)
    pair_send(0)

    prow[...] = jnp.zeros(prow.shape, F32)
    prow[0:2, 0:n * nn] = pot_ref[...]
    pcol[...] = prow[...].T

    order = [(b, 0), (b, 1), (mate, 0), (mate, 1), (back1, 0), (back2, 0), (fwd2, 0), (back1, 1), (back2, 1),
             (fwd2, 1)]
    shape = (2 * n, 10 * n)
    ci = lax.broadcasted_iota(jnp.int32, shape, 1)
    gid = jnp.zeros(shape, jnp.int32)
    for q, (dev, k) in enumerate(order):
        gid = jnp.where((ci >= q * n) & (ci < (q + 1) * n), dev * 2 + k, gid)
    r, c = rows_and_cols((2 * n, n))
    pick_r = jnp.where(r - n * quotient(r, n) == c, 1.0, 0.0)
    r, c = rows_and_cols((n, 10 * n))
    pick_c = jnp.where(c - n * quotient(c, n) == r, 1.0, 0.0)
    bt = [hdot(hdot(pick_r, db_ref[:, u, :].astype(F32)), pick_c) for u in range(3)]
    t1.wait_recv()
    t2.wait_recv()
    M = [jnp.zeros(shape, F32) for _ in range(3)]
    for d in range(3):
        code = tbl[d, 0:2 * n, 9:10]
        factor = jnp.where(code < 0, 0.0, jnp.where(code == 0, 0.5, jnp.where(code == 1, 1.0, 2.0)))
        for a in range(3):
            t = jnp.zeros(shape, F32)
            for u in range(3):
                t = t + jnp.where(tbl[d, 0:2 * n, a * 3 + u:a * 3 + u + 1] == gid, bt[u], 0.0)
            t = t * factor
            M[a] = M[a] + 0.5 * lax.dot_general(t[:, 0:2 * n], t, (((0,), (0,)), ((), ())), precision=HIGH,
                                                preferred_element_type=F32)
    half = 2 * pad
    r, c = rows_and_cols((half, 2 * n))
    rs = quotient(r, pad)
    rq = r - rs * pad
    ri1 = quotient(rq, n)
    ri2 = rq - ri1 * n
    ok = rq < nn
    cs = quotient(c, n)
    ci = c - cs * n
    L1 = jnp.where(ok & (cs == rs) & (ci == ri1), 1.0, 0.0)
    L2 = jnp.where(ok & (cs == rs) & (ci == ri2), 1.0, 0.0)
    LM1 = hdot(L1, M[1])
    LM2 = hdot(L2, M[2])
    r, c = rows_and_cols((n * 32, 2 * n))
    ri = quotient(r, 32)
    rs = quotient(r, 16) - 2 * ri
    cs = quotient(c, n)
    L0 = jnp.where((cs == rs) & ((c - cs * n) == ri), 1.0, 0.0)
    LM0 = hdot(L0, M[0])

    def expand(m12, m0, base, count):
        wide = count * pad
        r, c = rows_and_cols((10 * n, wide))
        cs = quotient(c, pad)
        cq = c - cs * pad
        cl1 = quotient(cq, n)
        cl2 = cq - cl1 * n
        ok = cq < nn
        rs = quotient(r, n)
        ri = r - rs * n
        ok = ok & (cs + base == rs)
        C1 = jnp.where(ok & (ri == cl1), 1.0, 0.0)
        C2 = jnp.where(ok & (ri == cl2), 1.0, 0.0)
        r, c = rows_and_cols((half, wide))
        rq = r - quotient(r, pad) * pad
        cq = c - quotient(c, pad) * pad
        ri1 = quotient(rq, n)
        cl1 = quotient(cq, n)
        same1 = ri1 == cl1
        same2 = (rq - ri1 * n) == (cq - cl1 * n)
        full = jnp.where(same2, hdot(LM1, C1), 0.0) + jnp.where(same1, hdot(LM2, C2), 0.0)
        hi, lo = split_two(full)
        m12[0:half, :] = hi
        m12[half:2 * half, :] = lo
        step = count * 16
        r, c = rows_and_cols((10 * n, n * step))
        cl = quotient(c, step)
        cs = quotient(c - cl * step, 16)
        rs = quotient(r, n)
        C0 = jnp.where((rs == cs + base) & ((r - rs * n) == cl), 1.0, 0.0)
        r, c = rows_and_cols((n * 32, n * step))
        same = (r - 16 * quotient(r, 16)) == (c - 16 * quotient(c, 16))
        full = jnp.where(same, hdot(LM0, C0), 0.0)
        hi, lo = split_two(full)
        m0[0:n * 32, :] = hi
        m0[n * 32:n * 64, :] = lo

    def apply_inner(S, m12, fresh):
        count = S.shape[1]

        @pl.loop(0, n)
        def _(i):
            got = jnp.dot(m12[...], S[i].reshape(count * pad, w), preferred_element_type=F32)
            got = (got[0:half] + got[half:2 * half]).reshape(2, pad, w)
            Wsc[i] = got if fresh else Wsc[i] + got

    def apply_outer(S, m0):
        count = S.shape[1]

        @pl.loop(0, pad // 16)
        def _(i):
            rows = pl.ds(pl.multiple_of(i * 16, 16), 16)
            got = jnp.dot(m0[...], S[:, :, rows, :].reshape(n * count * 16, w), preferred_element_type=F32)
            Wsc[:, :, rows, :] = Wsc[:, :, rows, :] + (got[0:n * 32] + got[n * 32:n * 64]).reshape(n, 2, 16, w)

    expand(m12a, m0a, 0, 4)
    for k in range(2):
        h0[k].wait_recv()
        spread(halo.at[0, k], SA, 2 + k)
    apply_inner(SA, m12a, True)
    apply_outer(SA, m0a)
    expand(m12b, m0b, 4, 3)
    expand(m12c, m0c, 7, 3)

    sends[0].wait_recv()
    xf0.start()
    sends[1].wait_recv()
    xf1.start()
    h1[0].wait_recv()
    h3[0].start()
    spread(halo.at[1, 0], SB, 0)
    h2[0].wait_recv()
    spread(halo.at[2, 0], SB, 1)
    h3[0].wait_recv()
    spread(halo.at[3, 0], SB, 2)
    apply_inner(SB, m12b, False)
    apply_outer(SB, m0b)

    h1[1].wait_recv()
    h3[1].start()
    pair_add(0)
    c_one(0)
    sends[2].wait_recv()
    correlate(gath.at[0], left)
    pair_send(1)
    sends[3].wait_recv()
    correlate(gath.at[1], right)
    pair_send(2)
    pair_add(1)
    c_one(1)
    spread(halo.at[1, 1], SC, 0)
    h2[1].wait_recv()
    spread(halo.at[2, 1], SC, 1)
    h3[1].wait_recv()
    spread(halo.at[3, 1], SC, 2)
    pair_add(2)
    c_one(2)
    apply_inner(SC, m12c, False)
    apply_outer(SC, m0c)

    for k in range(2):
        for l in range(n):
            full = Wsc[l, k] + (pcol[l * nn:l * nn + pad, k:k + 1] * alive[k]) * SA[l, k].astype(F32)
            hi, lo = split_two(full)
            R[k, l * nn:(l + 1) * nn, w:2 * w] = hi[0:nn]
            R[k, l * nn:(l + 1) * nn, 2 * w:3 * w] = lo[0:nn]

    for i in range(3):
        c_two_a(i)
    pl.when(z != last)(c_two_b)
    fock_part(a_ref, o)
    fock_part(gath.at[0], left)
    pl.when(z != last)(c_end)
    xf0.wait_recv()
    xf1.wait_recv()
    correlate(gath.at[2], last)
    pair_send(3)
    fock_part(gath.at[1], right)
    pair_add(3)
    late = late_one()
    fock_part(gath.at[2], last)

    first = {}

    for h in range(2):
        first[0, h] = send(p_ref.at[1, :, :, 1 - core, part[h]], abuf.at[0, h], sa.at[0, h], ra.at[0, h], partner)
    for i in range(3):
        g_two(i)
    late_two(late)

    def add_pair(f, h):
        first[f, h].wait_recv()
        X[f, h] = p_ref[1, :, :, core, part[h]] + abuf[f, h]

    def scatter_one(f, h):
        out = []
        for d in range(1, ys if h == 0 else zs):
            if h == 0:
                t = lax.rem(y + d, ys)
                src = X.at[f, h, :, t]
            else:
                t = lax.rem(z + d, zs)
                src = X.at[f, h, t]
            out.append(send(src, B1.at[f, h, d - 1], s1.at[f, h, d - 1], r1.at[f, h, d - 1],
                            (ypeer if h == 0 else zpeer)[d - 1]))
        return out

    def scatter_two(f, h, copies):
        for copy in copies:
            copy.wait_recv()
        acc = X[f, h, :, y] if h == 0 else X[f, h, z]
        for d in range(1, ys if h == 0 else zs):
            acc = acc + B1[f, h, d - 1]
        Y[f, h] = acc
        out = []
        for d in range(1, zs if h == 0 else ys):
            t = lax.rem(z + d, zs) if h == 0 else lax.rem(y + d, ys)
            out.append(send(Y.at[f, h, t], B2.at[f, h, d - 1], s2.at[f, h, d - 1], r2.at[f, h, d - 1],
                            (zpeer if h == 0 else ypeer)[d - 1]))
        return out

    def scatter_end(f, h, copies):
        for copy in copies:
            copy.wait_recv()
        acc = Y[f, h, z] if h == 0 else Y[f, h, y]
        for d in range(1, zs if h == 0 else ys):
            acc = acc + B2[f, h, d - 1]
        return acc

    one = {}
    two = {}
    for h in range(2):
        add_pair(0, h)
    late_end()
    forwards = [g_end(i) for i in range(3)]
    for h in range(2):
        one[0, h] = scatter_one(0, h)
    forwards.append(g_end(3))

    def diagonal(count, start):
        r = lax.broadcasted_iota(jnp.int32, (count, w), 0) + start
        c = lax.broadcasted_iota(jnp.int32, (count, w), 1) + o * w
        return r == c

    def product(left):
        lhi, llo = split_two(left)
        both = jnp.concatenate([lhi.astype(F32), llo.astype(F32)], axis=0).astype(BF16)
        big = jnp.dot(both, pan_hi[...], preferred_element_type=F32)
        return big[0:half_rows] + big[half_rows:rows] + jnp.dot(lhi, pan_lo[...], preferred_element_type=F32)

    def row_gather(g, h, value):
        urow[g, h, o] = value
        out = []
        for d in range(1, groups):
            out.append(send(urow.at[g, h, o], urow.at[g, h, o], su.at[g, h, d - 1], ru.at[g, h, d - 1], xpeer[d - 1]))
        return out

    def arrived(copies):
        for copy in copies:
            copy.wait_recv()

    step = total_rows // zs

    def turn_panel(k):
        block = jnp.where(diagonal(step, k * step), 1.5, 0.0) - 0.5 * cpan[k].reshape(step, w)
        hi, lo = split_two(block)
        span = pl.ds(k * step, step)
        pan_hi[span, :] = hi
        pan_lo[span, :] = lo

    for d in range(1, groups):
        remote(crow.at[0], crow.at[0], sx.at[0, d - 1], rx.at[0, d - 1], partner).wait_recv()
    for copy in forwards:
        copy.wait_recv()
    for k in range(zs):
        turn_panel(k)
    moved = {}
    for h in range(2):
        row = jnp.concatenate([crow[k, part[h]] for k in range(groups)], axis=1)
        moved[0, h] = row_gather(0, h, product(row))
    for h in range(2):
        arrived(moved[0, h])
        row = jnp.concatenate([urow[0, h, k] for k in range(groups)], axis=1)
        moved[1, h] = row_gather(1, h, product(row))
    for h in range(2):
        two[0, h] = scatter_two(0, h, one[0, h])
    for h in range(2):
        arrived(moved[1, h])
        row = jnp.concatenate([urow[1, h, k] for k in range(groups)], axis=1)
        right = product(row)
        turn = jnp.where(diagonal(half_rows, b * rows + h * half_rows), 1.5, 0.0) - 0.5 * corr_ref[part[h], :]
        inv_ref[part[h], :] = 1.5 * turn - 0.5 * right
    for h in range(2):
        fock_ref[part[h], :] = scatter_end(0, h, two[0, h])

    def sent(ref, sem):
        remote(ref, ref, sem, rl1.at[0], partner).wait_send()

    for i in range(3):
        e = ahead(i)

        @pl.when(e > 0)
        def _():
            sent(B1b.at[e - 1], s1b.at[e - 1])
            sent(B2a.at[e - 1], s2a.at[e - 1])

    @pl.when(z != last)
    def _():
        for e in range(1, zs):
            sent(cpan.at[0, 0, core], ga_s.at[e - 1])
        for d in range(1, ys):
            sent(B2b.at[d - 1], s2b.at[d - 1])

    for e in range(1, zs):
        sent(YL, sl2.at[e - 1])
    for zp in range(zs):
        for d in range(1, ys):
            sent(cpan.at[0, 0, core], gb_s.at[zp, d - 1])
    for d in range(1, groups):
        sent(crow.at[0], sx.at[0, d - 1])
    for copy in started:
        copy.wait_send()
    for i in range(4):
        sends[i].wait_send()
    xf0.wait_send()
    xf1.wait_send()
    t1.wait_send()
    t2.wait_send()
    for k in range(2):
        h0[k].wait_send()
        h1[k].wait_send()
        h2[k].wait_send()
        h3[k].wait_send()


def whole(orbitals, potential, deriv_blocks, levels, box_counts, neighbours):
    slots, coefs, w = orbitals.shape
    n = deriv_blocks.shape[1]
    nn = n * n
    pad = -(-nn // 16) * 16
    boxes = lax.axis_size("box")
    groups = lax.axis_size("orb")
    zs = groups
    ys = boxes // 2 // zs
    fy = max(ys - 1, 1)
    total = groups * w
    rows = total // boxes
    half = rows // 2
    far = max(zs, ys) - 1
    vm = pl.BlockSpec(memory_space=pltpu.VMEM)
    sm = pl.BlockSpec(memory_space=pltpu.SMEM)
    column = -(-((n - 1) * nn + pad) // 128) * 128
    dma = pltpu.SemaphoreType.DMA
    out = jax.ShapeDtypeStruct((rows, w), F32)
    return pl.pallas_call(
        functools.partial(whole_kernel, n, pad, zs, ys),
        out_shape=(out, out, out),
        in_specs=[pl.BlockSpec(memory_space=pl.ANY), sm, sm, sm, vm, vm],
        out_specs=(vm, vm, vm),
        scratch_shapes=[
            pltpu.VMEM((slots, coefs, w), BF16),
            dma(()),
            pltpu.VMEM((3, slots, coefs, w), BF16),
            pltpu.VMEM((4, slots, coefs, w), BF16),
            pltpu.VMEM((n, 4, pad, w), BF16),
            pltpu.VMEM((n, 3, pad, w), BF16),
            pltpu.VMEM((n, 3, pad, w), BF16),
            pltpu.VMEM((n, 2, pad, w), F32),
            pltpu.VMEM((slots, coefs, 3 * w), BF16),
            pltpu.VMEM((4 * pad, 4 * pad), BF16),
            pltpu.VMEM((4 * pad, 3 * pad), BF16),
            pltpu.VMEM((4 * pad, 3 * pad), BF16),
            pltpu.VMEM((n * 64, n * 64), BF16),
            pltpu.VMEM((n * 64, n * 48), BF16),
            pltpu.VMEM((n * 64, n * 48), BF16),
            pltpu.VMEM((3, -(-slots * n // 8) * 8, 128), jnp.int32),
            pltpu.VMEM((8, column), F32),
            pltpu.VMEM((column, 8), F32),
            pltpu.VMEM((2, groups, total // groups // (2 * rows), 2, rows, w), F32),
            pltpu.VMEM((zs, ys, rows, w), F32),
            pltpu.VMEM((zs, ys, rows, w), F32),
            pltpu.VMEM((zs, fy, half, w), F32),
            pltpu.VMEM((zs - 1, ys, half, w), F32),
            pltpu.VMEM((zs, half, w), F32),
            pltpu.VMEM((ys, half, w), F32),
            pltpu.VMEM((zs - 1, half, w), F32),
            pltpu.VMEM((fy, half, w), F32),
            pltpu.VMEM((fy, rows, w), F32),
            pltpu.VMEM((rows, w), F32),
            pltpu.VMEM((zs - 1, rows, w), F32),
            pltpu.VMEM((1, 2, zs, ys, half, w), F32),
            pltpu.VMEM((1, 2, zs, ys, half, w), F32),
            pltpu.VMEM((1, 2, far, zs, half, w), F32),
            pltpu.VMEM((1, 2, zs, half, w), F32),
            pltpu.VMEM((1, 2, far, half, w), F32),
            pltpu.VMEM((zs, ys, 2, rows, w), F32),
            pltpu.VMEM((groups, rows, w), F32),
            pltpu.VMEM((2, 2, groups, half, w), F32),
            pltpu.VMEM((total, w), BF16),
            pltpu.VMEM((total, w), BF16),
            dma((6,)), dma((3, 2)), dma((8,)), dma((4, 2)), dma((2,)), dma((2,)),
            dma((zs,)), dma((zs,)),
            dma((zs, fy)), dma((zs, fy)), dma((zs - 1,)), dma((zs - 1,)),
            dma((zs - 1,)), dma((zs - 1,)), dma((fy,)), dma((fy,)),
            dma((zs - 1,)), dma((zs - 1,)), dma((zs, fy)), dma((zs, fy)), dma((zs,)), dma((zs,)),
            dma((fy,)), dma((fy,)), dma((zs - 1,)), dma((zs - 1,)),
            dma((1, 2)), dma((1, 2)),
            dma((1, 2, far)), dma((1, 2, far)),
            dma((1, 2, far)), dma((1, 2, far)),
            dma((1, groups - 1)), dma((1, groups - 1)),
            dma((2, 2, groups - 1)), dma((2, 2, groups - 1)),
        ],
        compiler_params=pltpu.CompilerParams(collective_id=0, has_side_effects=True, vmem_limit_bytes=63 << 20),
        name="whole",
    )(orbitals, jnp.transpose(neighbours, (0, 2, 1)), levels, box_counts, potential,
      jnp.transpose(deriv_blocks, (1, 0, 2)))


def settle_kernel(*refs):
    for src, dst in zip(refs[:3], refs[3:]):
        dst[...] = src[...]


def settle(arrays):
    vm = pl.BlockSpec(memory_space=pltpu.VMEM)
    return pl.pallas_call(
        settle_kernel,
        out_shape=tuple(jax.ShapeDtypeStruct(a.shape, a.dtype) for a in arrays),
        in_specs=[vm] * 3,
        out_specs=(vm,) * 3,
        name="settle",
    )(*arrays)


def body(orbitals, potential, deriv_blocks, levels, box_counts, neighbours):
    return settle(whole(orbitals, potential, deriv_blocks, levels, box_counts, neighbours))


def solution(mesh):
    in_specs = (
        P("box", None, "orb"),
        P("box", None),
        P(),
        P("box"),
        P("box"),
        P("box", None, None),
    )
    out_specs = (P("box", "orb"), P("box", "orb"), P("box", "orb"))
    return jax.shard_map(body, mesh=mesh, in_specs=in_specs, out_specs=out_specs, check_vma=False)
```

```python
import functools

import jax
import jax.numpy as jnp
from jax import lax
from jax.experimental import pallas as pl
from jax.experimental.pallas import tpu as pltpu
from jax.sharding import PartitionSpec as P

MESH = pl.DeviceIdType.MESH
HIGH = lax.Precision.HIGHEST
F32 = jnp.float32
BF16 = jnp.bfloat16


def quotient(x, n):
    return jnp.floor((x + 0.5) * (1.0 / n))


def rows_and_cols(shape):
    r = lax.broadcasted_iota(jnp.int32, shape, 0).astype(F32)
    c = lax.broadcasted_iota(jnp.int32, shape, 1).astype(F32)
    return r, c


def split_two(x):
    hi = x.astype(BF16)
    return hi, (x - hi.astype(F32)).astype(BF16)


def hdot(a, b):
    return jnp.dot(a, b, precision=HIGH, preferred_element_type=F32)


def whole_kernel(n, pad, zs, ys, a_hbm, nb_ref, lev_ref, cnt_ref, pot_hbm, db_hbm, fock_ref, corr_ref, inv_ref,
                 a_ref, pot_ref, db_ref, in_sem, gath, halo, SA, SB, SC, Wsc, R, m12a, m12b, m12c, m0a, m0b, m0c, tbl, prow, pcol,
                 p_ref, abuf0, X0, B1a, B1b, Ya, Yb, B2a, B2b, BL1, YL, BL2, abuf, X, B1, Y, B2,
                 cpan, crow, urow, pan_hi, pan_lo,
                 xs_sem, xr_sem, hs_sem, hr_sem, ts_sem, tr_sem,
                 sa0, ra0, s1a, r1a, s1b, r1b, s2a, r2a, s2b, r2b, ga_s, ga_r, gb_s, gb_r, gf_s, gf_r, gl_s, gl_r,
                 sl1, rl1, sl2, rl2,
                 sa, ra, s1, r1, s2, r2, sx, rx, su, ru):
    b = lax.axis_index("box")
    o = lax.axis_index("orb")
    boxes = lax.axis_size("box")
    groups = lax.axis_size("orb")
    core = lax.rem(b, 2)
    chip = b // 2
    z = chip // ys
    y = lax.rem(chip, ys)
    sgn = 1 - 2 * core
    mate = b + sgn
    back1 = lax.rem(b - sgn + boxes, boxes)
    fwd2 = lax.rem(b + 2 * sgn + boxes, boxes)
    back2 = lax.rem(b - 2 * sgn + boxes, boxes)
    right = lax.rem(o + 1, groups)
    left = lax.rem(o + groups - 1, groups)
    nn = n * n
    w = a_ref.shape[2]
    rows = corr_ref.shape[0]
    half_rows = rows // 2
    total_rows = zs * ys * 2 * rows

    def at(zz, yy):
        return ((zz * ys + yy) * 2 + core, o)

    partner = (mate, o)
    zpeer = [at(lax.rem(z + d, zs), y) for d in range(1, zs)]
    ypeer = [at(z, lax.rem(y + d, ys)) for d in range(1, ys)]
    xpeer = [(b, lax.rem(o + d, groups)) for d in range(1, groups)]

    barrier = pltpu.get_barrier_semaphore()
    peers = [partner, (back1, o), (fwd2, o), (back2, o)] + xpeer + ypeer + zpeer
    for dev in peers:
        pl.semaphore_signal(barrier, inc=1, device_id=dev, device_id_type=MESH)

    fetches = [pltpu.make_async_copy(src, dst, in_sem.at[i]) for i, (src, dst) in
               enumerate(((a_hbm, a_ref), (pot_hbm, pot_ref), (db_hbm, db_ref)))]
    for fetch in fetches:
        fetch.start()

    shape = tbl.shape[1:]
    r = lax.broadcasted_iota(jnp.int32, shape, 0)
    c = lax.broadcasted_iota(jnp.int32, shape, 1)
    own = jnp.zeros(shape, jnp.int32)
    for k in range(2):
        mine = (r >= k * n) & (r < (k + 1) * n)
        for a in range(3):
            own = jnp.where(mine & (c == a * 3), nb_ref[k, 0, a], own)
            own = jnp.where(mine & (c == a * 3 + 1), b * 2 + k, own)
            own = jnp.where(mine & (c == a * 3 + 2), nb_ref[k, 1, a], own)
        code = jnp.where(cnt_ref[0] > k, lev_ref[k], -1)
        own = jnp.where(mine & (c == 9), code, own)
    tbl[0] = own

    pl.semaphore_wait(barrier, len(peers))

    def remote(src, dst, ssem, rsem, dev):
        return pltpu.make_async_remote_copy(src_ref=src, dst_ref=dst, send_sem=ssem, recv_sem=rsem,
                                            device_id=dev, device_id_type=MESH)

    sends = {}
    for i, (k, q, dev) in enumerate(((0, 0, (b, right)), (1, 1, (b, left)), (1, 0, (b, right)), (0, 1, (b, left)))):
        sends[i] = remote(a_hbm.at[k], gath.at[q, k], xs_sem.at[i], xr_sem.at[q, k], dev)
    xf0 = remote(gath.at[0, 0], gath.at[2, 0], xs_sem.at[4], xr_sem.at[2, 0], (b, right))
    xf1 = remote(gath.at[1, 1], gath.at[2, 1], xs_sem.at[5], xr_sem.at[2, 1], (b, left))
    h1 = [remote(a_hbm.at[k], halo.at[1, k], hs_sem.at[k], hr_sem.at[1, k], (back1, o)) for k in range(2)]
    h2 = [remote(a_hbm.at[k], halo.at[2, k], hs_sem.at[2 + k], hr_sem.at[2, k], (fwd2, o)) for k in range(2)]
    h0 = [remote(a_hbm.at[k], halo.at[0, k], hs_sem.at[4 + k], hr_sem.at[0, k], partner) for k in range(2)]
    h3 = [remote(halo.at[1, k], halo.at[3, k], hs_sem.at[6 + k], hr_sem.at[3, k], partner) for k in range(2)]
    t1 = remote(tbl.at[0], tbl.at[1], ts_sem.at[0], tr_sem.at[0], partner)
    t2 = remote(tbl.at[0], tbl.at[2], ts_sem.at[1], tr_sem.at[1], (back1, o))
    sends[0].start()
    sends[1].start()
    t2.start()
    h1[0].start()
    h2[0].start()
    t1.start()
    h0[0].start()
    h0[1].start()
    sends[2].start()
    sends[3].start()
    h1[1].start()
    h2[1].start()

    for fetch in fetches:
        fetch.wait()

    alive = [jnp.where(cnt_ref[0] > k, 1.0, 0.0) for k in range(2)]
    for k in range(2):
        R[k, :, 0:w] = (a_ref[k].astype(F32) * alive[k]).astype(BF16)

    def correlate(block, place):
        total = jnp.zeros((w, w), F32)
        for k in range(2):
            total = total + lax.dot_general(block[k], R[k, :, 0:w], (((0,), (0,)), ((), ())),
                                            preferred_element_type=F32)
        p_ref[0, place] = total.reshape(ys, 2, rows, w)

    def fock_part(block, place):
        total = jnp.zeros((w, 2 * w), F32)
        for k in range(2):
            total = total + lax.dot_general(block[k], R[k, :, w:3 * w], (((0,), (0,)), ((), ())),
                                            preferred_element_type=F32)
        p_ref[1, place] = (total[:, 0:w] + total[:, w:2 * w]).reshape(ys, 2, rows, w)

    edge = nn // 16 * 16
    for S in (SA, SB, SC):
        S[:, :, edge:pad, :] = jnp.zeros((n, S.shape[1], pad - edge, w), BF16)

    def spread(block, S, q):
        for l in range(n):
            S[l, q, 0:nn, :] = block[l * nn:(l + 1) * nn, :]

    spread(a_ref.at[0], SA, 0)
    spread(a_ref.at[1], SA, 1)
    started = []

    def send(src, dst, ssem, rsem, dev):
        copy = pltpu.make_async_remote_copy(src_ref=src, dst_ref=dst, send_sem=ssem, recv_sem=rsem,
                                            device_id=dev, device_id_type=MESH)
        copy.start()
        started.append(copy)
        return copy

    part = [pl.ds(0, half_rows), pl.ds(half_rows, half_rows)]

    order_z = [o, left, right, lax.rem(o + 2, groups)]
    last = order_z[3]
    low, high = part
    pairs = {}
    one_a = {}

    def ahead(i):
        return lax.rem(order_z[i] - z + zs, zs)

    def behind(i):
        return lax.rem(z - order_z[i] + zs, zs)

    def pair_send(i):
        zp = order_z[i]
        pairs[i] = send(p_ref.at[0, zp, :, 1 - core], abuf0.at[zp], sa0.at[i], ra0.at[i], partner)

    def pair_add(i):
        zp = order_z[i]
        pairs[i].wait_recv()
        X0[zp] = p_ref[0, zp, :, core] + abuf0[zp]

    def c_one(i):
        zp = order_z[i]
        for d in range(1, ys):
            one_a[i, d] = send(X0.at[zp, lax.rem(y + d, ys), low], B1a.at[i, d - 1], s1a.at[i, d - 1],
                               r1a.at[i, d - 1], ypeer[d - 1])
        e = ahead(i)

        @pl.when(e > 0)
        def _():
            remote(X0.at[zp, :, high], B1b.at[e - 1], s1b.at[e - 1], r1b.at[e - 1], at(zp, y)).start()

    def c_two_a(i):
        zp = order_z[i]
        acc = X0[zp, y, low]
        for d in range(1, ys):
            one_a[i, d].wait_recv()
            acc = acc + B1a[i, d - 1]
        Ya[zp] = acc
        e = ahead(i)

        @pl.when(e > 0)
        def _():
            remote(Ya.at[zp], B2a.at[e - 1], s2a.at[e - 1], r2a.at[e - 1], at(zp, y)).start()

    def c_two_b():
        for e in range(1, zs):
            remote(B1b.at[e - 1], B1b.at[e - 1], s1b.at[e - 1], r1b.at[e - 1], partner).wait_recv()
        acc = X0[z, :, high]
        for e in range(1, zs):
            acc = acc + B1b[e - 1]
        Yb[...] = acc
        for d in range(1, ys):
            remote(Yb.at[lax.rem(y + d, ys)], B2b.at[d - 1], s2b.at[d - 1], r2b.at[d - 1], ypeer[d - 1]).start()

    def publish():
        spot = cpan.at[z, y, core]
        for e in range(1, zs):
            remote(spot, spot, ga_s.at[e - 1], ga_r.at[e - 1], zpeer[e - 1]).start()
        for d in range(1, ys):
            remote(spot, spot, gb_s.at[z, d - 1], gb_r.at[z, d - 1], ypeer[d - 1]).start()
        for d in range(1, groups):
            remote(spot, crow.at[o], sx.at[0, d - 1], rx.at[0, d - 1], xpeer[d - 1]).start()

    def c_end():
        piece = Ya[z]
        for e in range(1, zs):
            remote(B2a.at[e - 1], B2a.at[e - 1], s2a.at[e - 1], r2a.at[e - 1], partner).wait_recv()
            piece = piece + B2a[e - 1]
        corr_ref[low, :] = piece
        cpan[z, y, core, low] = piece
        crow[o, low] = piece
        piece = Yb[y]
        for d in range(1, ys):
            remote(B2b.at[d - 1], B2b.at[d - 1], s2b.at[d - 1], r2b.at[d - 1], partner).wait_recv()
            piece = piece + B2b[d - 1]
        corr_ref[high, :] = piece
        cpan[z, y, core, high] = piece
        crow[o, high] = piece
        publish()

    def g_two(i):
        zp = order_z[i]
        spot = cpan.at[zp, y, core]
        e = behind(i)

        @pl.when(e > 0)
        def _():
            remote(spot, spot, ga_s.at[e - 1], ga_r.at[e - 1], partner).wait_recv()
            for d in range(1, ys):
                remote(spot, spot, gb_s.at[zp, d - 1], gb_r.at[zp, d - 1], ypeer[d - 1]).start()

    def g_end(i):
        zp = order_z[i]
        spot = cpan.at[zp, y, core]
        for d in range(1, ys):
            remote(spot, spot, gb_s.at[zp, d - 1], gb_r.at[zp, d - 1], partner).wait_recv()
        column = cpan.at[zp, :, core]
        return send(column, column, gf_s.at[i], gf_r.at[i], partner)

    def late_one():
        out = []
        for d in range(1, ys):
            out.append(send(X0.at[last, lax.rem(y + d, ys)], BL1.at[d - 1], sl1.at[d - 1], rl1.at[d - 1], ypeer[d - 1]))
        return out

    def late_two(copies):
        acc = X0[last, y]
        for d, copy in enumerate(copies):
            copy.wait_recv()
            acc = acc + BL1[d]
        YL[...] = acc
        for e in range(1, zs):
            remote(YL, BL2.at[e - 1], sl2.at[e - 1], rl2.at[e - 1], zpeer[e - 1]).start()

    def late_end():
        piece = YL[...]
        for e in range(1, zs):
            remote(BL2.at[e - 1], BL2.at[e - 1], sl2.at[e - 1], rl2.at[e - 1], partner).wait_recv()
            piece = piece + BL2[e - 1]
        cpan[last, y, core] = piece
        spot = cpan.at[last, y, core]
        for d in range(1, ys):
            remote(spot, spot, gb_s.at[last, d - 1], gb_r.at[last, d - 1], ypeer[d - 1]).start()
        forwards.append(send(spot, spot, gl_s.at[0], gl_r.at[0], partner))

        @pl.when(z == last)
        def _():
            corr_ref[...] = piece
            crow[o] = piece
            for d in range(1, groups):
                remote(spot, crow.at[o], sx.at[0, d - 1], rx.at[0, d - 1], xpeer[d - 1]).start()

    def late_forward():
        for d in range(1, ys):
            spot = cpan.at[last, lax.rem(y - d + ys, ys), core]
            remote(spot, spot, gb_s.at[last, d - 1], gb_r.at[last, d - 1], partner).wait_recv()
            forwards.append(send(spot, spot, gl_s.at[d], gl_r.at[d], partner))

    correlate(a_ref, o)
    pair_send(0)

    prow[...] = jnp.zeros(prow.shape, F32)
    prow[0:2, 0:n * nn] = pot_ref[...]
    pcol[...] = prow[...].T

    order = [(b, 0), (b, 1), (mate, 0), (mate, 1), (back1, 0), (back2, 0), (fwd2, 0), (back1, 1), (back2, 1),
             (fwd2, 1)]
    shape = (2 * n, 10 * n)
    ci = lax.broadcasted_iota(jnp.int32, shape, 1)
    gid = jnp.zeros(shape, jnp.int32)
    for q, (dev, k) in enumerate(order):
        gid = jnp.where((ci >= q * n) & (ci < (q + 1) * n), dev * 2 + k, gid)
    r, c = rows_and_cols((2 * n, n))
    pick_r = jnp.where(r - n * quotient(r, n) == c, 1.0, 0.0)
    r, c = rows_and_cols((n, 10 * n))
    pick_c = jnp.where(c - n * quotient(c, n) == r, 1.0, 0.0)
    bt = [hdot(hdot(pick_r, db_ref[:, u, :].astype(F32)), pick_c) for u in range(3)]
    t1.wait_recv()
    t2.wait_recv()
    M = [jnp.zeros(shape, F32) for _ in range(3)]
    for d in range(3):
        code = tbl[d, 0:2 * n, 9:10]
        factor = jnp.where(code < 0, 0.0, jnp.where(code == 0, 0.5, jnp.where(code == 1, 1.0, 2.0)))
        for a in range(3):
            t = jnp.zeros(shape, F32)
            for u in range(3):
                t = t + jnp.where(tbl[d, 0:2 * n, a * 3 + u:a * 3 + u + 1] == gid, bt[u], 0.0)
            t = t * factor
            M[a] = M[a] + 0.5 * lax.dot_general(t[:, 0:2 * n], t, (((0,), (0,)), ((), ())), precision=HIGH,
                                                preferred_element_type=F32)
    half = 2 * pad
    r, c = rows_and_cols((half, 2 * n))
    rs = quotient(r, pad)
    rq = r - rs * pad
    ri1 = quotient(rq, n)
    ri2 = rq - ri1 * n
    ok = rq < nn
    cs = quotient(c, n)
    ci = c - cs * n
    L1 = jnp.where(ok & (cs == rs) & (ci == ri1), 1.0, 0.0)
    L2 = jnp.where(ok & (cs == rs) & (ci == ri2), 1.0, 0.0)
    LM1 = hdot(L1, M[1])
    LM2 = hdot(L2, M[2])
    r, c = rows_and_cols((n * 32, 2 * n))
    ri = quotient(r, 32)
    rs = quotient(r, 16) - 2 * ri
    cs = quotient(c, n)
    L0 = jnp.where((cs == rs) & ((c - cs * n) == ri), 1.0, 0.0)
    LM0 = hdot(L0, M[0])

    def expand(m12, m0, base, count):
        wide = count * pad
        r, c = rows_and_cols((10 * n, wide))
        cs = quotient(c, pad)
        cq = c - cs * pad
        cl1 = quotient(cq, n)
        cl2 = cq - cl1 * n
        ok = cq < nn
        rs = quotient(r, n)
        ri = r - rs * n
        ok = ok & (cs + base == rs)
        C1 = jnp.where(ok & (ri == cl1), 1.0, 0.0)
        C2 = jnp.where(ok & (ri == cl2), 1.0, 0.0)
        r, c = rows_and_cols((half, wide))
        rq = r - quotient(r, pad) * pad
        cq = c - quotient(c, pad) * pad
        ri1 = quotient(rq, n)
        cl1 = quotient(cq, n)
        same1 = ri1 == cl1
        same2 = (rq - ri1 * n) == (cq - cl1 * n)
        full = jnp.where(same2, hdot(LM1, C1), 0.0) + jnp.where(same1, hdot(LM2, C2), 0.0)
        hi, lo = split_two(full)
        m12[0:half, :] = hi
        m12[half:2 * half, :] = lo
        step = count * 16
        r, c = rows_and_cols((10 * n, n * step))
        cl = quotient(c, step)
        cs = quotient(c - cl * step, 16)
        rs = quotient(r, n)
        C0 = jnp.where((rs == cs + base) & ((r - rs * n) == cl), 1.0, 0.0)
        r, c = rows_and_cols((n * 32, n * step))
        same = (r - 16 * quotient(r, 16)) == (c - 16 * quotient(c, 16))
        full = jnp.where(same, hdot(LM0, C0), 0.0)
        hi, lo = split_two(full)
        m0[0:n * 32, :] = hi
        m0[n * 32:n * 64, :] = lo

    def apply_inner(S, m12, fresh):
        count = S.shape[1]

        @pl.loop(0, n)
        def _(i):
            got = jnp.dot(m12[...], S[i].reshape(count * pad, w), preferred_element_type=F32)
            got = (got[0:half] + got[half:2 * half]).reshape(2, pad, w)
            Wsc[i] = got if fresh else Wsc[i] + got

    def apply_outer(S, m0):
        count = S.shape[1]

        @pl.loop(0, pad // 16)
        def _(i):
            rows = pl.ds(pl.multiple_of(i * 16, 16), 16)
            got = jnp.dot(m0[...], S[:, :, rows, :].reshape(n * count * 16, w), preferred_element_type=F32)
            Wsc[:, :, rows, :] = Wsc[:, :, rows, :] + (got[0:n * 32] + got[n * 32:n * 64]).reshape(n, 2, 16, w)

    expand(m12a, m0a, 0, 4)
    for k in range(2):
        h0[k].wait_recv()
        spread(halo.at[0, k], SA, 2 + k)
    apply_inner(SA, m12a, True)
    apply_outer(SA, m0a)
    expand(m12b, m0b, 4, 3)
    expand(m12c, m0c, 7, 3)

    sends[0].wait_recv()
    xf0.start()
    sends[1].wait_recv()
    xf1.start()
    h1[0].wait_recv()
    h3[0].start()
    spread(halo.at[1, 0], SB, 0)
    h2[0].wait_recv()
    spread(halo.at[2, 0], SB, 1)
    h3[0].wait_recv()
    spread(halo.at[3, 0], SB, 2)
    apply_inner(SB, m12b, False)
    apply_outer(SB, m0b)

    h1[1].wait_recv()
    h3[1].start()
    pair_add(0)
    c_one(0)
    sends[2].wait_recv()
    correlate(gath.at[0], left)
    pair_send(1)
    sends[3].wait_recv()
    correlate(gath.at[1], right)
    pair_send(2)
    pair_add(1)
    c_one(1)
    spread(halo.at[1, 1], SC, 0)
    h2[1].wait_recv()
    spread(halo.at[2, 1], SC, 1)
    h3[1].wait_recv()
    spread(halo.at[3, 1], SC, 2)
    pair_add(2)
    c_one(2)
    apply_inner(SC, m12c, False)
    apply_outer(SC, m0c)

    for k in range(2):
        for l in range(n):
            full = Wsc[l, k] + (pcol[l * nn:l * nn + pad, k:k + 1] * alive[k]) * SA[l, k].astype(F32)
            hi, lo = split_two(full)
            R[k, l * nn:(l + 1) * nn, w:2 * w] = hi[0:nn]
            R[k, l * nn:(l + 1) * nn, 2 * w:3 * w] = lo[0:nn]

    for i in range(3):
        c_two_a(i)
    pl.when(z != last)(c_two_b)
    fock_part(a_ref, o)
    fock_part(gath.at[0], left)
    xf0.wait_recv()
    xf1.wait_recv()
    correlate(gath.at[2], last)
    pair_send(3)
    pl.when(z != last)(c_end)
    pair_add(3)
    late = late_one()
    fock_part(gath.at[1], right)
    fock_part(gath.at[2], last)

    first = {}

    for h in range(2):
        first[0, h] = send(p_ref.at[1, :, :, 1 - core, part[h]], abuf.at[0, h], sa.at[0, h], ra.at[0, h], partner)
    for i in range(3):
        g_two(i)
    late_two(late)

    def add_pair(f, h):
        first[f, h].wait_recv()
        X[f, h] = p_ref[1, :, :, core, part[h]] + abuf[f, h]

    def scatter_one(f, h):
        out = []
        for d in range(1, ys if h == 0 else zs):
            if h == 0:
                t = lax.rem(y + d, ys)
                src = X.at[f, h, :, t]
            else:
                t = lax.rem(z + d, zs)
                src = X.at[f, h, t]
            out.append(send(src, B1.at[f, h, d - 1], s1.at[f, h, d - 1], r1.at[f, h, d - 1],
                            (ypeer if h == 0 else zpeer)[d - 1]))
        return out

    def scatter_two(f, h, copies):
        for copy in copies:
            copy.wait_recv()
        acc = X[f, h, :, y] if h == 0 else X[f, h, z]
        for d in range(1, ys if h == 0 else zs):
            acc = acc + B1[f, h, d - 1]
        Y[f, h] = acc
        out = []
        for d in range(1, zs if h == 0 else ys):
            t = lax.rem(z + d, zs) if h == 0 else lax.rem(y + d, ys)
            out.append(send(Y.at[f, h, t], B2.at[f, h, d - 1], s2.at[f, h, d - 1], r2.at[f, h, d - 1],
                            (zpeer if h == 0 else ypeer)[d - 1]))
        return out

    def scatter_end(f, h, copies):
        for copy in copies:
            copy.wait_recv()
        acc = Y[f, h, z] if h == 0 else Y[f, h, y]
        for d in range(1, zs if h == 0 else ys):
            acc = acc + B2[f, h, d - 1]
        return acc

    one = {}
    two = {}
    for h in range(2):
        add_pair(0, h)
    forwards = []
    late_end()
    early = [g_end(i) for i in range(3)]
    for h in range(2):
        one[0, h] = scatter_one(0, h)

    def diagonal(count, start):
        r = lax.broadcasted_iota(jnp.int32, (count, w), 0) + start
        c = lax.broadcasted_iota(jnp.int32, (count, w), 1) + o * w
        return r == c

    def product(left):
        lhi, llo = split_two(left)
        both = jnp.concatenate([lhi.astype(F32), llo.astype(F32)], axis=0).astype(BF16)
        big = jnp.dot(both, pan_hi[...], preferred_element_type=F32)
        return big[0:half_rows] + big[half_rows:rows] + jnp.dot(lhi, pan_lo[...], preferred_element_type=F32)

    def row_gather(g, h, value):
        urow[g, h, o] = value
        out = []
        for d in range(1, groups):
            out.append(send(urow.at[g, h, o], urow.at[g, h, o], su.at[g, h, d - 1], ru.at[g, h, d - 1], xpeer[d - 1]))
        return out

    def arrived(copies):
        for copy in copies:
            copy.wait_recv()

    step = total_rows // zs

    def turn_panel(zp):
        first_row = pl.multiple_of(zp * step, 128)
        block = jnp.where(diagonal(step, first_row), 1.5, 0.0) - 0.5 * cpan[zp].reshape(step, w)
        hi, lo = split_two(block)
        span = pl.ds(first_row, step)
        pan_hi[span, :] = hi
        pan_lo[span, :] = lo

    for i in range(3):
        early[i].wait_recv()
        turn_panel(order_z[i])
    late_forward()
    for d in range(1, groups):
        remote(crow.at[0], crow.at[0], sx.at[0, d - 1], rx.at[0, d - 1], partner).wait_recv()
    for copy in forwards:
        copy.wait_recv()
    turn_panel(last)
    moved = {}
    for h in range(2):
        row = jnp.concatenate([crow[k, part[h]] for k in range(groups)], axis=1)
        moved[0, h] = row_gather(0, h, product(row))
    for h in range(2):
        arrived(moved[0, h])
        row = jnp.concatenate([urow[0, h, k] for k in range(groups)], axis=1)
        moved[1, h] = row_gather(1, h, product(row))
    for h in range(2):
        two[0, h] = scatter_two(0, h, one[0, h])
    for h in range(2):
        arrived(moved[1, h])
        row = jnp.concatenate([urow[1, h, k] for k in range(groups)], axis=1)
        right = product(row)
        turn = jnp.where(diagonal(half_rows, b * rows + h * half_rows), 1.5, 0.0) - 0.5 * corr_ref[part[h], :]
        inv_ref[part[h], :] = 1.5 * turn - 0.5 * right
    for h in range(2):
        fock_ref[part[h], :] = scatter_end(0, h, two[0, h])

    def sent(ref, sem):
        remote(ref, ref, sem, rl1.at[0], partner).wait_send()

    for i in range(3):
        e = ahead(i)

        @pl.when(e > 0)
        def _():
            sent(B1b.at[e - 1], s1b.at[e - 1])
            sent(B2a.at[e - 1], s2a.at[e - 1])

    @pl.when(z != last)
    def _():
        for e in range(1, zs):
            sent(cpan.at[0, 0, core], ga_s.at[e - 1])
        for d in range(1, ys):
            sent(B2b.at[d - 1], s2b.at[d - 1])

    for e in range(1, zs):
        sent(YL, sl2.at[e - 1])
    for zp in range(zs):
        for d in range(1, ys):
            sent(cpan.at[0, 0, core], gb_s.at[zp, d - 1])
    for d in range(1, groups):
        sent(crow.at[0], sx.at[0, d - 1])
    for copy in started:
        copy.wait_send()
    for i in range(4):
        sends[i].wait_send()
    xf0.wait_send()
    xf1.wait_send()
    t1.wait_send()
    t2.wait_send()
    for k in range(2):
        h0[k].wait_send()
        h1[k].wait_send()
        h2[k].wait_send()
        h3[k].wait_send()


def whole(orbitals, potential, deriv_blocks, levels, box_counts, neighbours):
    slots, coefs, w = orbitals.shape
    n = deriv_blocks.shape[1]
    nn = n * n
    pad = -(-nn // 16) * 16
    boxes = lax.axis_size("box")
    groups = lax.axis_size("orb")
    zs = groups
    ys = boxes // 2 // zs
    fy = max(ys - 1, 1)
    total = groups * w
    rows = total // boxes
    half = rows // 2
    far = max(zs, ys) - 1
    vm = pl.BlockSpec(memory_space=pltpu.VMEM)
    sm = pl.BlockSpec(memory_space=pltpu.SMEM)
    hbm = pl.BlockSpec(memory_space=pl.ANY)
    column = -(-((n - 1) * nn + pad) // 128) * 128
    dma = pltpu.SemaphoreType.DMA
    out = jax.ShapeDtypeStruct((rows, w), F32)
    return pl.pallas_call(
        functools.partial(whole_kernel, n, pad, zs, ys),
        out_shape=(out, out, out),
        in_specs=[hbm, sm, sm, sm, hbm, hbm],
        out_specs=(vm, vm, vm),
        scratch_shapes=[
            pltpu.VMEM((slots, coefs, w), BF16),
            pltpu.VMEM((slots, coefs), F32),
            pltpu.VMEM((n, 3, n), BF16),
            dma((3,)),
            pltpu.VMEM((3, slots, coefs, w), BF16),
            pltpu.VMEM((4, slots, coefs, w), BF16),
            pltpu.VMEM((n, 4, pad, w), BF16),
            pltpu.VMEM((n, 3, pad, w), BF16),
            pltpu.VMEM((n, 3, pad, w), BF16),
            pltpu.VMEM((n, 2, pad, w), F32),
            pltpu.VMEM((slots, coefs, 3 * w), BF16),
            pltpu.VMEM((4 * pad, 4 * pad), BF16),
            pltpu.VMEM((4 * pad, 3 * pad), BF16),
            pltpu.VMEM((4 * pad, 3 * pad), BF16),
            pltpu.VMEM((n * 64, n * 64), BF16),
            pltpu.VMEM((n * 64, n * 48), BF16),
            pltpu.VMEM((n * 64, n * 48), BF16),
            pltpu.VMEM((3, -(-slots * n // 8) * 8, 128), jnp.int32),
            pltpu.VMEM((8, column), F32),
            pltpu.VMEM((column, 8), F32),
            pltpu.VMEM((2, groups, total // groups // (2 * rows), 2, rows, w), F32),
            pltpu.VMEM((zs, ys, rows, w), F32),
            pltpu.VMEM((zs, ys, rows, w), F32),
            pltpu.VMEM((zs, fy, half, w), F32),
            pltpu.VMEM((zs - 1, ys, half, w), F32),
            pltpu.VMEM((zs, half, w), F32),
            pltpu.VMEM((ys, half, w), F32),
            pltpu.VMEM((zs - 1, half, w), F32),
            pltpu.VMEM((fy, half, w), F32),
            pltpu.VMEM((fy, rows, w), F32),
            pltpu.VMEM((rows, w), F32),
            pltpu.VMEM((zs - 1, rows, w), F32),
            pltpu.VMEM((1, 2, zs, ys, half, w), F32),
            pltpu.VMEM((1, 2, zs, ys, half, w), F32),
            pltpu.VMEM((1, 2, far, zs, half, w), F32),
            pltpu.VMEM((1, 2, zs, half, w), F32),
            pltpu.VMEM((1, 2, far, half, w), F32),
            pltpu.VMEM((zs, ys, 2, rows, w), F32),
            pltpu.VMEM((groups, rows, w), F32),
            pltpu.VMEM((2, 2, groups, half, w), F32),
            pltpu.VMEM((total, w), BF16),
            pltpu.VMEM((total, w), BF16),
            dma((6,)), dma((3, 2)), dma((8,)), dma((4, 2)), dma((2,)), dma((2,)),
            dma((zs,)), dma((zs,)),
            dma((zs, fy)), dma((zs, fy)), dma((zs - 1,)), dma((zs - 1,)),
            dma((zs - 1,)), dma((zs - 1,)), dma((fy,)), dma((fy,)),
            dma((zs - 1,)), dma((zs - 1,)), dma((zs, fy)), dma((zs, fy)), dma((zs,)), dma((zs,)),
            dma((ys,)), dma((ys,)), dma((fy,)), dma((fy,)), dma((zs - 1,)), dma((zs - 1,)),
            dma((1, 2)), dma((1, 2)),
            dma((1, 2, far)), dma((1, 2, far)),
            dma((1, 2, far)), dma((1, 2, far)),
            dma((1, groups - 1)), dma((1, groups - 1)),
            dma((2, 2, groups - 1)), dma((2, 2, groups - 1)),
        ],
        compiler_params=pltpu.CompilerParams(collective_id=0, has_side_effects=True, vmem_limit_bytes=63 << 20),
        name="whole",
    )(orbitals, jnp.transpose(neighbours, (0, 2, 1)), levels, box_counts, potential,
      jnp.transpose(deriv_blocks, (1, 0, 2)))


def settle_kernel(*refs):
    for src, dst in zip(refs[:3], refs[3:]):
        dst[...] = src[...]


def settle(arrays):
    vm = pl.BlockSpec(memory_space=pltpu.VMEM)
    return pl.pallas_call(
        settle_kernel,
        out_shape=tuple(jax.ShapeDtypeStruct(a.shape, a.dtype) for a in arrays),
        in_specs=[vm] * 3,
        out_specs=(vm,) * 3,
        name="settle",
    )(*arrays)


def body(orbitals, potential, deriv_blocks, levels, box_counts, neighbours):
    return settle(whole(orbitals, potential, deriv_blocks, levels, box_counts, neighbours))


def solution(mesh):
    in_specs = (
        P("box", None, "orb"),
        P("box", None),
        P(),
        P("box"),
        P("box"),
        P("box", None, None),
    )
    out_specs = (P("box", "orb"), P("box", "orb"), P("box", "orb"))
    return jax.shard_map(body, mesh=mesh, in_specs=in_specs, out_specs=out_specs, check_vma=False)
```

```python
import functools

import jax
import jax.numpy as jnp
from jax import lax
from jax.experimental import pallas as pl
from jax.experimental.pallas import tpu as pltpu
from jax.sharding import PartitionSpec as P

MESH = pl.DeviceIdType.MESH
HIGH = lax.Precision.HIGHEST
F32 = jnp.float32
BF16 = jnp.bfloat16


def quotient(x, n):
    return jnp.floor((x + 0.5) * (1.0 / n))


def far_first(count):
    return sorted(range(1, count), key=lambda d: -min(d, count - d))


def rows_and_cols(shape):
    r = lax.broadcasted_iota(jnp.int32, shape, 0).astype(F32)
    c = lax.broadcasted_iota(jnp.int32, shape, 1).astype(F32)
    return r, c


def split_two(x):
    hi = x.astype(BF16)
    return hi, (x - hi.astype(F32)).astype(BF16)


def hdot(a, b):
    return jnp.dot(a, b, precision=HIGH, preferred_element_type=F32)


def whole_kernel(n, pad, zs, ys, a_hbm, nb_ref, lev_ref, cnt_ref, pot_hbm, db_hbm, fock_ref, corr_ref, inv_ref,
                 a_ref, pot_ref, db_ref, in_sem, gath, halo, SA, SB, SC, Wsc, R, m12a, m12b, m12c, m0a, m0b, m0c, tbl, prow, pcol,
                 p_ref, abuf0, X0, B1a, B1b, Ya, Yb, B2a, B2b, BL1, YL, BL2, abuf, X, B1, Y, B2,
                 cpan, crow, urow, pan_hi, pan_lo,
                 xs_sem, xr_sem, hs_sem, hr_sem, ts_sem, tr_sem,
                 sa0, ra0, s1a, r1a, s1b, r1b, s2a, r2a, s2b, r2b, ga_s, ga_r, gb_s, gb_r, gf_s, gf_r, gl_s, gl_r,
                 sl1, rl1, sl2, rl2,
                 sa, ra, s1, r1, s2, r2, sx, rx, su, ru):
    b = lax.axis_index("box")
    o = lax.axis_index("orb")
    boxes = lax.axis_size("box")
    groups = lax.axis_size("orb")
    core = lax.rem(b, 2)
    chip = b // 2
    z = chip // ys
    y = lax.rem(chip, ys)
    sgn = 1 - 2 * core
    mate = b + sgn
    back1 = lax.rem(b - sgn + boxes, boxes)
    fwd2 = lax.rem(b + 2 * sgn + boxes, boxes)
    back2 = lax.rem(b - 2 * sgn + boxes, boxes)
    right = lax.rem(o + 1, groups)
    left = lax.rem(o + groups - 1, groups)
    nn = n * n
    w = a_ref.shape[2]
    rows = corr_ref.shape[0]
    half_rows = rows // 2
    total_rows = zs * ys * 2 * rows

    def at(zz, yy):
        return ((zz * ys + yy) * 2 + core, o)

    partner = (mate, o)
    zpeer = [at(lax.rem(z + d, zs), y) for d in range(1, zs)]
    ypeer = [at(z, lax.rem(y + d, ys)) for d in range(1, ys)]
    xpeer = [(b, lax.rem(o + d, groups)) for d in range(1, groups)]

    barrier = pltpu.get_barrier_semaphore()
    peers = [partner, (back1, o), (fwd2, o), (back2, o)] + xpeer + ypeer + zpeer
    for dev in peers:
        pl.semaphore_signal(barrier, inc=1, device_id=dev, device_id_type=MESH)

    fetches = [pltpu.make_async_copy(src, dst, in_sem.at[i]) for i, (src, dst) in
               enumerate(((a_hbm, a_ref), (pot_hbm, pot_ref), (db_hbm, db_ref)))]
    for fetch in fetches:
        fetch.start()

    shape = tbl.shape[1:]
    r = lax.broadcasted_iota(jnp.int32, shape, 0)
    c = lax.broadcasted_iota(jnp.int32, shape, 1)
    own = jnp.zeros(shape, jnp.int32)
    for k in range(2):
        mine = (r >= k * n) & (r < (k + 1) * n)
        for a in range(3):
            own = jnp.where(mine & (c == a * 3), nb_ref[k, 0, a], own)
            own = jnp.where(mine & (c == a * 3 + 1), b * 2 + k, own)
            own = jnp.where(mine & (c == a * 3 + 2), nb_ref[k, 1, a], own)
        code = jnp.where(cnt_ref[0] > k, lev_ref[k], -1)
        own = jnp.where(mine & (c == 9), code, own)
    tbl[0] = own

    pl.semaphore_wait(barrier, len(peers))

    def remote(src, dst, ssem, rsem, dev):
        return pltpu.make_async_remote_copy(src_ref=src, dst_ref=dst, send_sem=ssem, recv_sem=rsem,
                                            device_id=dev, device_id_type=MESH)

    sends = {}
    for i, (k, q, dev) in enumerate(((0, 0, (b, right)), (1, 1, (b, left)), (1, 0, (b, right)), (0, 1, (b, left)))):
        sends[i] = remote(a_hbm.at[k], gath.at[q, k], xs_sem.at[i], xr_sem.at[q, k], dev)
    xf0 = remote(gath.at[0, 0], gath.at[2, 0], xs_sem.at[4], xr_sem.at[2, 0], (b, right))
    xf1 = remote(gath.at[1, 1], gath.at[2, 1], xs_sem.at[5], xr_sem.at[2, 1], (b, left))
    h1 = [remote(a_hbm.at[k], halo.at[1, k], hs_sem.at[k], hr_sem.at[1, k], (back1, o)) for k in range(2)]
    h2 = [remote(a_hbm.at[k], halo.at[2, k], hs_sem.at[2 + k], hr_sem.at[2, k], (fwd2, o)) for k in range(2)]
    h0 = [remote(a_hbm.at[k], halo.at[0, k], hs_sem.at[4 + k], hr_sem.at[0, k], partner) for k in range(2)]
    h3 = [remote(halo.at[1, k], halo.at[3, k], hs_sem.at[6 + k], hr_sem.at[3, k], partner) for k in range(2)]
    t1 = remote(tbl.at[0], tbl.at[1], ts_sem.at[0], tr_sem.at[0], partner)
    t2 = remote(tbl.at[0], tbl.at[2], ts_sem.at[1], tr_sem.at[1], (back1, o))
    sends[0].start()
    sends[1].start()
    t2.start()
    h1[0].start()
    h2[0].start()
    t1.start()
    h0[0].start()
    h0[1].start()
    sends[2].start()
    sends[3].start()
    h1[1].start()
    h2[1].start()

    for fetch in fetches:
        fetch.wait()

    alive = [jnp.where(cnt_ref[0] > k, 1.0, 0.0) for k in range(2)]
    for k in range(2):
        R[k, :, 0:w] = (a_ref[k].astype(F32) * alive[k]).astype(BF16)

    def correlate(block, place):
        total = jnp.zeros((w, w), F32)
        for k in range(2):
            total = total + lax.dot_general(block[k], R[k, :, 0:w], (((0,), (0,)), ((), ())),
                                            preferred_element_type=F32)
        p_ref[0, place] = total.reshape(ys, 2, rows, w)

    def fock_part(block, place):
        total = jnp.zeros((w, 2 * w), F32)
        for k in range(2):
            total = total + lax.dot_general(block[k], R[k, :, w:3 * w], (((0,), (0,)), ((), ())),
                                            preferred_element_type=F32)
        p_ref[1, place] = (total[:, 0:w] + total[:, w:2 * w]).reshape(ys, 2, rows, w)

    edge = nn // 16 * 16
    for S in (SA, SB, SC):
        S[:, :, edge:pad, :] = jnp.zeros((n, S.shape[1], pad - edge, w), BF16)

    def spread(block, S, q):
        for l in range(n):
            S[l, q, 0:nn, :] = block[l * nn:(l + 1) * nn, :]

    spread(a_ref.at[0], SA, 0)
    spread(a_ref.at[1], SA, 1)
    started = []

    def send(src, dst, ssem, rsem, dev):
        copy = pltpu.make_async_remote_copy(src_ref=src, dst_ref=dst, send_sem=ssem, recv_sem=rsem,
                                            device_id=dev, device_id_type=MESH)
        copy.start()
        started.append(copy)
        return copy

    part = [pl.ds(0, half_rows), pl.ds(half_rows, half_rows)]

    order_z = [o, left, right, lax.rem(o + 2, groups)]
    last = order_z[3]
    low, high = part
    pairs = {}
    one_a = {}

    def ahead(i):
        return lax.rem(order_z[i] - z + zs, zs)

    def behind(i):
        return lax.rem(z - order_z[i] + zs, zs)

    def pair_send(i):
        zp = order_z[i]
        pairs[i] = send(p_ref.at[0, zp, :, 1 - core], abuf0.at[zp], sa0.at[i], ra0.at[i], partner)

    def pair_add(i):
        zp = order_z[i]
        pairs[i].wait_recv()
        X0[zp] = p_ref[0, zp, :, core] + abuf0[zp]

    def c_one(i):
        zp = order_z[i]
        for d in range(1, ys):
            one_a[i, d] = send(X0.at[zp, lax.rem(y + d, ys), low], B1a.at[i, d - 1], s1a.at[i, d - 1],
                               r1a.at[i, d - 1], ypeer[d - 1])
        e = ahead(i)

        @pl.when(e > 0)
        def _():
            remote(X0.at[zp, :, high], B1b.at[e - 1], s1b.at[e - 1], r1b.at[e - 1], at(zp, y)).start()

    def c_two_a(i):
        zp = order_z[i]
        acc = X0[zp, y, low]
        for d in range(1, ys):
            one_a[i, d].wait_recv()
            acc = acc + B1a[i, d - 1]
        Ya[zp] = acc
        e = ahead(i)

        @pl.when(e > 0)
        def _():
            remote(Ya.at[zp], B2a.at[e - 1], s2a.at[e - 1], r2a.at[e - 1], at(zp, y)).start()

    def c_two_b():
        for e in range(1, zs):
            remote(B1b.at[e - 1], B1b.at[e - 1], s1b.at[e - 1], r1b.at[e - 1], partner).wait_recv()
        acc = X0[z, :, high]
        for e in range(1, zs):
            acc = acc + B1b[e - 1]
        Yb[...] = acc
        for d in range(1, ys):
            remote(Yb.at[lax.rem(y + d, ys)], B2b.at[d - 1], s2b.at[d - 1], r2b.at[d - 1], ypeer[d - 1]).start()

    def publish():
        spot = cpan.at[z, y, core]
        for e in far_first(zs):
            remote(spot, spot, ga_s.at[e - 1], ga_r.at[e - 1], zpeer[e - 1]).start()
        for d in far_first(ys):
            remote(spot, spot, gb_s.at[z, d - 1], gb_r.at[z, d - 1], ypeer[d - 1]).start()
        for d in far_first(groups):
            remote(spot, crow.at[o], sx.at[0, d - 1], rx.at[0, d - 1], xpeer[d - 1]).start()

    def c_end():
        piece = Ya[z]
        for e in range(1, zs):
            remote(B2a.at[e - 1], B2a.at[e - 1], s2a.at[e - 1], r2a.at[e - 1], partner).wait_recv()
            piece = piece + B2a[e - 1]
        corr_ref[low, :] = piece
        cpan[z, y, core, low] = piece
        crow[o, low] = piece
        piece = Yb[y]
        for d in range(1, ys):
            remote(B2b.at[d - 1], B2b.at[d - 1], s2b.at[d - 1], r2b.at[d - 1], partner).wait_recv()
            piece = piece + B2b[d - 1]
        corr_ref[high, :] = piece
        cpan[z, y, core, high] = piece
        crow[o, high] = piece
        publish()

    def g_two(i):
        zp = order_z[i]
        spot = cpan.at[zp, y, core]
        e = behind(i)

        @pl.when(e > 0)
        def _():
            remote(spot, spot, ga_s.at[e - 1], ga_r.at[e - 1], partner).wait_recv()
            for d in far_first(ys):
                remote(spot, spot, gb_s.at[zp, d - 1], gb_r.at[zp, d - 1], ypeer[d - 1]).start()

    def g_end(i):
        zp = order_z[i]
        spot = cpan.at[zp, y, core]
        for d in range(1, ys):
            remote(spot, spot, gb_s.at[zp, d - 1], gb_r.at[zp, d - 1], partner).wait_recv()
        column = cpan.at[zp, :, core]
        return send(column, column, gf_s.at[i], gf_r.at[i], partner)

    def late_one():
        out = {}
        for d in far_first(ys):
            out[d] = send(X0.at[last, lax.rem(y + d, ys)], BL1.at[d - 1], sl1.at[d - 1], rl1.at[d - 1], ypeer[d - 1])
        return [out[d] for d in range(1, ys)]

    def late_two(copies):
        acc = X0[last, y]
        for d, copy in enumerate(copies):
            copy.wait_recv()
            acc = acc + BL1[d]
        YL[...] = acc
        for e in far_first(zs):
            remote(YL, BL2.at[e - 1], sl2.at[e - 1], rl2.at[e - 1], zpeer[e - 1]).start()

    def late_end():
        piece = YL[...]
        for e in range(1, zs):
            remote(BL2.at[e - 1], BL2.at[e - 1], sl2.at[e - 1], rl2.at[e - 1], partner).wait_recv()
            piece = piece + BL2[e - 1]
        cpan[last, y, core] = piece
        spot = cpan.at[last, y, core]
        for d in far_first(ys):
            remote(spot, spot, gb_s.at[last, d - 1], gb_r.at[last, d - 1], ypeer[d - 1]).start()
        forwards.append(send(spot, spot, gl_s.at[0], gl_r.at[0], partner))

        @pl.when(z == last)
        def _():
            corr_ref[...] = piece
            crow[o] = piece
            for d in range(1, groups):
                remote(spot, crow.at[o], sx.at[0, d - 1], rx.at[0, d - 1], xpeer[d - 1]).start()

    def late_forward():
        for d in range(1, ys):
            spot = cpan.at[last, lax.rem(y - d + ys, ys), core]
            remote(spot, spot, gb_s.at[last, d - 1], gb_r.at[last, d - 1], partner).wait_recv()
            forwards.append(send(spot, spot, gl_s.at[d], gl_r.at[d], partner))

    correlate(a_ref, o)
    pair_send(0)

    prow[...] = jnp.zeros(prow.shape, F32)
    prow[0:2, 0:n * nn] = pot_ref[...]
    pcol[...] = prow[...].T

    order = [(b, 0), (b, 1), (mate, 0), (mate, 1), (back1, 0), (back2, 0), (fwd2, 0), (back1, 1), (back2, 1),
             (fwd2, 1)]
    shape = (2 * n, 10 * n)
    ci = lax.broadcasted_iota(jnp.int32, shape, 1)
    gid = jnp.zeros(shape, jnp.int32)
    for q, (dev, k) in enumerate(order):
        gid = jnp.where((ci >= q * n) & (ci < (q + 1) * n), dev * 2 + k, gid)
    r, c = rows_and_cols((2 * n, n))
    pick_r = jnp.where(r - n * quotient(r, n) == c, 1.0, 0.0)
    r, c = rows_and_cols((n, 10 * n))
    pick_c = jnp.where(c - n * quotient(c, n) == r, 1.0, 0.0)
    bt = [hdot(hdot(pick_r, db_ref[:, u, :].astype(F32)), pick_c) for u in range(3)]
    t1.wait_recv()
    t2.wait_recv()
    M = [jnp.zeros(shape, F32) for _ in range(3)]
    for d in range(3):
        code = tbl[d, 0:2 * n, 9:10]
        factor = jnp.where(code < 0, 0.0, jnp.where(code == 0, 0.5, jnp.where(code == 1, 1.0, 2.0)))
        for a in range(3):
            t = jnp.zeros(shape, F32)
            for u in range(3):
                t = t + jnp.where(tbl[d, 0:2 * n, a * 3 + u:a * 3 + u + 1] == gid, bt[u], 0.0)
            t = t * factor
            M[a] = M[a] + 0.5 * lax.dot_general(t[:, 0:2 * n], t, (((0,), (0,)), ((), ())), precision=HIGH,
                                                preferred_element_type=F32)
    half = 2 * pad
    r, c = rows_and_cols((half, 2 * n))
    rs = quotient(r, pad)
    rq = r - rs * pad
    ri1 = quotient(rq, n)
    ri2 = rq - ri1 * n
    ok = rq < nn
    cs = quotient(c, n)
    ci = c - cs * n
    L1 = jnp.where(ok & (cs == rs) & (ci == ri1), 1.0, 0.0)
    L2 = jnp.where(ok & (cs == rs) & (ci == ri2), 1.0, 0.0)
    LM1 = hdot(L1, M[1])
    LM2 = hdot(L2, M[2])
    r, c = rows_and_cols((n * 32, 2 * n))
    ri = quotient(r, 32)
    rs = quotient(r, 16) - 2 * ri
    cs = quotient(c, n)
    L0 = jnp.where((cs == rs) & ((c - cs * n) == ri), 1.0, 0.0)
    LM0 = hdot(L0, M[0])

    def expand(m12, m0, base, count):
        wide = count * pad
        r, c = rows_and_cols((10 * n, wide))
        cs = quotient(c, pad)
        cq = c - cs * pad
        cl1 = quotient(cq, n)
        cl2 = cq - cl1 * n
        ok = cq < nn
        rs = quotient(r, n)
        ri = r - rs * n
        ok = ok & (cs + base == rs)
        C1 = jnp.where(ok & (ri == cl1), 1.0, 0.0)
        C2 = jnp.where(ok & (ri == cl2), 1.0, 0.0)
        r, c = rows_and_cols((half, wide))
        rq = r - quotient(r, pad) * pad
        cq = c - quotient(c, pad) * pad
        ri1 = quotient(rq, n)
        cl1 = quotient(cq, n)
        same1 = ri1 == cl1
        same2 = (rq - ri1 * n) == (cq - cl1 * n)
        full = jnp.where(same2, hdot(LM1, C1), 0.0) + jnp.where(same1, hdot(LM2, C2), 0.0)
        hi, lo = split_two(full)
        m12[0:half, :] = hi
        m12[half:2 * half, :] = lo
        step = count * 16
        r, c = rows_and_cols((10 * n, n * step))
        cl = quotient(c, step)
        cs = quotient(c - cl * step, 16)
        rs = quotient(r, n)
        C0 = jnp.where((rs == cs + base) & ((r - rs * n) == cl), 1.0, 0.0)
        r, c = rows_and_cols((n * 32, n * step))
        same = (r - 16 * quotient(r, 16)) == (c - 16 * quotient(c, 16))
        full = jnp.where(same, hdot(LM0, C0), 0.0)
        hi, lo = split_two(full)
        m0[0:n * 32, :] = hi
        m0[n * 32:n * 64, :] = lo

    def apply_inner(S, m12, fresh):
        count = S.shape[1]

        @pl.loop(0, n)
        def _(i):
            got = jnp.dot(m12[...], S[i].reshape(count * pad, w), preferred_element_type=F32)
            got = (got[0:half] + got[half:2 * half]).reshape(2, pad, w)
            Wsc[i] = got if fresh else Wsc[i] + got

    def apply_outer(S, m0):
        count = S.shape[1]

        @pl.loop(0, pad // 16)
        def _(i):
            rows = pl.ds(pl.multiple_of(i * 16, 16), 16)
            got = jnp.dot(m0[...], S[:, :, rows, :].reshape(n * count * 16, w), preferred_element_type=F32)
            Wsc[:, :, rows, :] = Wsc[:, :, rows, :] + (got[0:n * 32] + got[n * 32:n * 64]).reshape(n, 2, 16, w)

    expand(m12a, m0a, 0, 4)
    for k in range(2):
        h0[k].wait_recv()
        spread(halo.at[0, k], SA, 2 + k)
    apply_inner(SA, m12a, True)
    apply_outer(SA, m0a)
    expand(m12b, m0b, 4, 3)
    expand(m12c, m0c, 7, 3)

    sends[0].wait_recv()
    xf0.start()
    sends[1].wait_recv()
    xf1.start()
    h1[0].wait_recv()
    h3[0].start()
    spread(halo.at[1, 0], SB, 0)
    h2[0].wait_recv()
    spread(halo.at[2, 0], SB, 1)
    h3[0].wait_recv()
    spread(halo.at[3, 0], SB, 2)
    apply_inner(SB, m12b, False)
    apply_outer(SB, m0b)

    h1[1].wait_recv()
    h3[1].start()
    pair_add(0)
    c_one(0)
    sends[2].wait_recv()
    correlate(gath.at[0], left)
    pair_send(1)
    sends[3].wait_recv()
    correlate(gath.at[1], right)
    pair_send(2)
    pair_add(1)
    c_one(1)
    spread(halo.at[1, 1], SC, 0)
    h2[1].wait_recv()
    spread(halo.at[2, 1], SC, 1)
    h3[1].wait_recv()
    spread(halo.at[3, 1], SC, 2)
    pair_add(2)
    c_one(2)
    apply_inner(SC, m12c, False)
    apply_outer(SC, m0c)

    for k in range(2):
        for l in range(n):
            full = Wsc[l, k] + (pcol[l * nn:l * nn + pad, k:k + 1] * alive[k]) * SA[l, k].astype(F32)
            hi, lo = split_two(full)
            R[k, l * nn:(l + 1) * nn, w:2 * w] = hi[0:nn]
            R[k, l * nn:(l + 1) * nn, 2 * w:3 * w] = lo[0:nn]

    for i in range(3):
        c_two_a(i)
    pl.when(z != last)(c_two_b)
    fock_part(a_ref, o)
    fock_part(gath.at[0], left)
    xf0.wait_recv()
    xf1.wait_recv()
    correlate(gath.at[2], last)
    pair_send(3)
    pl.when(z != last)(c_end)
    pair_add(3)
    late = late_one()
    fock_part(gath.at[1], right)
    fock_part(gath.at[2], last)

    first = {}

    for h in range(2):
        first[0, h] = send(p_ref.at[1, :, :, 1 - core, part[h]], abuf.at[0, h], sa.at[0, h], ra.at[0, h], partner)
    for i in range(3):
        g_two(i)
    late_two(late)

    def add_pair(f, h):
        first[f, h].wait_recv()
        X[f, h] = p_ref[1, :, :, core, part[h]] + abuf[f, h]

    def scatter_one(f, h):
        out = []
        for d in range(1, ys if h == 0 else zs):
            if h == 0:
                t = lax.rem(y + d, ys)
                src = X.at[f, h, :, t]
            else:
                t = lax.rem(z + d, zs)
                src = X.at[f, h, t]
            out.append(send(src, B1.at[f, h, d - 1], s1.at[f, h, d - 1], r1.at[f, h, d - 1],
                            (ypeer if h == 0 else zpeer)[d - 1]))
        return out

    def scatter_two(f, h, copies):
        for copy in copies:
            copy.wait_recv()
        acc = X[f, h, :, y] if h == 0 else X[f, h, z]
        for d in range(1, ys if h == 0 else zs):
            acc = acc + B1[f, h, d - 1]
        Y[f, h] = acc
        out = []
        for d in range(1, zs if h == 0 else ys):
            t = lax.rem(z + d, zs) if h == 0 else lax.rem(y + d, ys)
            out.append(send(Y.at[f, h, t], B2.at[f, h, d - 1], s2.at[f, h, d - 1], r2.at[f, h, d - 1],
                            (zpeer if h == 0 else ypeer)[d - 1]))
        return out

    def scatter_end(f, h, copies):
        for copy in copies:
            copy.wait_recv()
        acc = Y[f, h, z] if h == 0 else Y[f, h, y]
        for d in range(1, zs if h == 0 else ys):
            acc = acc + B2[f, h, d - 1]
        return acc

    one = {}
    two = {}
    for h in range(2):
        add_pair(0, h)
    forwards = []
    late_end()
    early = [g_end(i) for i in range(3)]
    for h in range(2):
        one[0, h] = scatter_one(0, h)

    def diagonal(count, start):
        r = lax.broadcasted_iota(jnp.int32, (count, w), 0) + start
        c = lax.broadcasted_iota(jnp.int32, (count, w), 1) + o * w
        return r == c

    def product(left):
        lhi, llo = split_two(left)
        both = jnp.concatenate([lhi.astype(F32), llo.astype(F32)], axis=0).astype(BF16)
        big = jnp.dot(both, pan_hi[...], preferred_element_type=F32)
        return big[0:half_rows] + big[half_rows:rows] + jnp.dot(lhi, pan_lo[...], preferred_element_type=F32)

    def row_gather(g, h, value):
        urow[g, h, o] = value
        out = []
        for d in far_first(groups):
            out.append(send(urow.at[g, h, o], urow.at[g, h, o], su.at[g, h, d - 1], ru.at[g, h, d - 1], xpeer[d - 1]))
        return out

    def arrived(copies):
        for copy in copies:
            copy.wait_recv()

    step = total_rows // zs

    def turn_panel(zp):
        first_row = pl.multiple_of(zp * step, 128)
        block = jnp.where(diagonal(step, first_row), 1.5, 0.0) - 0.5 * cpan[zp].reshape(step, w)
        hi, lo = split_two(block)
        span = pl.ds(first_row, step)
        pan_hi[span, :] = hi
        pan_lo[span, :] = lo

    for i in range(3):
        early[i].wait_recv()
        turn_panel(order_z[i])
    late_forward()
    for d in range(1, groups):
        remote(crow.at[0], crow.at[0], sx.at[0, d - 1], rx.at[0, d - 1], partner).wait_recv()
    for copy in forwards:
        copy.wait_recv()
    turn_panel(last)
    moved = {}
    for h in range(2):
        row = jnp.concatenate([crow[k, part[h]] for k in range(groups)], axis=1)
        moved[0, h] = row_gather(0, h, product(row))
    for h in range(2):
        arrived(moved[0, h])
        row = jnp.concatenate([urow[0, h, k] for k in range(groups)], axis=1)
        moved[1, h] = row_gather(1, h, product(row))
    for h in range(2):
        two[0, h] = scatter_two(0, h, one[0, h])
    for h in range(2):
        arrived(moved[1, h])
        row = jnp.concatenate([urow[1, h, k] for k in range(groups)], axis=1)
        right = product(row)
        turn = jnp.where(diagonal(half_rows, b * rows + h * half_rows), 1.5, 0.0) - 0.5 * corr_ref[part[h], :]
        inv_ref[part[h], :] = 1.5 * turn - 0.5 * right
    for h in range(2):
        fock_ref[part[h], :] = scatter_end(0, h, two[0, h])

    def sent(ref, sem):
        remote(ref, ref, sem, rl1.at[0], partner).wait_send()

    for i in range(3):
        e = ahead(i)

        @pl.when(e > 0)
        def _():
            sent(B1b.at[e - 1], s1b.at[e - 1])
            sent(B2a.at[e - 1], s2a.at[e - 1])

    @pl.when(z != last)
    def _():
        for e in range(1, zs):
            sent(cpan.at[0, 0, core], ga_s.at[e - 1])
        for d in range(1, ys):
            sent(B2b.at[d - 1], s2b.at[d - 1])

    for e in range(1, zs):
        sent(YL, sl2.at[e - 1])
    for zp in range(zs):
        for d in range(1, ys):
            sent(cpan.at[0, 0, core], gb_s.at[zp, d - 1])
    for d in range(1, groups):
        sent(crow.at[0], sx.at[0, d - 1])
    for copy in started:
        copy.wait_send()
    for i in range(4):
        sends[i].wait_send()
    xf0.wait_send()
    xf1.wait_send()
    t1.wait_send()
    t2.wait_send()
    for k in range(2):
        h0[k].wait_send()
        h1[k].wait_send()
        h2[k].wait_send()
        h3[k].wait_send()


def whole(orbitals, potential, deriv_blocks, levels, box_counts, neighbours):
    slots, coefs, w = orbitals.shape
    n = deriv_blocks.shape[1]
    nn = n * n
    pad = -(-nn // 16) * 16
    boxes = lax.axis_size("box")
    groups = lax.axis_size("orb")
    zs = groups
    ys = boxes // 2 // zs
    fy = max(ys - 1, 1)
    total = groups * w
    rows = total // boxes
    half = rows // 2
    far = max(zs, ys) - 1
    vm = pl.BlockSpec(memory_space=pltpu.VMEM)
    sm = pl.BlockSpec(memory_space=pltpu.SMEM)
    hbm = pl.BlockSpec(memory_space=pl.ANY)
    column = -(-((n - 1) * nn + pad) // 128) * 128
    dma = pltpu.SemaphoreType.DMA
    out = jax.ShapeDtypeStruct((rows, w), F32)
    return pl.pallas_call(
        functools.partial(whole_kernel, n, pad, zs, ys),
        out_shape=(out, out, out),
        in_specs=[hbm, sm, sm, sm, hbm, hbm],
        out_specs=(vm, vm, vm),
        scratch_shapes=[
            pltpu.VMEM((slots, coefs, w), BF16),
            pltpu.VMEM((slots, coefs), F32),
            pltpu.VMEM((n, 3, n), BF16),
            dma((3,)),
            pltpu.VMEM((3, slots, coefs, w), BF16),
            pltpu.VMEM((4, slots, coefs, w), BF16),
            pltpu.VMEM((n, 4, pad, w), BF16),
            pltpu.VMEM((n, 3, pad, w), BF16),
            pltpu.VMEM((n, 3, pad, w), BF16),
            pltpu.VMEM((n, 2, pad, w), F32),
            pltpu.VMEM((slots, coefs, 3 * w), BF16),
            pltpu.VMEM((4 * pad, 4 * pad), BF16),
            pltpu.VMEM((4 * pad, 3 * pad), BF16),
            pltpu.VMEM((4 * pad, 3 * pad), BF16),
            pltpu.VMEM((n * 64, n * 64), BF16),
            pltpu.VMEM((n * 64, n * 48), BF16),
            pltpu.VMEM((n * 64, n * 48), BF16),
            pltpu.VMEM((3, -(-slots * n // 8) * 8, 128), jnp.int32),
            pltpu.VMEM((8, column), F32),
            pltpu.VMEM((column, 8), F32),
            pltpu.VMEM((2, groups, total // groups // (2 * rows), 2, rows, w), F32),
            pltpu.VMEM((zs, ys, rows, w), F32),
            pltpu.VMEM((zs, ys, rows, w), F32),
            pltpu.VMEM((zs, fy, half, w), F32),
            pltpu.VMEM((zs - 1, ys, half, w), F32),
            pltpu.VMEM((zs, half, w), F32),
            pltpu.VMEM((ys, half, w), F32),
            pltpu.VMEM((zs - 1, half, w), F32),
            pltpu.VMEM((fy, half, w), F32),
            pltpu.VMEM((fy, rows, w), F32),
            pltpu.VMEM((rows, w), F32),
            pltpu.VMEM((zs - 1, rows, w), F32),
            pltpu.VMEM((1, 2, zs, ys, half, w), F32),
            pltpu.VMEM((1, 2, zs, ys, half, w), F32),
            pltpu.VMEM((1, 2, far, zs, half, w), F32),
            pltpu.VMEM((1, 2, zs, half, w), F32),
            pltpu.VMEM((1, 2, far, half, w), F32),
            pltpu.VMEM((zs, ys, 2, rows, w), F32),
            pltpu.VMEM((groups, rows, w), F32),
            pltpu.VMEM((2, 2, groups, half, w), F32),
            pltpu.VMEM((total, w), BF16),
            pltpu.VMEM((total, w), BF16),
            dma((6,)), dma((3, 2)), dma((8,)), dma((4, 2)), dma((2,)), dma((2,)),
            dma((zs,)), dma((zs,)),
            dma((zs, fy)), dma((zs, fy)), dma((zs - 1,)), dma((zs - 1,)),
            dma((zs - 1,)), dma((zs - 1,)), dma((fy,)), dma((fy,)),
            dma((zs - 1,)), dma((zs - 1,)), dma((zs, fy)), dma((zs, fy)), dma((zs,)), dma((zs,)),
            dma((ys,)), dma((ys,)), dma((fy,)), dma((fy,)), dma((zs - 1,)), dma((zs - 1,)),
            dma((1, 2)), dma((1, 2)),
            dma((1, 2, far)), dma((1, 2, far)),
            dma((1, 2, far)), dma((1, 2, far)),
            dma((1, groups - 1)), dma((1, groups - 1)),
            dma((2, 2, groups - 1)), dma((2, 2, groups - 1)),
        ],
        compiler_params=pltpu.CompilerParams(collective_id=0, has_side_effects=True, vmem_limit_bytes=63 << 20),
        name="whole",
    )(orbitals, jnp.transpose(neighbours, (0, 2, 1)), levels, box_counts, potential,
      jnp.transpose(deriv_blocks, (1, 0, 2)))


def settle_kernel(*refs):
    for src, dst in zip(refs[:3], refs[3:]):
        dst[...] = src[...]


def settle(arrays):
    vm = pl.BlockSpec(memory_space=pltpu.VMEM)
    return pl.pallas_call(
        settle_kernel,
        out_shape=tuple(jax.ShapeDtypeStruct(a.shape, a.dtype) for a in arrays),
        in_specs=[vm] * 3,
        out_specs=(vm,) * 3,
        name="settle",
    )(*arrays)


def body(orbitals, potential, deriv_blocks, levels, box_counts, neighbours):
    return settle(whole(orbitals, potential, deriv_blocks, levels, box_counts, neighbours))


def solution(mesh):
    in_specs = (
        P("box", None, "orb"),
        P("box", None),
        P(),
        P("box"),
        P("box"),
        P("box", None, None),
    )
    out_specs = (P("box", "orb"), P("box", "orb"), P("box", "orb"))
    return jax.shard_map(body, mesh=mesh, in_specs=in_specs, out_specs=out_specs, check_vma=False)
```

```python
import functools

import jax
import jax.numpy as jnp
from jax import lax
from jax.experimental import pallas as pl
from jax.experimental.pallas import tpu as pltpu
from jax.sharding import PartitionSpec as P

MESH = pl.DeviceIdType.MESH
HIGH = lax.Precision.HIGHEST
F32 = jnp.float32
BF16 = jnp.bfloat16


def quotient(x, n):
    return jnp.floor((x + 0.5) * (1.0 / n))


def far_first(count):
    return sorted(range(1, count), key=lambda d: -min(d, count - d))


def rows_and_cols(shape):
    r = lax.broadcasted_iota(jnp.int32, shape, 0).astype(F32)
    c = lax.broadcasted_iota(jnp.int32, shape, 1).astype(F32)
    return r, c


def split_two(x):
    hi = x.astype(BF16)
    return hi, (x - hi.astype(F32)).astype(BF16)


def hdot(a, b):
    return jnp.dot(a, b, precision=HIGH, preferred_element_type=F32)


def whole_kernel(n, pad, zs, ys, a_hbm, nb_ref, lev_ref, cnt_ref, pot_hbm, db_hbm, fock_ref, corr_ref, inv_ref,
                 a_ref, pot_ref, db_ref, in_sem, gath, halo, SA, SB, SC, Wsc, R, m12a, m12b, m12c, m0a, m0b, m0c, tbl, prow, pcol,
                 p_ref, abuf0, X0, B1a, B1b, Ya, Yb, B2a, B2b, BL1, YL, BL2, abuf, X, B1, Y, B2,
                 cpan, crow, urow, pan_hi, pan_lo,
                 xs_sem, xr_sem, hs_sem, hr_sem, ts_sem, tr_sem,
                 sa0, ra0, s1a, r1a, s1b, r1b, s2a, r2a, s2b, r2b, ga_s, ga_r, gb_s, gb_r, gf_s, gf_r, gl_s, gl_r,
                 sl1, rl1, sl2, rl2,
                 sa, ra, s1, r1, s2, r2, sx, rx, su, ru):
    b = lax.axis_index("box")
    o = lax.axis_index("orb")
    boxes = lax.axis_size("box")
    groups = lax.axis_size("orb")
    core = lax.rem(b, 2)
    chip = b // 2
    z = chip // ys
    y = lax.rem(chip, ys)
    sgn = 1 - 2 * core
    mate = b + sgn
    back1 = lax.rem(b - sgn + boxes, boxes)
    fwd2 = lax.rem(b + 2 * sgn + boxes, boxes)
    back2 = lax.rem(b - 2 * sgn + boxes, boxes)
    right = lax.rem(o + 1, groups)
    left = lax.rem(o + groups - 1, groups)
    nn = n * n
    w = a_ref.shape[2]
    rows = corr_ref.shape[0]
    half_rows = rows // 2
    total_rows = zs * ys * 2 * rows

    def at(zz, yy):
        return ((zz * ys + yy) * 2 + core, o)

    partner = (mate, o)
    zpeer = [at(lax.rem(z + d, zs), y) for d in range(1, zs)]
    ypeer = [at(z, lax.rem(y + d, ys)) for d in range(1, ys)]
    xpeer = [(b, lax.rem(o + d, groups)) for d in range(1, groups)]

    barrier = pltpu.get_barrier_semaphore()
    peers = [partner, (back1, o), (fwd2, o), (back2, o)] + xpeer + ypeer + zpeer
    for dev in peers:
        pl.semaphore_signal(barrier, inc=1, device_id=dev, device_id_type=MESH)

    fetches = [pltpu.make_async_copy(src, dst, in_sem.at[i]) for i, (src, dst) in
               enumerate(((a_hbm, a_ref), (pot_hbm, pot_ref), (db_hbm, db_ref)))]
    for fetch in fetches:
        fetch.start()

    shape = tbl.shape[1:]
    r = lax.broadcasted_iota(jnp.int32, shape, 0)
    c = lax.broadcasted_iota(jnp.int32, shape, 1)
    own = jnp.zeros(shape, jnp.int32)
    for k in range(2):
        mine = (r >= k * n) & (r < (k + 1) * n)
        for a in range(3):
            own = jnp.where(mine & (c == a * 3), nb_ref[k, 0, a], own)
            own = jnp.where(mine & (c == a * 3 + 1), b * 2 + k, own)
            own = jnp.where(mine & (c == a * 3 + 2), nb_ref[k, 1, a], own)
        code = jnp.where(cnt_ref[0] > k, lev_ref[k], -1)
        own = jnp.where(mine & (c == 9), code, own)
    tbl[0] = own

    pl.semaphore_wait(barrier, len(peers))

    def remote(src, dst, ssem, rsem, dev):
        return pltpu.make_async_remote_copy(src_ref=src, dst_ref=dst, send_sem=ssem, recv_sem=rsem,
                                            device_id=dev, device_id_type=MESH)

    sends = {}
    for i, (k, q, dev) in enumerate(((0, 0, (b, right)), (1, 1, (b, left)), (1, 0, (b, right)), (0, 1, (b, left)))):
        sends[i] = remote(a_hbm.at[k], gath.at[q, k], xs_sem.at[i], xr_sem.at[q, k], dev)
    xf0 = remote(gath.at[0, 0], gath.at[2, 0], xs_sem.at[4], xr_sem.at[2, 0], (b, right))
    xf1 = remote(gath.at[1, 1], gath.at[2, 1], xs_sem.at[5], xr_sem.at[2, 1], (b, left))
    h1 = [remote(a_hbm.at[k], halo.at[1, k], hs_sem.at[k], hr_sem.at[1, k], (back1, o)) for k in range(2)]
    h2 = [remote(a_hbm.at[k], halo.at[2, k], hs_sem.at[2 + k], hr_sem.at[2, k], (fwd2, o)) for k in range(2)]
    h0 = [remote(a_hbm.at[k], halo.at[0, k], hs_sem.at[4 + k], hr_sem.at[0, k], partner) for k in range(2)]
    h3 = [remote(halo.at[1, k], halo.at[3, k], hs_sem.at[6 + k], hr_sem.at[3, k], partner) for k in range(2)]
    t1 = remote(tbl.at[0], tbl.at[1], ts_sem.at[0], tr_sem.at[0], partner)
    t2 = remote(tbl.at[0], tbl.at[2], ts_sem.at[1], tr_sem.at[1], (back1, o))
    sends[0].start()
    sends[1].start()
    t2.start()
    h1[0].start()
    h2[0].start()
    t1.start()
    h0[0].start()
    h0[1].start()
    sends[2].start()
    sends[3].start()
    h1[1].start()
    h2[1].start()

    for fetch in fetches:
        fetch.wait()

    alive = [jnp.where(cnt_ref[0] > k, 1.0, 0.0) for k in range(2)]
    for k in range(2):
        R[k, :, 0:w] = (a_ref[k].astype(F32) * alive[k]).astype(BF16)

    def correlate(block, place):
        total = jnp.zeros((w, w), F32)
        for k in range(2):
            total = total + lax.dot_general(block[k], R[k, :, 0:w], (((0,), (0,)), ((), ())),
                                            preferred_element_type=F32)
        p_ref[0, place] = total.reshape(ys, 2, rows, w)

    def fock_part(block, place):
        total = jnp.zeros((w, 2 * w), F32)
        for k in range(2):
            total = total + lax.dot_general(block[k], R[k, :, w:3 * w], (((0,), (0,)), ((), ())),
                                            preferred_element_type=F32)
        p_ref[1, place] = (total[:, 0:w] + total[:, w:2 * w]).reshape(ys, 2, rows, w)

    edge = nn // 16 * 16
    for S in (SA, SB, SC):
        S[:, :, edge:pad, :] = jnp.zeros((n, S.shape[1], pad - edge, w), BF16)

    def spread(block, S, q):
        for l in range(n):
            S[l, q, 0:nn, :] = block[l * nn:(l + 1) * nn, :]

    spread(a_ref.at[0], SA, 0)
    spread(a_ref.at[1], SA, 1)
    started = []

    def send(src, dst, ssem, rsem, dev):
        copy = pltpu.make_async_remote_copy(src_ref=src, dst_ref=dst, send_sem=ssem, recv_sem=rsem,
                                            device_id=dev, device_id_type=MESH)
        copy.start()
        started.append(copy)
        return copy

    part = [pl.ds(0, half_rows), pl.ds(half_rows, half_rows)]

    order_z = [o, left, right, lax.rem(o + 2, groups)]
    last = order_z[3]
    low, high = part
    pairs = {}
    one_a = {}

    def ahead(i):
        return lax.rem(order_z[i] - z + zs, zs)

    def behind(i):
        return lax.rem(z - order_z[i] + zs, zs)

    def pair_send(i):
        zp = order_z[i]
        pairs[i] = send(p_ref.at[0, zp, :, 1 - core], abuf0.at[zp], sa0.at[i], ra0.at[i], partner)

    def pair_add(i):
        zp = order_z[i]
        pairs[i].wait_recv()
        X0[zp] = p_ref[0, zp, :, core] + abuf0[zp]

    def c_one(i):
        zp = order_z[i]
        for d in far_first(ys):
            one_a[i, d] = send(X0.at[zp, lax.rem(y + d, ys), low], B1a.at[i, d - 1], s1a.at[i, d - 1],
                               r1a.at[i, d - 1], ypeer[d - 1])
        e = ahead(i)

        @pl.when(e > 0)
        def _():
            remote(X0.at[zp, :, high], B1b.at[e - 1], s1b.at[e - 1], r1b.at[e - 1], at(zp, y)).start()

    def c_two_a(i):
        zp = order_z[i]
        acc = X0[zp, y, low]
        for d in range(1, ys):
            one_a[i, d].wait_recv()
            acc = acc + B1a[i, d - 1]
        Ya[zp] = acc
        e = ahead(i)

        @pl.when(e > 0)
        def _():
            remote(Ya.at[zp], B2a.at[e - 1], s2a.at[e - 1], r2a.at[e - 1], at(zp, y)).start()

    def c_two_b():
        for e in range(1, zs):
            remote(B1b.at[e - 1], B1b.at[e - 1], s1b.at[e - 1], r1b.at[e - 1], partner).wait_recv()
        acc = X0[z, :, high]
        for e in range(1, zs):
            acc = acc + B1b[e - 1]
        Yb[...] = acc
        for d in range(1, ys):
            remote(Yb.at[lax.rem(y + d, ys)], B2b.at[d - 1], s2b.at[d - 1], r2b.at[d - 1], ypeer[d - 1]).start()

    def publish():
        spot = cpan.at[z, y, core]
        for e in far_first(zs):
            remote(spot, spot, ga_s.at[e - 1], ga_r.at[e - 1], zpeer[e - 1]).start()
        for d in far_first(ys):
            remote(spot, spot, gb_s.at[z, d - 1], gb_r.at[z, d - 1], ypeer[d - 1]).start()
        for d in far_first(groups):
            remote(spot, crow.at[o], sx.at[0, d - 1], rx.at[0, d - 1], xpeer[d - 1]).start()

    def c_end():
        piece = Ya[z]
        for e in range(1, zs):
            remote(B2a.at[e - 1], B2a.at[e - 1], s2a.at[e - 1], r2a.at[e - 1], partner).wait_recv()
            piece = piece + B2a[e - 1]
        corr_ref[low, :] = piece
        cpan[z, y, core, low] = piece
        crow[o, low] = piece
        piece = Yb[y]
        for d in range(1, ys):
            remote(B2b.at[d - 1], B2b.at[d - 1], s2b.at[d - 1], r2b.at[d - 1], partner).wait_recv()
            piece = piece + B2b[d - 1]
        corr_ref[high, :] = piece
        cpan[z, y, core, high] = piece
        crow[o, high] = piece
        publish()

    def g_two(i):
        zp = order_z[i]
        spot = cpan.at[zp, y, core]
        e = behind(i)

        @pl.when(e > 0)
        def _():
            remote(spot, spot, ga_s.at[e - 1], ga_r.at[e - 1], partner).wait_recv()
            for d in far_first(ys):
                remote(spot, spot, gb_s.at[zp, d - 1], gb_r.at[zp, d - 1], ypeer[d - 1]).start()

    def g_end(i):
        zp = order_z[i]
        spot = cpan.at[zp, y, core]
        for d in range(1, ys):
            remote(spot, spot, gb_s.at[zp, d - 1], gb_r.at[zp, d - 1], partner).wait_recv()
        column = cpan.at[zp, :, core]
        return send(column, column, gf_s.at[i], gf_r.at[i], partner)

    def late_one():
        out = {}
        for d in far_first(ys):
            out[d] = send(X0.at[last, lax.rem(y + d, ys)], BL1.at[d - 1], sl1.at[d - 1], rl1.at[d - 1], ypeer[d - 1])
        return [out[d] for d in range(1, ys)]

    def late_two(copies):
        acc = X0[last, y]
        for d, copy in enumerate(copies):
            copy.wait_recv()
            acc = acc + BL1[d]
        YL[...] = acc
        for e in far_first(zs):
            remote(YL, BL2.at[e - 1], sl2.at[e - 1], rl2.at[e - 1], zpeer[e - 1]).start()

    def late_end():
        piece = YL[...]
        for e in range(1, zs):
            remote(BL2.at[e - 1], BL2.at[e - 1], sl2.at[e - 1], rl2.at[e - 1], partner).wait_recv()
            piece = piece + BL2[e - 1]
        cpan[last, y, core] = piece
        spot = cpan.at[last, y, core]
        for d in far_first(ys):
            remote(spot, spot, gb_s.at[last, d - 1], gb_r.at[last, d - 1], ypeer[d - 1]).start()
        forwards.append(send(spot, spot, gl_s.at[0], gl_r.at[0], partner))

        @pl.when(z == last)
        def _():
            corr_ref[...] = piece
            crow[o] = piece
            for d in range(1, groups):
                remote(spot, crow.at[o], sx.at[0, d - 1], rx.at[0, d - 1], xpeer[d - 1]).start()

    def late_forward():
        for d in range(1, ys):
            spot = cpan.at[last, lax.rem(y - d + ys, ys), core]
            remote(spot, spot, gb_s.at[last, d - 1], gb_r.at[last, d - 1], partner).wait_recv()
            forwards.append(send(spot, spot, gl_s.at[d], gl_r.at[d], partner))

    correlate(a_ref, o)
    pair_send(0)

    prow[...] = jnp.zeros(prow.shape, F32)
    prow[0:2, 0:n * nn] = pot_ref[...]
    pcol[...] = prow[...].T

    order = [(b, 0), (b, 1), (mate, 0), (mate, 1), (back1, 0), (back2, 0), (fwd2, 0), (back1, 1), (back2, 1),
             (fwd2, 1)]
    shape = (2 * n, 10 * n)
    ci = lax.broadcasted_iota(jnp.int32, shape, 1)
    gid = jnp.zeros(shape, jnp.int32)
    for q, (dev, k) in enumerate(order):
        gid = jnp.where((ci >= q * n) & (ci < (q + 1) * n), dev * 2 + k, gid)
    r, c = rows_and_cols((2 * n, n))
    pick_r = jnp.where(r - n * quotient(r, n) == c, 1.0, 0.0)
    r, c = rows_and_cols((n, 10 * n))
    pick_c = jnp.where(c - n * quotient(c, n) == r, 1.0, 0.0)
    bt = [hdot(hdot(pick_r, db_ref[:, u, :].astype(F32)), pick_c) for u in range(3)]
    t1.wait_recv()
    t2.wait_recv()
    M = [jnp.zeros(shape, F32) for _ in range(3)]
    for d in range(3):
        code = tbl[d, 0:2 * n, 9:10]
        factor = jnp.where(code < 0, 0.0, jnp.where(code == 0, 0.5, jnp.where(code == 1, 1.0, 2.0)))
        for a in range(3):
            t = jnp.zeros(shape, F32)
            for u in range(3):
                t = t + jnp.where(tbl[d, 0:2 * n, a * 3 + u:a * 3 + u + 1] == gid, bt[u], 0.0)
            t = t * factor
            M[a] = M[a] + 0.5 * lax.dot_general(t[:, 0:2 * n], t, (((0,), (0,)), ((), ())), precision=HIGH,
                                                preferred_element_type=F32)
    half = 2 * pad
    r, c = rows_and_cols((half, 2 * n))
    rs = quotient(r, pad)
    rq = r - rs * pad
    ri1 = quotient(rq, n)
    ri2 = rq - ri1 * n
    ok = rq < nn
    cs = quotient(c, n)
    ci = c - cs * n
    L1 = jnp.where(ok & (cs == rs) & (ci == ri1), 1.0, 0.0)
    L2 = jnp.where(ok & (cs == rs) & (ci == ri2), 1.0, 0.0)
    LM1 = hdot(L1, M[1])
    LM2 = hdot(L2, M[2])
    r, c = rows_and_cols((n * 32, 2 * n))
    ri = quotient(r, 32)
    rs = quotient(r, 16) - 2 * ri
    cs = quotient(c, n)
    L0 = jnp.where((cs == rs) & ((c - cs * n) == ri), 1.0, 0.0)
    LM0 = hdot(L0, M[0])

    def expand(m12, m0, base, count):
        wide = count * pad
        r, c = rows_and_cols((10 * n, wide))
        cs = quotient(c, pad)
        cq = c - cs * pad
        cl1 = quotient(cq, n)
        cl2 = cq - cl1 * n
        ok = cq < nn
        rs = quotient(r, n)
        ri = r - rs * n
        ok = ok & (cs + base == rs)
        C1 = jnp.where(ok & (ri == cl1), 1.0, 0.0)
        C2 = jnp.where(ok & (ri == cl2), 1.0, 0.0)
        r, c = rows_and_cols((half, wide))
        rq = r - quotient(r, pad) * pad
        cq = c - quotient(c, pad) * pad
        ri1 = quotient(rq, n)
        cl1 = quotient(cq, n)
        same1 = ri1 == cl1
        same2 = (rq - ri1 * n) == (cq - cl1 * n)
        full = jnp.where(same2, hdot(LM1, C1), 0.0) + jnp.where(same1, hdot(LM2, C2), 0.0)
        hi, lo = split_two(full)
        m12[0:half, :] = hi
        m12[half:2 * half, :] = lo
        step = count * 16
        r, c = rows_and_cols((10 * n, n * step))
        cl = quotient(c, step)
        cs = quotient(c - cl * step, 16)
        rs = quotient(r, n)
        C0 = jnp.where((rs == cs + base) & ((r - rs * n) == cl), 1.0, 0.0)
        r, c = rows_and_cols((n * 32, n * step))
        same = (r - 16 * quotient(r, 16)) == (c - 16 * quotient(c, 16))
        full = jnp.where(same, hdot(LM0, C0), 0.0)
        hi, lo = split_two(full)
        m0[0:n * 32, :] = hi
        m0[n * 32:n * 64, :] = lo

    def apply_inner(S, m12, fresh):
        count = S.shape[1]

        @pl.loop(0, n)
        def _(i):
            got = jnp.dot(m12[...], S[i].reshape(count * pad, w), preferred_element_type=F32)
            got = (got[0:half] + got[half:2 * half]).reshape(2, pad, w)
            Wsc[i] = got if fresh else Wsc[i] + got

    def apply_outer(S, m0):
        count = S.shape[1]

        @pl.loop(0, pad // 16)
        def _(i):
            rows = pl.ds(pl.multiple_of(i * 16, 16), 16)
            got = jnp.dot(m0[...], S[:, :, rows, :].reshape(n * count * 16, w), preferred_element_type=F32)
            Wsc[:, :, rows, :] = Wsc[:, :, rows, :] + (got[0:n * 32] + got[n * 32:n * 64]).reshape(n, 2, 16, w)

    expand(m12a, m0a, 0, 4)
    for k in range(2):
        h0[k].wait_recv()
        spread(halo.at[0, k], SA, 2 + k)
    apply_inner(SA, m12a, True)
    apply_outer(SA, m0a)
    expand(m12b, m0b, 4, 3)
    expand(m12c, m0c, 7, 3)

    sends[0].wait_recv()
    xf0.start()
    sends[1].wait_recv()
    xf1.start()
    h1[0].wait_recv()
    h3[0].start()
    spread(halo.at[1, 0], SB, 0)
    h2[0].wait_recv()
    spread(halo.at[2, 0], SB, 1)
    h3[0].wait_recv()
    spread(halo.at[3, 0], SB, 2)
    apply_inner(SB, m12b, False)
    apply_outer(SB, m0b)

    h1[1].wait_recv()
    h3[1].start()
    pair_add(0)
    c_one(0)
    sends[2].wait_recv()
    correlate(gath.at[0], left)
    pair_send(1)
    sends[3].wait_recv()
    correlate(gath.at[1], right)
    pair_send(2)
    pair_add(1)
    c_one(1)
    spread(halo.at[1, 1], SC, 0)
    h2[1].wait_recv()
    spread(halo.at[2, 1], SC, 1)
    h3[1].wait_recv()
    spread(halo.at[3, 1], SC, 2)
    pair_add(2)
    c_one(2)
    apply_inner(SC, m12c, False)
    apply_outer(SC, m0c)

    for k in range(2):
        for l in range(n):
            full = Wsc[l, k] + (pcol[l * nn:l * nn + pad, k:k + 1] * alive[k]) * SA[l, k].astype(F32)
            hi, lo = split_two(full)
            R[k, l * nn:(l + 1) * nn, w:2 * w] = hi[0:nn]
            R[k, l * nn:(l + 1) * nn, 2 * w:3 * w] = lo[0:nn]

    for i in range(3):
        c_two_a(i)
    pl.when(z != last)(c_two_b)
    fock_part(a_ref, o)
    fock_part(gath.at[0], left)
    xf0.wait_recv()
    xf1.wait_recv()
    correlate(gath.at[2], last)
    pair_send(3)
    pl.when(z != last)(c_end)
    pair_add(3)
    late = late_one()
    fock_part(gath.at[1], right)
    fock_part(gath.at[2], last)

    first = {}

    for h in range(2):
        first[0, h] = send(p_ref.at[1, :, :, 1 - core, part[h]], abuf.at[0, h], sa.at[0, h], ra.at[0, h], partner)
    for i in range(3):
        g_two(i)
    late_two(late)

    def add_pair(f, h):
        first[f, h].wait_recv()
        X[f, h] = p_ref[1, :, :, core, part[h]] + abuf[f, h]

    def scatter_one(f, h):
        out = []
        for d in far_first(ys if h == 0 else zs):
            if h == 0:
                t = lax.rem(y + d, ys)
                src = X.at[f, h, :, t]
            else:
                t = lax.rem(z + d, zs)
                src = X.at[f, h, t]
            out.append(send(src, B1.at[f, h, d - 1], s1.at[f, h, d - 1], r1.at[f, h, d - 1],
                            (ypeer if h == 0 else zpeer)[d - 1]))
        return out

    def scatter_two(f, h, copies):
        for copy in copies:
            copy.wait_recv()
        acc = X[f, h, :, y] if h == 0 else X[f, h, z]
        for d in range(1, ys if h == 0 else zs):
            acc = acc + B1[f, h, d - 1]
        Y[f, h] = acc
        out = []
        for d in far_first(zs if h == 0 else ys):
            t = lax.rem(z + d, zs) if h == 0 else lax.rem(y + d, ys)
            out.append(send(Y.at[f, h, t], B2.at[f, h, d - 1], s2.at[f, h, d - 1], r2.at[f, h, d - 1],
                            (zpeer if h == 0 else ypeer)[d - 1]))
        return out

    def scatter_end(f, h, copies):
        for copy in copies:
            copy.wait_recv()
        acc = Y[f, h, z] if h == 0 else Y[f, h, y]
        for d in range(1, zs if h == 0 else ys):
            acc = acc + B2[f, h, d - 1]
        return acc

    one = {}
    two = {}
    for h in range(2):
        add_pair(0, h)
    forwards = []
    late_end()
    early = [g_end(i) for i in range(3)]
    for h in range(2):
        one[0, h] = scatter_one(0, h)

    def diagonal(count, start):
        r = lax.broadcasted_iota(jnp.int32, (count, w), 0) + start
        c = lax.broadcasted_iota(jnp.int32, (count, w), 1) + o * w
        return r == c

    def product(left):
        lhi, llo = split_two(left)
        both = jnp.concatenate([lhi.astype(F32), llo.astype(F32)], axis=0).astype(BF16)
        big = jnp.dot(both, pan_hi[...], preferred_element_type=F32)
        return big[0:half_rows] + big[half_rows:rows] + jnp.dot(lhi, pan_lo[...], preferred_element_type=F32)

    def row_gather(g, h, value):
        urow[g, h, o] = value
        out = []
        for d in far_first(groups):
            out.append(send(urow.at[g, h, o], urow.at[g, h, o], su.at[g, h, d - 1], ru.at[g, h, d - 1], xpeer[d - 1]))
        return out

    def arrived(copies):
        for copy in copies:
            copy.wait_recv()

    step = total_rows // zs

    def turn_panel(zp):
        first_row = pl.multiple_of(zp * step, 128)
        block = jnp.where(diagonal(step, first_row), 1.5, 0.0) - 0.5 * cpan[zp].reshape(step, w)
        hi, lo = split_two(block)
        span = pl.ds(first_row, step)
        pan_hi[span, :] = hi
        pan_lo[span, :] = lo

    for i in range(3):
        early[i].wait_recv()
        turn_panel(order_z[i])
    late_forward()
    for d in range(1, groups):
        remote(crow.at[0], crow.at[0], sx.at[0, d - 1], rx.at[0, d - 1], partner).wait_recv()
    for copy in forwards:
        copy.wait_recv()
    turn_panel(last)
    moved = {}
    for h in range(2):
        row = jnp.concatenate([crow[k, part[h]] for k in range(groups)], axis=1)
        moved[0, h] = row_gather(0, h, product(row))
    for h in range(2):
        arrived(moved[0, h])
        row = jnp.concatenate([urow[0, h, k] for k in range(groups)], axis=1)
        moved[1, h] = row_gather(1, h, product(row))
    for h in range(2):
        two[0, h] = scatter_two(0, h, one[0, h])
    for h in range(2):
        arrived(moved[1, h])
        row = jnp.concatenate([urow[1, h, k] for k in range(groups)], axis=1)
        right = product(row)
        turn = jnp.where(diagonal(half_rows, b * rows + h * half_rows), 1.5, 0.0) - 0.5 * corr_ref[part[h], :]
        inv_ref[part[h], :] = 1.5 * turn - 0.5 * right
    for h in range(2):
        fock_ref[part[h], :] = scatter_end(0, h, two[0, h])

    def sent(ref, sem):
        remote(ref, ref, sem, rl1.at[0], partner).wait_send()

    for i in range(3):
        e = ahead(i)

        @pl.when(e > 0)
        def _():
            sent(B1b.at[e - 1], s1b.at[e - 1])
            sent(B2a.at[e - 1], s2a.at[e - 1])

    @pl.when(z != last)
    def _():
        for e in range(1, zs):
            sent(cpan.at[0, 0, core], ga_s.at[e - 1])
        for d in range(1, ys):
            sent(B2b.at[d - 1], s2b.at[d - 1])

    for e in range(1, zs):
        sent(YL, sl2.at[e - 1])
    for zp in range(zs):
        for d in range(1, ys):
            sent(cpan.at[0, 0, core], gb_s.at[zp, d - 1])
    for d in range(1, groups):
        sent(crow.at[0], sx.at[0, d - 1])
    for copy in started:
        copy.wait_send()
    for i in range(4):
        sends[i].wait_send()
    xf0.wait_send()
    xf1.wait_send()
    t1.wait_send()
    t2.wait_send()
    for k in range(2):
        h0[k].wait_send()
        h1[k].wait_send()
        h2[k].wait_send()
        h3[k].wait_send()


def whole(orbitals, potential, deriv_blocks, levels, box_counts, neighbours):
    slots, coefs, w = orbitals.shape
    n = deriv_blocks.shape[1]
    nn = n * n
    pad = -(-nn // 16) * 16
    boxes = lax.axis_size("box")
    groups = lax.axis_size("orb")
    zs = groups
    ys = boxes // 2 // zs
    fy = max(ys - 1, 1)
    total = groups * w
    rows = total // boxes
    half = rows // 2
    far = max(zs, ys) - 1
    vm = pl.BlockSpec(memory_space=pltpu.VMEM)
    sm = pl.BlockSpec(memory_space=pltpu.SMEM)
    hbm = pl.BlockSpec(memory_space=pl.ANY)
    column = -(-((n - 1) * nn + pad) // 128) * 128
    dma = pltpu.SemaphoreType.DMA
    out = jax.ShapeDtypeStruct((rows, w), F32)
    return pl.pallas_call(
        functools.partial(whole_kernel, n, pad, zs, ys),
        out_shape=(out, out, out),
        in_specs=[hbm, sm, sm, sm, hbm, hbm],
        out_specs=(vm, vm, vm),
        scratch_shapes=[
            pltpu.VMEM((slots, coefs, w), BF16),
            pltpu.VMEM((slots, coefs), F32),
            pltpu.VMEM((n, 3, n), BF16),
            dma((3,)),
            pltpu.VMEM((3, slots, coefs, w), BF16),
            pltpu.VMEM((4, slots, coefs, w), BF16),
            pltpu.VMEM((n, 4, pad, w), BF16),
            pltpu.VMEM((n, 3, pad, w), BF16),
            pltpu.VMEM((n, 3, pad, w), BF16),
            pltpu.VMEM((n, 2, pad, w), F32),
            pltpu.VMEM((slots, coefs, 3 * w), BF16),
            pltpu.VMEM((4 * pad, 4 * pad), BF16),
            pltpu.VMEM((4 * pad, 3 * pad), BF16),
            pltpu.VMEM((4 * pad, 3 * pad), BF16),
            pltpu.VMEM((n * 64, n * 64), BF16),
            pltpu.VMEM((n * 64, n * 48), BF16),
            pltpu.VMEM((n * 64, n * 48), BF16),
            pltpu.VMEM((3, -(-slots * n // 8) * 8, 128), jnp.int32),
            pltpu.VMEM((8, column), F32),
            pltpu.VMEM((column, 8), F32),
            pltpu.VMEM((2, groups, total // groups // (2 * rows), 2, rows, w), F32),
            pltpu.VMEM((zs, ys, rows, w), F32),
            pltpu.VMEM((zs, ys, rows, w), F32),
            pltpu.VMEM((zs, fy, half, w), F32),
            pltpu.VMEM((zs - 1, ys, half, w), F32),
            pltpu.VMEM((zs, half, w), F32),
            pltpu.VMEM((ys, half, w), F32),
            pltpu.VMEM((zs - 1, half, w), F32),
            pltpu.VMEM((fy, half, w), F32),
            pltpu.VMEM((fy, rows, w), F32),
            pltpu.VMEM((rows, w), F32),
            pltpu.VMEM((zs - 1, rows, w), F32),
            pltpu.VMEM((1, 2, zs, ys, half, w), F32),
            pltpu.VMEM((1, 2, zs, ys, half, w), F32),
            pltpu.VMEM((1, 2, far, zs, half, w), F32),
            pltpu.VMEM((1, 2, zs, half, w), F32),
            pltpu.VMEM((1, 2, far, half, w), F32),
            pltpu.VMEM((zs, ys, 2, rows, w), F32),
            pltpu.VMEM((groups, rows, w), F32),
            pltpu.VMEM((2, 2, groups, half, w), F32),
            pltpu.VMEM((total, w), BF16),
            pltpu.VMEM((total, w), BF16),
            dma((6,)), dma((3, 2)), dma((8,)), dma((4, 2)), dma((2,)), dma((2,)),
            dma((zs,)), dma((zs,)),
            dma((zs, fy)), dma((zs, fy)), dma((zs - 1,)), dma((zs - 1,)),
            dma((zs - 1,)), dma((zs - 1,)), dma((fy,)), dma((fy,)),
            dma((zs - 1,)), dma((zs - 1,)), dma((zs, fy)), dma((zs, fy)), dma((zs,)), dma((zs,)),
            dma((ys,)), dma((ys,)), dma((fy,)), dma((fy,)), dma((zs - 1,)), dma((zs - 1,)),
            dma((1, 2)), dma((1, 2)),
            dma((1, 2, far)), dma((1, 2, far)),
            dma((1, 2, far)), dma((1, 2, far)),
            dma((1, groups - 1)), dma((1, groups - 1)),
            dma((2, 2, groups - 1)), dma((2, 2, groups - 1)),
        ],
        compiler_params=pltpu.CompilerParams(collective_id=0, has_side_effects=True, vmem_limit_bytes=63 << 20),
        name="whole",
    )(orbitals, jnp.transpose(neighbours, (0, 2, 1)), levels, box_counts, potential,
      jnp.transpose(deriv_blocks, (1, 0, 2)))


def settle_kernel(*refs):
    for src, dst in zip(refs[:3], refs[3:]):
        dst[...] = src[...]


def settle(arrays):
    vm = pl.BlockSpec(memory_space=pltpu.VMEM)
    return pl.pallas_call(
        settle_kernel,
        out_shape=tuple(jax.ShapeDtypeStruct(a.shape, a.dtype) for a in arrays),
        in_specs=[vm] * 3,
        out_specs=(vm,) * 3,
        name="settle",
    )(*arrays)


def body(orbitals, potential, deriv_blocks, levels, box_counts, neighbours):
    return settle(whole(orbitals, potential, deriv_blocks, levels, box_counts, neighbours))


def solution(mesh):
    in_specs = (
        P("box", None, "orb"),
        P("box", None),
        P(),
        P("box"),
        P("box"),
        P("box", None, None),
    )
    out_specs = (P("box", "orb"), P("box", "orb"), P("box", "orb"))
    return jax.shard_map(body, mesh=mesh, in_specs=in_specs, out_specs=out_specs, check_vma=False)
```
